256 devices in a mesh: space: 128 (over y, z, x), orb: 2 (over core).
Axes of the slice: x: 4, y: 4, z: 8, core: 2. Of those that a mesh axis runs over, the one named last changes fastest.
Arguments:
- coefficients: float32 [2, 128, 128, 512], P(None, 'space', None, 'orb'), may hold values from -6 to 6
- margin: float32 [128, 16, 128, 128], P('space'), may hold values from -0.125 to 0.125
- step_matrix: float32 [128, 16, 128, 128], P('space'), may hold values from -0.1875 to 0.1875
- neighbours: int32 [128, 16], P('space'), may hold values from 0 to 127, as said below
- pattern: int32 [128, 16], P('space'), may hold values 0 or 1
Outputs:
- propagated: float32 [2, 128, 128, 512], P(None, 'space', None, 'orb')
- projections: float32 [2, 512, 512], P(None, 'space', 'orb')
The draws below stay inside these ranges and needn't reach their ends.
Inputs may be any that keep to these rules, and one draw needn't show every extreme that they name: neighbours[i, 0] = i; every other entry is an atom block of a spatial domain at most 2 domains away from that of block i (domain = block index); the block of slot 1 lies 2 domains ahead of block i and the block of slot 2 lies 2 domains behind it, each clipped to the first and last domain.
All inputs are finite; a program needn't handle non-finite values. No bound on the sum of `pattern` on one device may be relied on, other than what follows from the above.
Results may differ from the reference program's by a relative error of at most 0.0001.
Values sent between devices are 32-bit elements; how exact they have to be, the bound alone decides.
No kernel may reach another device: no remote copies, remote signals or barrier semaphores. Data moves between devices by JAX's collectives and lax.ppermute only.
A program may use at most 64 MiB of HBM per device.

```python
import jax
import jax.numpy as jnp
from jax import lax

BLOCK = 128
BLK_DEV = 1
NB = 16
REACH_DEV = 2
ORDER = 4
DOMAINS = 128
BLOCKS = 128
ORBS = 512
ROWS = 16384


def draw_neighbours(key, part):
    row_ids = jnp.arange(BLOCKS, dtype=jnp.int32)
    home_domain = row_ids // BLK_DEV
    key_offset, key_slot = jax.random.split(key)
    offsets = jax.random.randint(key_offset, (BLOCKS, NB), -REACH_DEV, REACH_DEV + 1, dtype=jnp.int32)
    column_ids = jnp.arange(NB, dtype=jnp.int32)[None, :]
    offsets = jnp.where(column_ids == 1, REACH_DEV, jnp.where(column_ids == 2, -REACH_DEV, offsets))
    target_domain = jnp.clip(home_domain[:, None] + offsets, 0, DOMAINS - 1)
    slot_ids = jax.random.randint(key_slot, (BLOCKS, NB), 0, BLK_DEV, dtype=jnp.int32)
    chosen = target_domain * BLK_DEV + slot_ids
    return jnp.where(column_ids == 0, row_ids[:, None], chosen).astype(jnp.int32)


def with_ends(values, stream_key, smallest, top_value):
    longest = values.shape.index(max(values.shape))
    spots = []
    for shift in (0, 1):
        where = [jax.random.randint(jax.random.fold_in(stream_key, axis), (), 0, length) for axis, length in enumerate(values.shape)]
        where[longest] = (where[longest] + shift) % values.shape[longest]
        spots.append(tuple(where))
    return values.at[spots[0]].set(smallest).at[spots[1]].set(top_value)


def shard_levels(own_key, dims, shards, smallest, top_value):
    def one(axis_at, parts):
        draws = jax.random.uniform(jax.random.fold_in(jax.random.fold_in(own_key, 6), axis_at), (parts,), jnp.float32, smallest / len(shards), top_value / len(shards))
        return jnp.repeat(jnp.exp(draws), dims[axis_at] // parts).reshape((-1,) + (1,) * (len(dims) - axis_at - 1))

    loudness = one(*shards[0])
    for cut in shards[1:]:
        loudness = loudness * one(*cut)
    return loudness


def scatter_about(own_key, shape, deviation, bound, shards=(), kind=jnp.bfloat16):
    drawn = jax.random.normal(own_key, shape, jnp.float32) * deviation
    if len(shards) > 0:
        drawn = shard_levels(own_key, shape, shards, -0.22, 0.18) * drawn
    return jnp.clip(drawn, min=-bound, max=bound).astype(kind)


def setup_inputs(seed: int = 0) -> dict:
    splits = jax.random.split(jax.random.key(seed), 6)
    coefficients = scatter_about(splits[0], (2, BLOCKS, BLOCK, ORBS), 1.0, 6.0, ((1, 128), (3, 2)), jnp.float32)
    margin = scatter_about(splits[1], (BLOCKS, NB, BLOCK, BLOCK), (BLOCK * NB) ** -0.5, 0.125, ((0, 128),), jnp.float32)
    step_matrix = scatter_about(splits[2], (BLOCKS, NB, BLOCK, BLOCK), (BLOCK * NB // 2) ** -0.5, 0.1875, ((0, 128),), jnp.float32)
    neighbours = draw_neighbours(jax.random.fold_in(splits[5], 71), 0)
    pattern = with_ends((jax.random.randint(splits[4], (BLOCKS, NB), 0, 4) < 3).astype(jnp.int32), jax.random.fold_in(splits[4], 1), 0, 1)
    return dict(coefficients=coefficients, margin=margin, step_matrix=step_matrix, neighbours=neighbours, pattern=pattern)


def apply_blocks(matrix, neighbours, state):
    groups = BLOCKS // BLK_DEV
    matrix_groups = matrix.reshape(groups, BLK_DEV, NB, BLOCK, BLOCK)
    index_groups = neighbours.reshape(groups, BLK_DEV, NB)

    def one_group(operands):
        block_mat, block_idx = operands
        picked = state[block_idx]
        return jnp.einsum("rkab,rkbc->rac", block_mat, picked, precision=lax.Precision.HIGHEST)

    result = lax.map(one_group, (matrix_groups, index_groups))
    return result.reshape(BLOCKS, BLOCK, 2 * ORBS)


def reference(coefficients, margin, step_matrix, neighbours, pattern):
    column_ids = jnp.arange(NB, dtype=jnp.int32)[None, :]
    weights = jnp.where(column_ids == 0, jnp.float32(1.0), pattern.astype(jnp.float32))
    margin_live = margin * weights[:, :, None, None]
    step_live = step_matrix * weights[:, :, None, None]
    state = jnp.concatenate([coefficients[0], coefficients[1]], axis=-1)
    moved = state + apply_blocks(margin_live, neighbours, state)
    total = moved
    term = moved
    for order_index in range(1, ORDER + 1):
        image = apply_blocks(step_live, neighbours, term)
        term = jnp.concatenate([image[..., ORBS:], -image[..., :ORBS]], axis=-1) / order_index
        total = total + term
    propagated = jnp.stack([total[..., :ORBS], total[..., ORBS:]])
    old_real = coefficients[0].reshape(ROWS, ORBS)
    old_imag = coefficients[1].reshape(ROWS, ORBS)
    new_real = propagated[0].reshape(ROWS, ORBS)
    new_imag = propagated[1].reshape(ROWS, ORBS)
    highest = lax.Precision.HIGHEST
    proj_real = jnp.einsum("ra,rb->ab", old_real, new_real, precision=highest) + jnp.einsum("ra,rb->ab", old_imag, new_imag, precision=highest)
    proj_imag = jnp.einsum("ra,rb->ab", old_real, new_imag, precision=highest) - jnp.einsum("ra,rb->ab", old_imag, new_real, precision=highest)
    projections = jnp.stack([proj_real, proj_imag]) / ROWS
    return propagated, projections
```

```python
import functools

import jax
import jax.numpy as jnp
from jax import lax
from jax.experimental import pallas as pl
from jax.experimental.pallas import tpu as pltpu
from jax.sharding import PartitionSpec as P

ORDER = 4
ROW = 4
BAND = 5
B = 128
HALF = B // 2
F32 = jnp.float32
BF16 = jnp.bfloat16

SMEM = pl.BlockSpec(memory_space=pltpu.SMEM)
VMEM = pl.BlockSpec(memory_space=pltpu.VMEM)


def cost(flops, moved):
    return pl.CostEstimate(flops=flops, bytes_accessed=moved, transcendentals=0)


def split(value):
    high = value.astype(BF16)
    return high, (value - high.astype(F32)).astype(BF16)


def product(a_high, a_low, b_high, b_low):
    dot = functools.partial(jnp.dot, preferred_element_type=F32)
    return dot(a_high, b_high) + (dot(a_high, b_low) + dot(a_low, b_high))


def turned(value):
    lane = lax.broadcasted_iota(jnp.int32, value.shape, 1)
    rolled = pltpu.roll(value, HALF, axis=1)
    return jnp.where(lane < HALF, rolled, -rolled)


def quarter_kernel(me, coef, out):
    x = (me[0] // 2) % ROW
    for q in range(ROW):
        columns = slice(q * HALF, (q + 1) * HALF)
        out[lax.rem(q - x + ROW, ROW)] = jnp.concatenate([coef[0, 0, :, columns], coef[1, 0, :, columns]], axis=1)


def band_kernel(me, nbr, pat, margin, step, margin_out, step_out):
    position = me[0] // 2
    for source, out in ((margin, margin_out), (step, step_out)):
        for d in range(BAND):
            total = None
            for k in range(16):
                weight = F32(1.0) if k == 0 else pat[0, k].astype(F32)
                here = jnp.where(nbr[0, k] == position + (d - 2), weight, F32(0.0))
                part = source[0, k] * here
                total = part if total is None else total + part
            out[:, d * B : (d + 1) * B] = total


def assemble(me, mine, g1, g2, g3, other, full):
    x = (me[0] // 2) % ROW
    core = me[0] % 2
    for j, ref in enumerate((mine, g1, g2, g3)):
        q = lax.rem(x - j + ROW, ROW)
        full[q, pl.ds(pl.multiple_of(core * HALF, HALF), HALF), :] = ref[...]
        full[q, pl.ds(pl.multiple_of((1 - core) * HALF, HALF), HALF), :] = other[j]


def margin_kernel(me, quarters, r1, r2, r3, h0, h1, h2, h3, mine, g1, g2, g3, other, low, high, v, full):
    x = (me[0] // 2) % ROW

    def put(place, tile):
        v[pl.ds(pl.multiple_of(place * B, B), B), :] = tile

    put(x + 2, quarters[0])
    for j, ref in enumerate((r1, r2, r3)):
        put(lax.rem(x - j - 1 + ROW, ROW) + 2, ref[...])
    for j, ref in enumerate((h0, h1, h2, h3)):
        q = lax.rem(x - j + ROW, ROW)
        put(jnp.where(q >= 2, q - 2, q + 6), ref[...])
    assemble(me, mine, g1, g2, g3, other, full)
    v_high, v_low = split(v[...])
    for q in range(ROW):
        m_high, m_low = split(full[q])
        rows = slice(q * B, (q + BAND) * B)
        value = v[(q + 2) * B : (q + 3) * B, :] + product(m_high, m_low, v_high[rows], v_low[rows])
        out = low if q < 2 else high
        out[(q % 2) * B : (q % 2 + 1) * B, :] = value


def parts_kernel(me, mine, g1, g2, g3, other, out_high, out_low, full):
    assemble(me, mine, g1, g2, g3, other, full)
    out_high[...], out_low[...] = split(full[...])


def images(m_high, m_low, before, low, high, after, scale):
    value = jnp.concatenate([before[...], low[...], high[...], after[...]], axis=0)
    v_high, v_low = split(value)
    for q in range(ROW):
        rows = slice(q * B, (q + BAND) * B)
        yield q, product(m_high[q], m_low[q], v_high[rows], v_low[rows]) * scale


def apply_kernel(scale, m_high, m_low, before, low, high, after, out_low, out_high):
    for q, value in images(m_high, m_low, before, low, high, after, scale):
        out = out_low if q < 2 else out_high
        out[(q % 2) * B : (q % 2 + 1) * B, :] = value


def last_kernel(scale, me, m_high, m_low, before, low, high, after, y0l, y0h, y1l, y1h, y2l, y2h, out):
    x = (me[0] // 2) % ROW
    for q, value in images(m_high, m_low, before, low, high, after, scale):
        rows = slice((q % 2) * B, (q % 2 + 1) * B)
        y0, y1, y2, y3 = ((y0l, y1l, y2l, low) if q < 2 else (y0h, y1h, y2h, high))
        out[lax.rem(q - x + ROW, ROW)] = (y0[rows, :] - y2[rows, :]) + value + turned(y1[rows, :] - y3[rows, :])


def old_kernel(me, coef, c1, c2, c3, other, out_high, out_low):
    x = (me[0] // 2) % ROW
    core = me[0] % 2
    width = coef.shape[3]
    for j, ref in enumerate((coef, c1, c2, c3)):
        q = lax.rem(x - j + ROW, ROW)
        for part in range(2):
            for place, tile in ((core, ref[part, 0]), (1 - core, other[j, part])):
                rows = pl.ds(pl.multiple_of(place * width, width), width)
                columns = pl.ds(pl.multiple_of((part * ROW + q) * B, B), B)
                out_high[rows, columns], out_low[rows, columns] = split(jnp.transpose(tile))


def project_kernel(me, old_high, old_low, new, out):
    x = (me[0] // 2) % ROW
    tiles = [new[lax.rem(q - x + ROW, ROW)] for q in range(ROW)]
    value = jnp.concatenate(tiles + [turned(t) for t in tiles], axis=0)
    v_high, v_low = split(value)
    out[...] = product(old_high[...], old_low[...], v_high, v_low)


def reduce_kernel(scale, parts, out):
    total = jnp.sum(parts[...].reshape(-1, 2 * ROW * 2, B), axis=0) * scale
    share = out.shape[1]
    for q in range(ROW):
        for part in range(2):
            tile = total[q * share : (q + 1) * share, part * HALF : (part + 1) * HALF]
            out[part, :, q * HALF : (q + 1) * HALF] = tile


def back_kernel(me, mine, b1, b2, b3, out, held):
    x = (me[0] // 2) % ROW
    for j, tile in enumerate((mine[0], b1[...], b2[...], b3[...])):
        held[lax.rem(x - j + ROW, ROW)] = tile
    for q in range(ROW):
        for part in range(2):
            out[part, 0, :, q * HALF : (q + 1) * HALF] = held[q, :, part * HALF : (part + 1) * HALF]


def local(domains, coefficients, margin, step_matrix, neighbours, pattern):
    width = coefficients.shape[3]
    rows = domains // ROW
    me = (lax.axis_index("space") * 2 + lax.axis_index("orb")).astype(jnp.int32).reshape(1)
    struct = jax.ShapeDtypeStruct

    def call(kernel, out_shape, in_specs, args, scratch=(), estimate=None, name=None):
        outs = jax.tree.map(lambda _: VMEM, out_shape)
        return pl.pallas_call(
            kernel,
            out_shape=out_shape,
            in_specs=in_specs,
            out_specs=outs,
            scratch_shapes=list(scratch),
            cost_estimate=estimate,
            name=name,
            compiler_params=pltpu.CompilerParams(vmem_limit_bytes=40 * 2**20),
        )(*args)

    def in_row(value, by):
        pairs = [(r * ROW + x, r * ROW + (x + by) % ROW) for r in range(rows) for x in range(ROW)]
        return lax.ppermute(value, "space", pairs)

    def across(value, by):
        pairs = [
            (r * ROW + x, (r + (1 if x >= 2 else -1)) % rows * ROW + (x + by) % ROW)
            for r in range(rows)
            for x in range(ROW)
        ]
        return lax.ppermute(value, "space", pairs)

    def next_row(value, by):
        pairs = [(i, (i + by * ROW) % domains) for i in range(domains)]
        return lax.ppermute(value, "space", pairs)

    def swap(value):
        return lax.ppermute(value, "orb", [(0, 1), (1, 0)])

    block = struct((2 * B, B), F32)
    tile_bytes = 4 * B * B

    quarters = call(
        quarter_kernel, struct((ROW, B, B), F32), [SMEM, VMEM], (me, coefficients), name="quarters",
        estimate=cost(10**6, 8 * tile_bytes),
    )
    own_row = [in_row(quarters[j], j) for j in range(1, ROW)]
    halo = [across(quarters[j], j) for j in range(ROW)]

    half_block = pl.BlockSpec((1, 16, HALF, B), lambda i, where, nbr, pat: (0, 0, lax.rem(where[0], 2), 0))
    whole = pl.BlockSpec((HALF, BAND * B), lambda i, where, nbr, pat: (0, 0))
    margin_half, step_half = pl.pallas_call(
        band_kernel,
        grid_spec=pltpu.PrefetchScalarGridSpec(
            num_scalar_prefetch=3, grid=(1,), in_specs=[half_block, half_block], out_specs=[whole, whole]
        ),
        out_shape=[struct((HALF, BAND * B), F32)] * 2,
        cost_estimate=cost(10**6, 22 * tile_bytes),
        name="bands",
    )(me, neighbours, pattern, margin, step_matrix)

    def gathered(half):
        others = [in_row(half, j) for j in range(1, ROW)]
        stack = jnp.stack([half] + others)
        return [half] + others + [swap(stack)]

    margin_parts = gathered(margin_half)
    step_parts = gathered(step_half)
    full = pltpu.VMEM((ROW, B, BAND * B), F32)
    apply_flops = 2 * 3 * ROW * B * BAND * B * B

    y0 = call(
        margin_kernel, [block, block], [SMEM] + [VMEM] * 13,
        [me, quarters] + own_row + halo + margin_parts,
        scratch=[pltpu.VMEM((2 * ROW * B, B), F32), full], name="margin",
        estimate=cost(apply_flops, 40 * tile_bytes),
    )
    half_type = struct((ROW, B, BAND * B), BF16)
    step_high, step_low = call(
        parts_kernel, [half_type, half_type], [SMEM] + [VMEM] * 5, [me] + step_parts, scratch=[full],
        name="step_parts", estimate=cost(10**6, 60 * tile_bytes),
    )

    old_row = [in_row(coefficients, j) for j in range(1, ROW)]
    old_stack = jnp.stack([coefficients[:, 0]] + [o[:, 0] for o in old_row])
    old_type = struct((2 * width, 2 * ROW * B), BF16)
    old_high, old_low = call(
        old_kernel, [old_type, old_type], [SMEM] + [VMEM] * 5, [me, coefficients] + old_row + [swap(old_stack)],
        name="old_parts", estimate=cost(10**6, 64 * tile_bytes),
    )

    def surrounded(y):
        return [next_row(y[1], 1), y[0], y[1], next_row(y[0], -1)]

    states = [list(y0)]
    for n in range(1, ORDER):
        y = call(
            functools.partial(apply_kernel, 1.0 / n), [block, block], [VMEM] * 6,
            [step_high, step_low] + surrounded(states[-1]), name="apply",
            estimate=cost(apply_flops, 32 * tile_bytes),
        )
        states.append(list(y))
    new = call(
        functools.partial(last_kernel, 1.0 / ORDER), struct((ROW, B, B), F32), [SMEM] + [VMEM] * 12,
        [me, step_high, step_low] + surrounded(states[3]) + states[0] + states[1] + states[2], name="last",
        estimate=cost(apply_flops, 44 * tile_bytes),
    )
    back = [in_row(new[j], j) for j in range(1, ROW)]
    partial_value = call(
        project_kernel, struct((2 * width, B), F32), [SMEM] + [VMEM] * 3, [me, old_high, old_low, new],
        name="project", estimate=cost(2 * 3 * 2 * width * 2 * ROW * B * B, 44 * tile_bytes),
    )
    parts = lax.all_to_all(partial_value, "space", 0, 0, tiled=True)
    share = 2 * width // domains
    owned = call(
        functools.partial(reduce_kernel, 1.0 / (domains * B)), struct((2, share, width), F32), [VMEM], [parts],
        name="reduce", estimate=cost(10**5, 5 * tile_bytes),
    )
    propagated = call(
        back_kernel, struct((2, 1, B, width), F32), [SMEM] + [VMEM] * 4, [me, new] + back,
        scratch=[pltpu.VMEM((ROW, B, B), F32)], name="back", estimate=cost(10**5, 8 * tile_bytes),
    )
    return propagated, owned


def solution(mesh):
    return jax.shard_map(
        functools.partial(local, mesh.shape["space"]),
        mesh=mesh,
        in_specs=(
            P(None, "space", None, "orb"),
            P("space", None, None, None),
            P("space", None, None, None),
            P("space", None),
            P("space", None),
        ),
        out_specs=(P(None, "space", None, "orb"), P(None, "space", "orb")),
        check_vma=False,
    )
```

```python
import functools

import jax
import jax.numpy as jnp
from jax import lax
from jax.experimental import pallas as pl
from jax.experimental.pallas import tpu as pltpu
from jax.sharding import Mesh, PartitionSpec as P

ORDER = 4
ROW = 4
BAND = 5
B = 128
HALF = B // 2
F32 = jnp.float32
BF16 = jnp.bfloat16

SMEM = pl.BlockSpec(memory_space=pltpu.SMEM)
VMEM = pl.BlockSpec(memory_space=pltpu.VMEM)


def cost(flops, moved):
    return pl.CostEstimate(flops=flops, bytes_accessed=moved, transcendentals=0)


def split(value):
    high = value.astype(BF16)
    return high, (value - high.astype(F32)).astype(BF16)


def product(a_high, a_low, b_high, b_low):
    dot = functools.partial(jnp.dot, preferred_element_type=F32)
    return dot(a_high, b_high) + (dot(a_high, b_low) + dot(a_low, b_high))


def turned(value):
    lane = lax.broadcasted_iota(jnp.int32, value.shape, 1)
    rolled = pltpu.roll(value, HALF, axis=1)
    return jnp.where(lane < HALF, rolled, -rolled)


def member(me):
    return lax.rem(lax.div(me[0], 2), ROW), lax.rem(me[0], 2)


def turn_to(q, x):
    return lax.rem(q - x + ROW, ROW)


def pack_kernel(me, nbr, pat, coef, margin, step, out):
    position = lax.div(me[0], 2)
    for i in range(ROW):
        columns = slice(i * HALF, (i + 1) * HALF)
        tile = jnp.concatenate([coef[0, 0, :, columns], coef[1, 0, :, columns]], axis=1)
        for q in range(ROW):
            out[q, i * B : (i + 1) * B, :] = tile
    for i, source in enumerate((margin, step)):
        for d in range(BAND):
            total = None
            for k in range(16):
                weight = F32(1.0) if k == 0 else pat[0, k].astype(F32)
                here = jnp.where(nbr[0, k] == position + (d - 2), weight, F32(0.0))
                part = source[0, k] * here
                total = part if total is None else total + part
            start = ROW * B + (i * BAND + d) * HALF
            for q in range(ROW):
                out[q, start : start + HALF, :] = total


def band_rows(i, q, core, mine, other, put):
    for place, ref in ((core, mine), (1 - core, other)):
        rows = pl.ds(pl.multiple_of(place * HALF, HALF), HALF)
        for d in range(BAND):
            start = ROW * B + (i * BAND + d) * HALF
            put(rows, slice(d * B, (d + 1) * B), ref[q, start : start + HALF, :])


def edge_kernel(me, mine, low, high):
    x, _ = member(me)
    for i, out in enumerate((low, high)):
        for q in range(2):
            out[q * B : (q + 1) * B, :] = mine[2 * i + q, pl.ds(pl.multiple_of(x * B, B), B), :]


def margin_kernel(me, mine, other, before, after, out, full):
    x, core = member(me)
    own = [mine[q, pl.ds(pl.multiple_of(x * B, B), B), :] for q in range(ROW)]
    v_high, v_low = split(jnp.concatenate([before[...]] + own + [after[...]], axis=0))
    for q in range(ROW):

        def put(rows, columns, tile):
            full[q, rows, columns] = tile

        band_rows(0, q, core, mine, other, put)
    for q in range(ROW):
        m_high, m_low = split(full[q])
        rows = slice(q * B, (q + BAND) * B)
        out[q * B : (q + 1) * B, :] = own[q] + product(m_high, m_low, v_high[rows], v_low[rows])


def ghost_kernel(me, mine, other, out):
    _, core = member(me)
    for i in range(2):

        def put(rows, columns, tile):
            out[i, rows, columns] = tile

        band_rows(1, i + 2 - 2 * core, core, mine, other, put)


def parts_kernel(me, mine, other, ghost, ghost_other, out_high, out_low):
    _, core = member(me)
    for q in range(ROW):

        def put(rows, columns, tile):
            out_high[q + 2, rows, columns], out_low[q + 2, rows, columns] = split(tile)

        band_rows(1, q, core, mine, other, put)
    for start, ref in ((core * 6, ghost), ((1 - core) * 6, ghost_other)):
        for i in range(2):
            out_high[start + i], out_low[start + i] = split(ref[i])


def two_steps(n, m_high, m_low, before, own, after):
    value = jnp.concatenate([before[...], own[...], after[...]], axis=0)
    v_high, v_low = split(value)
    firsts = []
    for q in range(2 * ROW):
        rows = slice(q * B, (q + BAND) * B)
        firsts.append(product(m_high[q], m_low[q], v_high[rows], v_low[rows]) * F32(1.0 / n))
    v_high, v_low = split(jnp.concatenate(firsts, axis=0))
    for q in range(ROW):
        rows = slice(q * B, (q + BAND) * B)
        second = product(m_high[q + 2], m_low[q + 2], v_high[rows], v_low[rows]) * F32(1.0 / (n + 1))
        yield q, firsts[q + 2], second


def two_kernel(n, m_high, m_low, before, own, after, first, second):
    for q, a, b in two_steps(n, m_high, m_low, before, own, after):
        first[q * B : (q + 1) * B, :] = a
        second[q * B : (q + 1) * B, :] = b


def last_kernel(n, me, m_high, m_low, before, own, after, y0, y1, out):
    x, _ = member(me)
    for q, y3, y4 in two_steps(n, m_high, m_low, before, own, after):
        rows = slice(q * B, (q + 1) * B)
        out[turn_to(q, x)] = (y0[rows, :] - own[rows, :]) + y4 + turned(y1[rows, :] - y3)


def old_kernel(me, mine, other, out_high, out_low):
    _, core = member(me)
    for q in range(ROW):
        for place, ref in ((core, mine), (1 - core, other)):
            for i in range(ROW):
                high, low = split(jnp.transpose(ref[q, i * B : (i + 1) * B, :]))
                rows = pl.ds(pl.multiple_of((place * ROW + i) * HALF, HALF), HALF)
                for part in range(2):
                    columns = slice((part * ROW + q) * B, (part * ROW + q + 1) * B)
                    out_high[rows, columns] = high[part * HALF : (part + 1) * HALF]
                    out_low[rows, columns] = low[part * HALF : (part + 1) * HALF]


def project_kernel(me, old_high, old_low, new, out):
    x, _ = member(me)
    tiles = [new[turn_to(q, x)] for q in range(ROW)]
    v_high, v_low = split(jnp.concatenate(tiles + [turned(t) for t in tiles], axis=0))
    out[...] = product(old_high[...], old_low[...], v_high, v_low)


def reduce_kernel(scale, parts, out):
    share = out.shape[1]
    total = jnp.sum(parts[...].reshape(-1, ROW * share, B), axis=0) * scale
    for q in range(ROW):
        for part in range(2):
            tile = total[q * share : (q + 1) * share, part * HALF : (part + 1) * HALF]
            out[part, :, q * HALF : (q + 1) * HALF] = tile


def back_kernel(me, mine, b1, b2, b3, out, held):
    x, _ = member(me)
    for j, tile in enumerate((mine[0], b1[...], b2[...], b3[...])):
        held[turn_to(x, j)] = tile
    for q in range(ROW):
        for part in range(2):
            out[part, 0, :, q * HALF : (q + 1) * HALF] = held[q, :, part * HALF : (part + 1) * HALF]


def local(rows, coefficients, margin, step_matrix, neighbours, pattern):
    width = coefficients.shape[3]
    domains = rows * ROW
    me = lax.axis_index(("row", "x", "orb")).astype(jnp.int32).reshape(1)
    struct = jax.ShapeDtypeStruct
    tile_bytes = 4 * B * B
    step_flops = 2 * 3 * B * BAND * B * B

    def call(kernel, out_shape, args, flops, moved, name, scratch=(), scalars=1):
        return pl.pallas_call(
            kernel,
            out_shape=out_shape,
            in_specs=[SMEM] * scalars + [VMEM] * (len(args) - scalars),
            out_specs=jax.tree.map(lambda _: VMEM, out_shape),
            scratch_shapes=list(scratch),
            cost_estimate=cost(flops, moved * tile_bytes),
            name=name,
            compiler_params=pltpu.CompilerParams(vmem_limit_bytes=40 * 2**20),
        )(*args)

    def in_row(value, by):
        return lax.ppermute(value, "x", [(x, (x + by) % ROW) for x in range(ROW)])

    def next_row(value, by):
        return lax.ppermute(value, "row", [(r, (r + by) % rows) for r in range(rows)])

    def swap(value):
        return lax.ppermute(value, "orb", [(0, 1), (1, 0)])

    def apart(value):
        pairs = []
        for r in range(rows):
            for x in range(ROW):
                for core, by in ((0, 1), (1, -1)):
                    pairs.append(((r * ROW + x) * 2 + core, ((r + by) % rows * ROW + x) * 2 + core))
        return lax.ppermute(value, ("row", "x", "orb"), pairs)

    half_block = pl.BlockSpec((1, 16, HALF, B), lambda i, where, nbr, pat: (0, 0, lax.rem(where[0], 2), 0))
    packed_rows = ROW * B + 2 * BAND * HALF
    packed = pl.pallas_call(
        pack_kernel,
        grid_spec=pltpu.PrefetchScalarGridSpec(
            num_scalar_prefetch=3,
            grid=(1,),
            in_specs=[pl.BlockSpec(coefficients.shape, lambda i, *_: (0, 0, 0, 0)), half_block, half_block],
            out_specs=pl.BlockSpec((ROW, packed_rows, B), lambda i, *_: (0, 0, 0)),
        ),
        out_shape=struct((ROW, packed_rows, B), F32),
        cost_estimate=cost(10**6, 44 * tile_bytes),
        name="pack",
    )(me, neighbours, pattern, coefficients, margin, step_matrix)
    mine = lax.all_to_all(packed, "x", 0, 0, tiled=True)
    edge = struct((2 * B, B), F32)
    low, high = call(edge_kernel, [edge, edge], [me, mine], 10**5, 8, "edges")
    high, low, held = lax.optimization_barrier((high, low, mine))
    before = next_row(high, 1)
    after = next_row(low, -1)
    other = swap(held)
    before, kept = lax.optimization_barrier((before, mine))
    state = struct((ROW * B, B), F32)
    y0 = call(
        margin_kernel, state, [me, mine, other, before, after], 10**11, 60, "margin",
        scratch=[pltpu.VMEM((ROW, B, BAND * B), F32)],
    )
    ghost = apart(call(ghost_kernel, struct((2, B, BAND * B), F32), [me, kept, other], 10**5, 20, "ghost"))
    ghost, y0 = lax.optimization_barrier((ghost, y0))
    parts_type = struct((2 * ROW, B, BAND * B), BF16)
    step = call(
        parts_kernel, [parts_type, parts_type], [me, mine, other, ghost, swap(ghost)], 10**6, 80, "step_parts"
    )
    step = list(step)

    old_type = struct((2 * width, 2 * ROW * B), BF16)
    old_high, old_low = call(old_kernel, [old_type, old_type], [me, mine, other], 10**6, 64, "old_parts")

    y1, y2 = call(
        functools.partial(two_kernel, 1), [state, state], step + [next_row(y0, 1), y0, next_row(y0, -1)],
        3 * ROW * step_flops, 64, "two", scalars=0,
    )
    before, old_high = lax.optimization_barrier((next_row(y2, 1), old_high))
    new = call(
        functools.partial(last_kernel, 3), struct((ROW, B, B), F32),
        [me] + step + [before, y2, next_row(y2, -1), y0, y1],
        3 * ROW * step_flops, 72, "last",
    )
    back = [in_row(new[j], j) for j in range(1, ROW)]
    partial_value = call(
        project_kernel, struct((2 * width, B), F32), [me, old_high, old_low, new],
        2 * 3 * 2 * width * 2 * ROW * B * B, 44, "project",
    )
    partial_value, *back = lax.optimization_barrier((partial_value, *back))
    parts = lax.all_to_all(partial_value, ("row", "x"), 0, 0, tiled=True)
    share = 2 * width // domains
    owned = call(
        functools.partial(reduce_kernel, 1.0 / (domains * B)), struct((2, share, width), F32), [parts],
        10**5, 5, "reduce", scalars=0,
    )
    propagated = call(
        back_kernel, struct((2, 1, B, width), F32), [me, new] + back, 10**5, 8, "back",
        scratch=[pltpu.VMEM((ROW, B, B), F32)],
    )
    return propagated, owned


def solution(mesh):
    rows = mesh.shape["space"] // ROW
    grouped = Mesh(mesh.devices.reshape(rows, ROW, mesh.shape["orb"]), ("row", "x", "orb"))
    space = ("row", "x")
    return jax.shard_map(
        functools.partial(local, rows),
        mesh=grouped,
        in_specs=(
            P(None, space, None, "orb"),
            P(space, None, None, None),
            P(space, None, None, None),
            P(space, None),
            P(space, None),
        ),
        out_specs=(P(None, space, None, "orb"), P(None, space, "orb")),
        check_vma=False,
    )
```

```python
import functools

import jax
import jax.numpy as jnp
from jax import lax
from jax.experimental import pallas as pl
from jax.experimental.pallas import tpu as pltpu
from jax.sharding import Mesh, PartitionSpec as P

ORDER = 4
ROW = 4
BAND = 5
B = 128
HALF = B // 2
F32 = jnp.float32
BF16 = jnp.bfloat16

SMEM = pl.BlockSpec(memory_space=pltpu.SMEM)
VMEM = pl.BlockSpec(memory_space=pltpu.VMEM)


def cost(flops, moved):
    return pl.CostEstimate(flops=flops, bytes_accessed=moved, transcendentals=0)


def split(value):
    high = value.astype(BF16)
    return high, (value - high.astype(F32)).astype(BF16)


def product(a_high, a_low, b_high, b_low):
    dot = functools.partial(jnp.dot, preferred_element_type=F32)
    return dot(a_high, b_high) + (dot(a_high, b_low) + dot(a_low, b_high))


def turned(value):
    lane = lax.broadcasted_iota(jnp.int32, value.shape, 1)
    rolled = pltpu.roll(value, HALF, axis=1)
    return jnp.where(lane < HALF, rolled, -rolled)


def member(me):
    return lax.rem(lax.div(me[0], 2), ROW), lax.rem(me[0], 2)


def turn_to(q, x):
    return lax.rem(q - x + ROW, ROW)


def parity(me):
    return lax.rem(lax.div(me[0], 2 * ROW), 2)


def pack_kernel(me, nbr, pat, coef, margin, step, out):
    position = lax.div(me[0], 2)
    for q in range(ROW):
        columns = slice(q * HALF, (q + 1) * HALF)
        out[q, :B, :] = jnp.concatenate([coef[0, 0, :, columns], coef[1, 0, :, columns]], axis=1)
    for i, source in enumerate((margin, step)):
        for d in range(BAND):
            total = None
            for k in range(16):
                weight = F32(1.0) if k == 0 else pat[0, k].astype(F32)
                here = jnp.where(nbr[0, k] == position + (d - 2), weight, F32(0.0))
                part = source[0, k] * here
                total = part if total is None else total + part
            start = B + (i * BAND + d) * HALF
            for q in range(ROW):
                out[q, start : start + HALF, :] = total


def band_rows(i, q, core, mine, other, put):
    for place, ref in ((core, mine), (1 - core, other)):
        rows = pl.ds(pl.multiple_of(place * HALF, HALF), HALF)
        for d in range(BAND):
            start = B + (i * BAND + d) * HALF
            put(rows, slice(d * B, (d + 1) * B), ref[q, start : start + HALF, :])


def edge_kernel(me, mine, to_a, to_b):
    odd = parity(me)
    for out, first in ((to_a, 2 - 2 * odd), (to_b, 2 * odd)):
        for q in range(2):
            out[q * B : (q + 1) * B, :] = mine[first + q, :B, :]


def window(odd, from_a, from_b, own, v_high, v_low):
    for start, tile in (
        ((1 - odd) * (ROW + 2) * B, from_a[...]),
        (odd * (ROW + 2) * B, from_b[...]),
        (2 * B, own),
    ):
        rows = pl.ds(pl.multiple_of(start, B), tile.shape[0])
        v_high[rows, :], v_low[rows, :] = split(tile)


def hand_out(odd, y, to_a, to_b):
    to_a[...] = y[pl.ds(pl.multiple_of((2 - 2 * odd) * B, B), 2 * B), :]
    to_b[...] = y[pl.ds(pl.multiple_of(2 * odd * B, B), 2 * B), :]


def margin_kernel(me, mine, other, from_a, from_b, out, to_a, to_b, full, v_high, v_low):
    _, core = member(me)
    odd = parity(me)
    own = [mine[q, :B, :] for q in range(ROW)]
    window(odd, from_a, from_b, jnp.concatenate(own, axis=0), v_high, v_low)
    for q in range(ROW):

        def put(rows, columns, tile):
            full[q, rows, columns] = tile

        band_rows(0, q, core, mine, other, put)
    for q in range(ROW):
        m_high, m_low = split(full[q])
        rows = slice(q * B, (q + BAND) * B)
        out[q * B : (q + 1) * B, :] = own[q] + product(m_high, m_low, v_high[rows], v_low[rows])
    hand_out(odd, out, to_a, to_b)


def parts_kernel(me, mine, other, out_high, out_low):
    _, core = member(me)
    for q in range(ROW):

        def put(rows, columns, tile):
            out_high[q, rows, columns], out_low[q, rows, columns] = split(tile)

        band_rows(1, q, core, mine, other, put)


def images(scale, m_high, m_low, v_high, v_low):
    for q in range(ROW):
        rows = slice(q * B, (q + BAND) * B)
        yield q, product(m_high[q], m_low[q], v_high[rows], v_low[rows]) * F32(scale)


def apply_kernel(scale, me, m_high, m_low, from_a, from_b, own, out, to_a, to_b, v_high, v_low):
    odd = parity(me)
    window(odd, from_a, from_b, own[...], v_high, v_low)
    for q, value in images(scale, m_high, m_low, v_high, v_low):
        out[q * B : (q + 1) * B, :] = value
    hand_out(odd, out, to_a, to_b)


def last_kernel(scale, me, m_high, m_low, from_a, from_b, own, y0, y1, y2, out, v_high, v_low):
    x, _ = member(me)
    window(parity(me), from_a, from_b, own[...], v_high, v_low)
    for q, y4 in images(scale, m_high, m_low, v_high, v_low):
        rows = slice(q * B, (q + 1) * B)
        out[turn_to(q, x)] = (y0[rows, :] - y2[rows, :]) + y4 + turned(y1[rows, :] - own[rows, :])


def old_kernel(me, coef, c1, c2, c3, other, out_high, out_low):
    x, core = member(me)
    width = coef.shape[3]
    for j, ref in enumerate((coef, c1, c2, c3)):
        q = turn_to(x, j)
        for part in range(2):
            for place, tile in ((core, ref[part, 0]), (1 - core, other[j, part])):
                rows = pl.ds(pl.multiple_of(place * width, width), width)
                columns = pl.ds(pl.multiple_of((part * ROW + q) * B, B), B)
                out_high[rows, columns], out_low[rows, columns] = split(jnp.transpose(tile))


def project_kernel(me, old_high, old_low, new, out):
    x, _ = member(me)
    tiles = [new[turn_to(q, x)] for q in range(ROW)]
    v_high, v_low = split(jnp.concatenate(tiles + [turned(t) for t in tiles], axis=0))
    out[...] = product(old_high[...], old_low[...], v_high, v_low)


def reduce_kernel(scale, parts, out):
    share = out.shape[1]
    total = jnp.sum(parts[...].reshape(-1, ROW * share, B), axis=0) * scale
    for q in range(ROW):
        for part in range(2):
            tile = total[q * share : (q + 1) * share, part * HALF : (part + 1) * HALF]
            out[part, :, q * HALF : (q + 1) * HALF] = tile


def back_kernel(me, mine, b1, b2, b3, out, held):
    x, _ = member(me)
    for j, tile in enumerate((mine[0], b1[...], b2[...], b3[...])):
        held[turn_to(x, j)] = tile
    for q in range(ROW):
        for part in range(2):
            out[part, 0, :, q * HALF : (q + 1) * HALF] = held[q, :, part * HALF : (part + 1) * HALF]


def local(rows, coefficients, margin, step_matrix, neighbours, pattern):
    width = coefficients.shape[3]
    domains = rows * ROW
    me = lax.axis_index(("row", "x", "orb")).astype(jnp.int32).reshape(1)
    struct = jax.ShapeDtypeStruct
    tile_bytes = 4 * B * B
    step_flops = 2 * 3 * B * BAND * B * B

    def call(kernel, out_shape, args, flops, moved, name, scratch=(), scalars=1):
        return pl.pallas_call(
            kernel,
            out_shape=out_shape,
            in_specs=[SMEM] * scalars + [VMEM] * (len(args) - scalars),
            out_specs=jax.tree.map(lambda _: VMEM, out_shape),
            scratch_shapes=list(scratch),
            cost_estimate=cost(flops, moved * tile_bytes),
            name=name,
            compiler_params=pltpu.CompilerParams(vmem_limit_bytes=40 * 2**20),
        )(*args)

    def in_row(value, by):
        return lax.ppermute(value, "x", [(x, (x + by) % ROW) for x in range(ROW)])

    def swap(value):
        return lax.ppermute(value, "orb", [(0, 1), (1, 0)])

    def exchange(to_a, to_b):
        def swap_rows(value, first):
            pairs = [(r, r + 1) for r in range(first, rows - 1, 2)]
            return lax.ppermute(value, "row", pairs + [(j, i) for i, j in pairs])

        return [swap_rows(to_a, 0), swap_rows(to_b, 1)]

    half_block = pl.BlockSpec((1, 16, HALF, B), lambda i, where, nbr, pat: (0, 0, lax.rem(where[0], 2), 0))
    packed_rows = B + 2 * BAND * HALF
    packed = pl.pallas_call(
        pack_kernel,
        grid_spec=pltpu.PrefetchScalarGridSpec(
            num_scalar_prefetch=3,
            grid=(1,),
            in_specs=[pl.BlockSpec(coefficients.shape, lambda i, *_: (0, 0, 0, 0)), half_block, half_block],
            out_specs=pl.BlockSpec((ROW, packed_rows, B), lambda i, *_: (0, 0, 0)),
        ),
        out_shape=struct((ROW, packed_rows, B), F32),
        cost_estimate=cost(10**6, 44 * tile_bytes),
        name="pack",
    )(me, neighbours, pattern, coefficients, margin, step_matrix)
    mine = lax.all_to_all(packed, "x", 0, 0, tiled=True)
    state = struct((ROW * B, B), F32)
    edge = struct((2 * B, B), F32)
    parts = [pltpu.VMEM((2 * ROW * B, B), BF16)] * 2
    edges = call(edge_kernel, [edge, edge], [me, mine], 10**5, 8, "edges")
    *edges, held = lax.optimization_barrier((*edges, mine))
    arrived = exchange(*edges)
    other = swap(held)
    arrived[0], held = lax.optimization_barrier((arrived[0], coefficients))
    old = [coefficients, in_row(held, 1)]
    y0, *edges = call(
        margin_kernel, [state, edge, edge], [me, mine, other] + arrived, ROW * step_flops, 60, "margin",
        scratch=[pltpu.VMEM((ROW, B, BAND * B), F32)] + parts,
    )
    parts_type = struct((ROW, B, BAND * B), BF16)
    step = list(call(parts_kernel, [parts_type, parts_type], [me, mine, other], 10**6, 40, "step_parts"))

    states = [y0]
    for n in range(1, ORDER):
        arrived = exchange(*edges)
        *arrived, old[n], held = lax.optimization_barrier((*arrived, old[n], coefficients))
        if n < ROW - 1:
            old.append(in_row(held, n + 1))
        y, *edges = call(
            functools.partial(apply_kernel, 1.0 / n), [state, edge, edge], [me] + step + arrived + [states[-1]],
            ROW * step_flops, 40, "apply", scratch=parts,
        )
        states.append(y)
    arrived = exchange(*edges)
    old_stack = jnp.stack([o[:, 0] for o in old])
    old_type = struct((2 * width, 2 * ROW * B), BF16)
    old_high, old_low = call(
        old_kernel, [old_type, old_type], [me] + old + [swap(old_stack)], 10**6, 64, "old_parts"
    )
    arrived[0], old_high = lax.optimization_barrier((arrived[0], old_high))
    y0, y1, y2, y3 = states
    new = call(
        functools.partial(last_kernel, 1.0 / ORDER), struct((ROW, B, B), F32),
        [me] + step + arrived + [y3, y0, y1, y2], ROW * step_flops, 48, "last", scratch=parts,
    )
    back = [in_row(new[j], j) for j in range(1, ROW)]
    partial_value = call(
        project_kernel, struct((2 * width, B), F32), [me, old_high, old_low, new],
        2 * 3 * 2 * width * 2 * ROW * B * B, 44, "project",
    )
    partial_value, *back = lax.optimization_barrier((partial_value, *back))
    sums = lax.all_to_all(partial_value, ("row", "x"), 0, 0, tiled=True)
    share = 2 * width // domains
    owned = call(
        functools.partial(reduce_kernel, 1.0 / (domains * B)), struct((2, share, width), F32), [sums],
        10**5, 5, "reduce", scalars=0,
    )
    propagated = call(
        back_kernel, struct((2, 1, B, width), F32), [me, new] + back, 10**5, 8, "back",
        scratch=[pltpu.VMEM((ROW, B, B), F32)],
    )
    return propagated, owned


def solution(mesh):
    rows = mesh.shape["space"] // ROW
    grouped = Mesh(mesh.devices.reshape(rows, ROW, mesh.shape["orb"]), ("row", "x", "orb"))
    space = ("row", "x")
    return jax.shard_map(
        functools.partial(local, rows),
        mesh=grouped,
        in_specs=(
            P(None, space, None, "orb"),
            P(space, None, None, None),
            P(space, None, None, None),
            P(space, None),
            P(space, None),
        ),
        out_specs=(P(None, space, None, "orb"), P(None, space, "orb")),
        check_vma=False,
    )
```

```python
import functools

import jax
import jax.numpy as jnp
from jax import lax
from jax.experimental import pallas as pl
from jax.experimental.pallas import tpu as pltpu
from jax.sharding import Mesh, PartitionSpec as P

ORDER = 4
ROW = 4
BAND = 5
B = 128
HALF = B // 2
F32 = jnp.float32
BF16 = jnp.bfloat16

SMEM = pl.BlockSpec(memory_space=pltpu.SMEM)
VMEM = pl.BlockSpec(memory_space=pltpu.VMEM)


def cost(flops, moved):
    return pl.CostEstimate(flops=flops, bytes_accessed=moved, transcendentals=0)


def split(value):
    high = value.astype(BF16)
    return high, (value - high.astype(F32)).astype(BF16)


def product(a_high, a_low, b_high, b_low):
    dot = functools.partial(jnp.dot, preferred_element_type=F32)
    return dot(a_high, b_high) + (dot(a_high, b_low) + dot(a_low, b_high))


def turned(value):
    lane = lax.broadcasted_iota(jnp.int32, value.shape, 1)
    rolled = pltpu.roll(value, HALF, axis=1)
    return jnp.where(lane < HALF, rolled, -rolled)


def member(me):
    return lax.rem(lax.div(me[0], 2), ROW), lax.rem(me[0], 2)


def turn_to(q, x):
    return lax.rem(q - x + ROW, ROW)


def parity(me):
    return lax.rem(lax.div(me[0], 2 * ROW), 2)


def bands(me, nbr, pat, source):
    position = lax.div(me[0], 2)
    for d in range(BAND):
        total = None
        for k in range(source.shape[1]):
            weight = F32(1.0) if k == 0 else pat[0, k].astype(F32)
            here = jnp.where(nbr[0, k] == position + (d - 2), weight, F32(0.0))
            part = source[0, k] * here
            total = part if total is None else total + part
        yield d * HALF, total


def pack_kernel(me, nbr, pat, coef, margin, out):
    for q in range(ROW):
        columns = slice(q * HALF, (q + 1) * HALF)
        out[q, :B, :] = jnp.concatenate([coef[0, 0, :, columns], coef[1, 0, :, columns]], axis=1)
    for start, total in bands(me, nbr, pat, margin):
        for q in range(ROW):
            out[q, B + start : B + start + HALF, :] = total


def step_kernel(me, nbr, pat, step, out):
    for start, total in bands(me, nbr, pat, step):
        out[start : start + HALF, :] = total


def gather_kernel(me, mine, s1, s2, s3, out):
    x, _ = member(me)
    for j, ref in enumerate((mine, s1, s2, s3)):
        out[turn_to(x, j)] = ref[...]


def band_rows(first, q, core, mine, other, put):
    for place, ref in ((core, mine), (1 - core, other)):
        rows = pl.ds(pl.multiple_of(place * HALF, HALF), HALF)
        for d in range(BAND):
            start = first + d * HALF
            put(rows, slice(d * B, (d + 1) * B), ref[q, start : start + HALF, :])


def edge_kernel(me, mine, to_a, to_b):
    odd = parity(me)
    for out, first in ((to_a, 2 - 2 * odd), (to_b, 2 * odd)):
        for q in range(2):
            out[q * B : (q + 1) * B, :] = mine[first + q, :B, :]


def window(odd, from_a, from_b, own, v_high, v_low):
    for start, tile in (
        ((1 - odd) * (ROW + 2) * B, from_a[...]),
        (odd * (ROW + 2) * B, from_b[...]),
        (2 * B, own),
    ):
        rows = pl.ds(pl.multiple_of(start, B), tile.shape[0])
        v_high[rows, :], v_low[rows, :] = split(tile)


def hand_out(odd, y, to_a, to_b):
    to_a[...] = y[pl.ds(pl.multiple_of((2 - 2 * odd) * B, B), 2 * B), :]
    to_b[...] = y[pl.ds(pl.multiple_of(2 * odd * B, B), 2 * B), :]


def margin_kernel(me, mine, other, from_a, from_b, out, to_a, to_b, full, v_high, v_low):
    _, core = member(me)
    odd = parity(me)
    own = [mine[q, :B, :] for q in range(ROW)]
    window(odd, from_a, from_b, jnp.concatenate(own, axis=0), v_high, v_low)
    for q in range(ROW):

        def put(rows, columns, tile):
            full[q, rows, columns] = tile

        band_rows(B, q, core, mine, other, put)
    for q in range(ROW):
        m_high, m_low = split(full[q])
        rows = slice(q * B, (q + BAND) * B)
        out[q * B : (q + 1) * B, :] = own[q] + product(m_high, m_low, v_high[rows], v_low[rows])
    hand_out(odd, out, to_a, to_b)


def parts_kernel(me, mine, other, out_high, out_low):
    _, core = member(me)
    for q in range(ROW):

        def put(rows, columns, tile):
            out_high[q, rows, columns], out_low[q, rows, columns] = split(tile)

        band_rows(0, q, core, mine, other, put)


def images(scale, m_high, m_low, v_high, v_low):
    for q in range(ROW):
        rows = slice(q * B, (q + BAND) * B)
        yield q, product(m_high[q], m_low[q], v_high[rows], v_low[rows]) * F32(scale)


def apply_kernel(scale, me, m_high, m_low, from_a, from_b, own, out, to_a, to_b, v_high, v_low):
    odd = parity(me)
    window(odd, from_a, from_b, own[...], v_high, v_low)
    for q, value in images(scale, m_high, m_low, v_high, v_low):
        out[q * B : (q + 1) * B, :] = value
    hand_out(odd, out, to_a, to_b)


def last_kernel(scale, me, m_high, m_low, from_a, from_b, own, y0, y1, y2, out, v_high, v_low):
    x, _ = member(me)
    window(parity(me), from_a, from_b, own[...], v_high, v_low)
    for q, y4 in images(scale, m_high, m_low, v_high, v_low):
        rows = slice(q * B, (q + 1) * B)
        out[turn_to(q, x)] = (y0[rows, :] - y2[rows, :]) + y4 + turned(y1[rows, :] - own[rows, :])


def old_kernel(me, coef, c1, c2, c3, other, out_high, out_low):
    x, core = member(me)
    width = coef.shape[3]
    for j, ref in enumerate((coef, c1, c2, c3)):
        q = turn_to(x, j)
        for part in range(2):
            for place, tile in ((core, ref[part, 0]), (1 - core, other[j, part])):
                rows = pl.ds(pl.multiple_of(place * width, width), width)
                columns = pl.ds(pl.multiple_of((part * ROW + q) * B, B), B)
                out_high[rows, columns], out_low[rows, columns] = split(jnp.transpose(tile))


def project_kernel(me, old_high, old_low, new, out):
    x, _ = member(me)
    tiles = [new[turn_to(q, x)] for q in range(ROW)]
    v_high, v_low = split(jnp.concatenate(tiles + [turned(t) for t in tiles], axis=0))
    out[...] = product(old_high[...], old_low[...], v_high, v_low)


def tail_kernel(scale, me, sums, new, *outs):
    x, _ = member(me)
    share = 4
    total = jnp.sum(sums[...].reshape(-1, ROW * share, B), axis=0) * scale
    for j, out in enumerate(outs):
        out[:B, :] = new[j]
        for q in range(ROW):

            @pl.when(q == lax.rem(x + j, ROW))
            def _():
                out[B : B + share, :] = total[q * share : (q + 1) * share, :]


def finish_kernel(me, mine, b1, b2, b3, propagated, owned, held):
    x, _ = member(me)
    share = owned.shape[1]
    for j, ref in enumerate((mine, b1, b2, b3)):
        held[turn_to(x, j)] = ref[...]
    for q in range(ROW):
        columns = slice(q * HALF, (q + 1) * HALF)
        for part in range(2):
            lanes = slice(part * HALF, (part + 1) * HALF)
            propagated[part, 0, :, columns] = held[q, :B, lanes]
            owned[part, :, columns] = held[q, B : B + share, lanes]


def local(rows, coefficients, margin, step_matrix, neighbours, pattern):
    width = coefficients.shape[3]
    domains = rows * ROW
    me = lax.axis_index(("row", "x", "orb")).astype(jnp.int32).reshape(1)
    struct = jax.ShapeDtypeStruct
    tile_bytes = 4 * B * B
    step_flops = 2 * 3 * B * BAND * B * B

    def call(kernel, out_shape, args, flops, moved, name, scratch=(), scalars=1):
        return pl.pallas_call(
            kernel,
            out_shape=out_shape,
            in_specs=[SMEM] * scalars + [VMEM] * (len(args) - scalars),
            out_specs=jax.tree.map(lambda _: VMEM, out_shape),
            scratch_shapes=list(scratch),
            cost_estimate=cost(flops, moved * tile_bytes),
            name=name,
            compiler_params=pltpu.CompilerParams(vmem_limit_bytes=40 * 2**20),
        )(*args)

    def in_row(value, by):
        return lax.ppermute(value, "x", [(x, (x + by) % ROW) for x in range(ROW)])

    def swap(value):
        return lax.ppermute(value, "orb", [(0, 1), (1, 0)])

    def exchange(to_a, to_b):
        def swap_rows(value, first):
            pairs = [(r, r + 1) for r in range(first, rows - 1, 2)]
            return lax.ppermute(value, "row", pairs + [(j, i) for i, j in pairs])

        return [swap_rows(to_a, 0), swap_rows(to_b, 1)]

    def prefetched(kernel, arrays, specs, out_shape, moved, name):
        zeros = (0,) * len(out_shape)
        return pl.pallas_call(
            kernel,
            grid_spec=pltpu.PrefetchScalarGridSpec(
                num_scalar_prefetch=3, grid=(1,), in_specs=specs, out_specs=pl.BlockSpec(out_shape, lambda i, *_: zeros)
            ),
            out_shape=struct(out_shape, F32),
            cost_estimate=cost(10**6, moved * tile_bytes),
            name=name,
        )(me, neighbours, pattern, *arrays)

    half_block = pl.BlockSpec((1, 16, HALF, B), lambda i, where, nbr, pat: (0, 0, lax.rem(where[0], 2), 0))
    whole = pl.BlockSpec(coefficients.shape, lambda i, *_: (0, 0, 0, 0))
    packed = prefetched(
        pack_kernel, (coefficients, margin), [whole, half_block], (ROW, B + BAND * HALF, B), 26, "pack"
    )
    mine = lax.all_to_all(packed, "x", 0, 0, tiled=True)
    state = struct((ROW * B, B), F32)
    edge = struct((2 * B, B), F32)
    parts = [pltpu.VMEM((2 * ROW * B, B), BF16)] * 2
    edges = call(edge_kernel, [edge, edge], [me, mine], 10**5, 8, "edges")
    *edges, held = lax.optimization_barrier((*edges, mine))
    arrived = exchange(*edges)
    other = swap(held)
    edges[0], held = lax.optimization_barrier((edges[0], step_matrix))
    step_half = prefetched(step_kernel, (held,), [half_block], (BAND * HALF, B), 10, "step")
    step_row = [step_half] + [in_row(step_half, j) for j in range(1, ROW)]
    y0, *edges = call(
        margin_kernel, [state, edge, edge], [me, mine, other] + arrived, ROW * step_flops, 60, "margin",
        scratch=[pltpu.VMEM((ROW, B, BAND * B), F32)] + parts,
    )
    parts_type = struct((ROW, B, BAND * B), BF16)
    _, *step_row = lax.optimization_barrier((y0, *step_row))
    step_mine = call(gather_kernel, struct((ROW, BAND * HALF, B), F32), [me] + step_row, 10**5, 20, "step_row")
    step = list(
        call(parts_kernel, [parts_type, parts_type], [me, step_mine, swap(step_mine)], 10**6, 40, "step_parts")
    )

    states = [y0]
    old = [coefficients]
    for n in range(1, ORDER):
        arrived = exchange(*edges)
        *arrived, old[-1], held = lax.optimization_barrier((*arrived, old[-1], coefficients))
        for j in ((), (1,), (2, 3), ())[n]:
            old.append(in_row(held, j))
        y, *edges = call(
            functools.partial(apply_kernel, 1.0 / n), [state, edge, edge], [me] + step + arrived + [states[-1]],
            ROW * step_flops, 40, "apply", scratch=parts,
        )
        states.append(y)
    arrived = exchange(*edges)
    old_stack = jnp.stack([o[:, 0] for o in old])
    old_type = struct((2 * width, 2 * ROW * B), BF16)
    old_high, old_low = call(
        old_kernel, [old_type, old_type], [me] + old + [swap(old_stack)], 10**6, 64, "old_parts"
    )
    arrived[0], old_high = lax.optimization_barrier((arrived[0], old_high))
    y0, y1, y2, y3 = states
    new = call(
        functools.partial(last_kernel, 1.0 / ORDER), struct((ROW, B, B), F32),
        [me] + step + arrived + [y3, y0, y1, y2], ROW * step_flops, 48, "last", scratch=parts,
    )
    partial_value = call(
        project_kernel, struct((2 * width, B), F32), [me, old_high, old_low, new],
        2 * 3 * 2 * width * 2 * ROW * B * B, 44, "project",
    )
    sums = lax.all_to_all(partial_value, "row", 0, 0, tiled=True)
    share = 2 * width // domains
    sent = struct((B + 2 * share, B), F32)
    tail = call(
        functools.partial(tail_kernel, 1.0 / (domains * B)), [sent] * ROW, [me, sums, new], 10**5, 12, "tail"
    )
    tail = [tail[0]] + [in_row(tail[j], j) for j in range(1, ROW)]
    return call(
        finish_kernel, (struct((2, 1, B, width), F32), struct((2, share, width), F32)), [me] + tail, 10**5, 8,
        "finish", scratch=[pltpu.VMEM((ROW, B + 2 * share, B), F32)],
    )


def solution(mesh):
    rows = mesh.shape["space"] // ROW
    grouped = Mesh(mesh.devices.reshape(rows, ROW, mesh.shape["orb"]), ("row", "x", "orb"))
    space = ("row", "x")
    return jax.shard_map(
        functools.partial(local, rows),
        mesh=grouped,
        in_specs=(
            P(None, space, None, "orb"),
            P(space, None, None, None),
            P(space, None, None, None),
            P(space, None),
            P(space, None),
        ),
        out_specs=(P(None, space, None, "orb"), P(None, space, "orb")),
        check_vma=False,
    )
```

```python
import functools

import jax
import jax.numpy as jnp
from jax import lax
from jax.experimental import pallas as pl
from jax.experimental.pallas import tpu as pltpu
from jax.sharding import Mesh, PartitionSpec as P

ORDER = 4
ROW = 4
BAND = 5
B = 128
HALF = B // 2
F32 = jnp.float32
BF16 = jnp.bfloat16

SMEM = pl.BlockSpec(memory_space=pltpu.SMEM)
VMEM = pl.BlockSpec(memory_space=pltpu.VMEM)


def cost(flops, moved):
    return pl.CostEstimate(flops=flops, bytes_accessed=moved, transcendentals=0)


def split(value):
    high = value.astype(BF16)
    return high, (value - high.astype(F32)).astype(BF16)


def product(a_high, a_low, b_high, b_low):
    dot = functools.partial(jnp.dot, preferred_element_type=F32)
    return dot(a_high, b_high) + (dot(a_high, b_low) + dot(a_low, b_high))


def turned(value):
    lane = lax.broadcasted_iota(jnp.int32, value.shape, 1)
    rolled = pltpu.roll(value, HALF, axis=1)
    return jnp.where(lane < HALF, rolled, -rolled)


def member(me):
    return lax.rem(lax.div(me[0], 2), ROW), lax.rem(me[0], 2)


def turn_to(q, x):
    return lax.rem(q - x + ROW, ROW)


def parity(me):
    return lax.rem(lax.div(me[0], 2 * ROW), 2)


def pack_kernel(me, nbr, pat, coef, margin, step, out):
    chunk = pl.program_id(0)

    @pl.when(chunk == 0)
    def _():
        for q in range(ROW):
            columns = slice(q * HALF, (q + 1) * HALF)
            out[q, :B, :] = jnp.concatenate([coef[0, 0, :, columns], coef[1, 0, :, columns]], axis=1)

    first = lax.div(me[0], 2) - 2
    size = margin.shape[2]
    for i, source in enumerate((margin, step)):
        totals = [jnp.zeros((size, B), F32)] * BAND
        for k in range(source.shape[1]):
            block = source[0, k]
            weight = F32(1.0) if k == 0 else pat[0, k].astype(F32)
            for d in range(BAND):
                totals[d] = totals[d] + block * jnp.where(nbr[0, k] == first + d, weight, F32(0.0))
        for d in range(BAND):
            start = pl.multiple_of(B + (i * BAND + d) * HALF + chunk * size, size)
            for q in range(ROW):
                out[q, pl.ds(start, size), :] = totals[d]


def place_half(out, q, place, source, first):
    rows = pl.ds(pl.multiple_of(place * HALF, HALF), HALF)
    for d in range(BAND):
        start = first + d * HALF
        yield q, rows, slice(d * B, (d + 1) * B), source(slice(start, start + HALF))


def edge_kernel(me, mine, to_a, to_b):
    odd = parity(me)
    for out, first in ((to_a, 2 - 2 * odd), (to_b, 2 * odd)):
        for q in range(2):
            out[q * B : (q + 1) * B, :] = mine[first + q, :B, :]
            start = 2 * B + q * BAND * HALF
            out[start : start + BAND * HALF, :] = mine[first + q, B + BAND * HALF :, :]


def window(odd, from_a, from_b, own, v_high, v_low):
    reach, size = from_a.shape[0], own.shape[0]
    v_high[reach : reach + size, :], v_low[reach : reach + size, :] = split(own)
    for start, tile in (((1 - odd) * (reach + size), from_a), (odd * (reach + size), from_b)):
        rows = pl.ds(pl.multiple_of(start, B), reach)
        v_high[rows, :], v_low[rows, :] = split(tile)


def margin_kernel(me, mine, other, from_a, from_b, out, full, v_high, v_low):
    _, core = member(me)
    own = [mine[q, :B, :] for q in range(ROW)]
    window(parity(me), from_a[: 2 * B, :], from_b[: 2 * B, :], jnp.concatenate(own, axis=0), v_high, v_low)
    for q in range(ROW):
        for place, ref in ((core, mine), (1 - core, other)):
            for _, rows, columns, tile in place_half(full, q, place, lambda at: ref[q, at, :], B):
                full[q, rows, columns] = tile
    for q in range(ROW):
        m_high, m_low = split(full[q])
        rows = slice(q * B, (q + BAND) * B)
        out[q * B : (q + 1) * B, :] = own[q] + product(m_high, m_low, v_high[rows], v_low[rows])


def parts_kernel(me, mine, other, from_a, from_b, other_a, other_b, out_high, out_low):
    _, core = member(me)
    odd = parity(me)
    for q in range(ROW):
        for place, ref in ((core, mine), (1 - core, other)):
            for to, rows, columns, tile in place_half(out_high, q + 2, place, lambda at: ref[q, at, :], B + BAND * HALF):
                out_high[to, rows, columns], out_low[to, rows, columns] = split(tile)
    for start, own, across in (((1 - odd) * 6, from_a, other_a), (odd * 6, from_b, other_b)):
        for q in range(2):
            for place, ref in ((core, own), (1 - core, across)):
                first = 2 * B + q * BAND * HALF
                for to, rows, columns, tile in place_half(out_high, start + q, place, lambda at: ref[at, :], first):
                    out_high[to, rows, columns], out_low[to, rows, columns] = split(tile)


def two_steps(n, me, m_high, m_low, from_a, from_b, own, v_high, v_low, w_high, w_low):
    window(parity(me), from_a[...], from_b[...], own[...], v_high, v_low)
    firsts = []
    for q in range(2 * ROW):
        rows = slice(q * B, (q + BAND) * B)
        value = product(m_high[q], m_low[q], v_high[rows], v_low[rows]) * F32(1.0 / n)
        w_high[q * B : (q + 1) * B, :], w_low[q * B : (q + 1) * B, :] = split(value)
        firsts.append(value)
    for q in range(ROW):
        rows = slice(q * B, (q + BAND) * B)
        second = product(m_high[q + 2], m_low[q + 2], w_high[rows], w_low[rows]) * F32(1.0 / (n + 1))
        yield q, firsts[q + 2], second


def two_kernel(n, me, m_high, m_low, from_a, from_b, own, first, second, *scratch):
    for q, a, b in two_steps(n, me, m_high, m_low, from_a, from_b, own, *scratch):
        first[q * B : (q + 1) * B, :] = a
        second[q * B : (q + 1) * B, :] = b


def last_kernel(n, me, m_high, m_low, from_a, from_b, own, y0, y1, out, *scratch):
    x, _ = member(me)
    for q, y3, y4 in two_steps(n, me, m_high, m_low, from_a, from_b, own, *scratch):
        rows = slice(q * B, (q + 1) * B)
        out[turn_to(q, x)] = (y0[rows, :] - own[rows, :]) + y4 + turned(y1[rows, :] - y3)


def old_kernel(me, coef, c1, c2, c3, other, out_high, out_low):
    x, core = member(me)
    width = coef.shape[3]
    for j, ref in enumerate((coef, c1, c2, c3)):
        q = turn_to(x, j)
        for part in range(2):
            for place, tile in ((core, ref[part, 0]), (1 - core, other[j, part])):
                rows = pl.ds(pl.multiple_of(place * width, width), width)
                columns = pl.ds(pl.multiple_of((part * ROW + q) * B, B), B)
                out_high[rows, columns], out_low[rows, columns] = split(jnp.transpose(tile))


def project_kernel(me, old_high, old_low, new, out):
    x, _ = member(me)
    tiles = [new[turn_to(q, x)] for q in range(ROW)]
    v_high, v_low = split(jnp.concatenate(tiles + [turned(t) for t in tiles], axis=0))
    out[...] = product(old_high[...], old_low[...], v_high, v_low)


def tail_kernel(scale, me, sums, new, *outs):
    x, _ = member(me)
    share = 4
    total = jnp.sum(sums[...].reshape(-1, ROW * share, B), axis=0) * scale
    for j, out in enumerate(outs):
        out[:B, :] = new[j]
        for q in range(ROW):

            @pl.when(q == lax.rem(x + j, ROW))
            def _():
                out[B : B + share, :] = total[q * share : (q + 1) * share, :]


def finish_kernel(me, mine, b1, b2, b3, propagated, owned, held):
    x, _ = member(me)
    share = owned.shape[1]
    for j, ref in enumerate((mine, b1, b2, b3)):
        held[turn_to(x, j)] = ref[...]
    for q in range(ROW):
        columns = slice(q * HALF, (q + 1) * HALF)
        for part in range(2):
            lanes = slice(part * HALF, (part + 1) * HALF)
            propagated[part, 0, :, columns] = held[q, :B, lanes]
            owned[part, :, columns] = held[q, B : B + share, lanes]


def local(rows, coefficients, margin, step_matrix, neighbours, pattern):
    width = coefficients.shape[3]
    domains = rows * ROW
    me = lax.axis_index(("row", "x", "orb")).astype(jnp.int32).reshape(1)
    struct = jax.ShapeDtypeStruct
    tile_bytes = 4 * B * B
    step_flops = 2 * 3 * B * BAND * B * B

    def call(kernel, out_shape, args, flops, moved, name, scratch=(), scalars=1):
        return pl.pallas_call(
            kernel,
            out_shape=out_shape,
            in_specs=[SMEM] * scalars + [VMEM] * (len(args) - scalars),
            out_specs=jax.tree.map(lambda _: VMEM, out_shape),
            scratch_shapes=list(scratch),
            cost_estimate=cost(flops, moved * tile_bytes),
            name=name,
            compiler_params=pltpu.CompilerParams(vmem_limit_bytes=40 * 2**20),
        )(*args)

    def in_row(value, by):
        return lax.ppermute(value, "x", [(x, (x + by) % ROW) for x in range(ROW)])

    def swap(value):
        return lax.ppermute(value, "orb", [(0, 1), (1, 0)])

    def exchange(to_a, to_b):
        def swap_rows(value, first):
            pairs = [(r, r + 1) for r in range(first, rows - 1, 2)]
            return lax.ppermute(value, "row", pairs + [(j, i) for i, j in pairs])

        return [swap_rows(to_a, 0), swap_rows(to_b, 1)]

    chunks = 4
    slots = neighbours.shape[1]
    half_block = pl.BlockSpec(
        (1, slots, HALF // chunks, B), lambda i, where, nbr, pat: (0, 0, lax.rem(where[0], 2) * chunks + i, 0)
    )
    packed_shape = (ROW, B + 2 * BAND * HALF, B)
    packed = pl.pallas_call(
        pack_kernel,
        grid_spec=pltpu.PrefetchScalarGridSpec(
            num_scalar_prefetch=3,
            grid=(chunks,),
            in_specs=[pl.BlockSpec(coefficients.shape, lambda i, *_: (0, 0, 0, 0)), half_block, half_block],
            out_specs=pl.BlockSpec(packed_shape, lambda i, *_: (0, 0, 0)),
        ),
        out_shape=struct(packed_shape, F32),
        cost_estimate=cost(10**6, 44 * tile_bytes),
        name="pack",
    )(me, neighbours, pattern, coefficients, margin, step_matrix)
    mine = lax.all_to_all(packed, "x", 0, 0, tiled=True)

    state = struct((ROW * B, B), F32)
    edge = struct((2 * B + 2 * BAND * HALF, B), F32)
    edges = call(edge_kernel, [edge, edge], [me, mine], 10**5, 28, "edges")
    *edges, held = lax.optimization_barrier((*edges, mine))
    other = swap(held)
    from_a, from_b = exchange(*edges)
    y0 = call(
        margin_kernel, state, [me, mine, other, from_a, from_b], ROW * step_flops, 60, "margin",
        scratch=[pltpu.VMEM((ROW, B, BAND * B), F32)] + [pltpu.VMEM((2 * ROW * B, B), BF16)] * 2,
    )
    parts_type = struct((2 * ROW, B, BAND * B), BF16)
    step = list(
        call(
            parts_kernel, [parts_type, parts_type], [me, mine, other, from_a, from_b, swap(from_a), swap(from_b)],
            10**6, 80, "step_parts",
        )
    )
    scratch = [pltpu.VMEM((3 * ROW * B, B), BF16)] * 2 + [pltpu.VMEM((2 * ROW * B, B), BF16)] * 2
    arrived = exchange(y0, y0)

    _, held = lax.optimization_barrier((step[0], coefficients))
    old = [coefficients] + [in_row(held, j) for j in range(1, ROW)]
    y1, y2 = call(
        functools.partial(two_kernel, 1), [state, state], [me] + step + arrived + [y0], 3 * ROW * step_flops, 64,
        "two", scratch=scratch,
    )
    _, *old = lax.optimization_barrier((y2, *old))
    arrived = exchange(y2, y2)
    old_stack = jnp.stack([o[:, 0] for o in old])
    old_type = struct((2 * width, 2 * ROW * B), BF16)
    old_high, old_low = call(
        old_kernel, [old_type, old_type], [me] + old + [swap(old_stack)], 10**6, 64, "old_parts"
    )
    arrived[0], old_high = lax.optimization_barrier((arrived[0], old_high))
    new = call(
        functools.partial(last_kernel, 3), struct((ROW, B, B), F32), [me] + step + arrived + [y2, y0, y1],
        3 * ROW * step_flops, 72, "last", scratch=scratch,
    )
    partial_value = call(
        project_kernel, struct((2 * width, B), F32), [me, old_high, old_low, new],
        2 * 3 * 2 * width * 2 * ROW * B * B, 44, "project",
    )
    sums = lax.all_to_all(partial_value, "row", 0, 0, tiled=True)
    share = 2 * width // domains
    sent = struct((B + 2 * share, B), F32)
    tail = call(
        functools.partial(tail_kernel, 1.0 / (domains * B)), [sent] * ROW, [me, sums, new], 10**5, 12, "tail"
    )
    tail = [tail[0]] + [in_row(tail[j], j) for j in range(1, ROW)]
    return call(
        finish_kernel, (struct((2, 1, B, width), F32), struct((2, share, width), F32)), [me] + tail, 10**5, 8,
        "finish", scratch=[pltpu.VMEM((ROW, B + 2 * share, B), F32)],
    )


def solution(mesh):
    rows = mesh.shape["space"] // ROW
    grouped = Mesh(mesh.devices.reshape(rows, ROW, mesh.shape["orb"]), ("row", "x", "orb"))
    space = ("row", "x")
    return jax.shard_map(
        functools.partial(local, rows),
        mesh=grouped,
        in_specs=(
            P(None, space, None, "orb"),
            P(space, None, None, None),
            P(space, None, None, None),
            P(space, None),
            P(space, None),
        ),
        out_specs=(P(None, space, None, "orb"), P(None, space, "orb")),
        check_vma=False,
    )
```

```python
import functools

import jax
import jax.numpy as jnp
from jax import lax
from jax.experimental import pallas as pl
from jax.experimental.pallas import tpu as pltpu
from jax.sharding import Mesh, PartitionSpec as P

ORDER = 4
ROW = 4
BAND = 5
B = 128
HALF = B // 2
F32 = jnp.float32
BF16 = jnp.bfloat16

SMEM = pl.BlockSpec(memory_space=pltpu.SMEM)
VMEM = pl.BlockSpec(memory_space=pltpu.VMEM)


def cost(flops, moved):
    return pl.CostEstimate(flops=flops, bytes_accessed=moved, transcendentals=0)


def split(value):
    high = value.astype(BF16)
    return high, (value - high.astype(F32)).astype(BF16)


def product(a_high, a_low, b_high, b_low):
    dot = functools.partial(jnp.dot, preferred_element_type=F32)
    return dot(a_high, b_high) + (dot(a_high, b_low) + dot(a_low, b_high))


def turned(value):
    lane = lax.broadcasted_iota(jnp.int32, value.shape, 1)
    rolled = pltpu.roll(value, HALF, axis=1)
    return jnp.where(lane < HALF, rolled, -rolled)


def member(me):
    return lax.rem(lax.div(me[0], 2), ROW), lax.rem(me[0], 2)


def turn_to(q, x):
    return lax.rem(q - x + ROW, ROW)


def parity(me):
    return lax.rem(lax.div(me[0], 2 * ROW), 2)


def pack_kernel(me, nbr, pat, coef, margin, step, out):
    chunk = pl.program_id(0)

    @pl.when(chunk == 0)
    def _():
        for q in range(ROW):
            columns = slice(q * HALF, (q + 1) * HALF)
            out[q, :B, :] = jnp.concatenate([coef[0, 0, :, columns], coef[1, 0, :, columns]], axis=1)

    first = lax.div(me[0], 2) - 2
    size = margin.shape[2]
    for i, source in enumerate((margin, step)):
        totals = [jnp.zeros((size, B), F32)] * BAND
        for k in range(source.shape[1]):
            block = source[0, k]
            weight = F32(1.0) if k == 0 else pat[0, k].astype(F32)
            for d in range(BAND):
                totals[d] = totals[d] + block * jnp.where(nbr[0, k] == first + d, weight, F32(0.0))
        for d in range(BAND):
            start = pl.multiple_of(B + (i * BAND + d) * HALF + chunk * size, size)
            for q in range(ROW):
                out[q, pl.ds(start, size), :] = totals[d]


def place_half(out, q, place, source, first):
    rows = pl.ds(pl.multiple_of(place * HALF, HALF), HALF)
    for d in range(BAND):
        start = first + d * HALF
        yield q, rows, slice(d * B, (d + 1) * B), source(slice(start, start + HALF))


def edge_kernel(me, mine, to_a, to_b):
    odd = parity(me)
    for out, first in ((to_a, 2 - 2 * odd), (to_b, 2 * odd)):
        for q in range(2):
            out[q * B : (q + 1) * B, :] = mine[first + q, :B, :]
            start = 2 * B + q * BAND * HALF
            out[start : start + BAND * HALF, :] = mine[first + q, B + BAND * HALF :, :]


def window(odd, from_a, from_b, own, v_high, v_low):
    reach, size = from_a.shape[0], own.shape[0]
    v_high[reach : reach + size, :], v_low[reach : reach + size, :] = split(own)
    for start, tile in (((1 - odd) * (reach + size), from_a), (odd * (reach + size), from_b)):
        rows = pl.ds(pl.multiple_of(start, B), reach)
        v_high[rows, :], v_low[rows, :] = split(tile)


def margin_kernel(me, mine, other, from_a, from_b, out, full, v_high, v_low):
    _, core = member(me)
    own = [mine[q, :B, :] for q in range(ROW)]
    window(parity(me), from_a[: 2 * B, :], from_b[: 2 * B, :], jnp.concatenate(own, axis=0), v_high, v_low)
    for q in range(ROW):
        for place, ref in ((core, mine), (1 - core, other)):
            for _, rows, columns, tile in place_half(full, q, place, lambda at: ref[q, at, :], B):
                full[q, rows, columns] = tile
    for q in range(ROW):
        m_high, m_low = split(full[q])
        rows = slice(q * B, (q + BAND) * B)
        out[q * B : (q + 1) * B, :] = own[q] + product(m_high, m_low, v_high[rows], v_low[rows])


def parts_kernel(me, mine, other, from_a, from_b, other_a, other_b, out_high, out_low):
    _, core = member(me)
    odd = parity(me)
    for q in range(ROW):
        for place, ref in ((core, mine), (1 - core, other)):
            for to, rows, columns, tile in place_half(out_high, q + 2, place, lambda at: ref[q, at, :], B + BAND * HALF):
                out_high[to, rows, columns], out_low[to, rows, columns] = split(tile)
    for start, own, across in (((1 - odd) * 6, from_a, other_a), (odd * 6, from_b, other_b)):
        for q in range(2):
            for place, ref in ((core, own), (1 - core, across)):
                first = 2 * B + q * BAND * HALF
                for to, rows, columns, tile in place_half(out_high, start + q, place, lambda at: ref[at, :], first):
                    out_high[to, rows, columns], out_low[to, rows, columns] = split(tile)


def two_steps(n, me, m_high, m_low, from_a, from_b, own, v_high, v_low, w_high, w_low):
    window(parity(me), from_a[...], from_b[...], own[...], v_high, v_low)
    firsts = []
    for q in range(2 * ROW):
        rows = slice(q * B, (q + BAND) * B)
        value = product(m_high[q], m_low[q], v_high[rows], v_low[rows]) * F32(1.0 / n)
        w_high[q * B : (q + 1) * B, :], w_low[q * B : (q + 1) * B, :] = split(value)
        firsts.append(value)
    for q in range(ROW):
        rows = slice(q * B, (q + BAND) * B)
        second = product(m_high[q + 2], m_low[q + 2], w_high[rows], w_low[rows]) * F32(1.0 / (n + 1))
        yield q, firsts[q + 2], second


def two_kernel(n, me, m_high, m_low, from_a, from_b, own, first, second, *scratch):
    for q, a, b in two_steps(n, me, m_high, m_low, from_a, from_b, own, *scratch):
        first[q * B : (q + 1) * B, :] = a
        second[q * B : (q + 1) * B, :] = b


def last_kernel(n, me, m_high, m_low, from_a, from_b, own, y0, y1, out, *scratch):
    x, _ = member(me)
    for q, y3, y4 in two_steps(n, me, m_high, m_low, from_a, from_b, own, *scratch):
        rows = slice(q * B, (q + 1) * B)
        out[turn_to(q, x)] = (y0[rows, :] - own[rows, :]) + y4 + turned(y1[rows, :] - y3)


def old_kernel(me, c0, c1, c2, c3, o0, o1, o2, o3, out_high, out_low):
    x, core = member(me)
    width = c0.shape[3]
    for j, (ref, other) in enumerate(((c0, o0), (c1, o1), (c2, o2), (c3, o3))):
        q = turn_to(x, j)
        for part in range(2):
            for place, tile in ((core, ref[part, 0]), (1 - core, other[part, 0])):
                rows = pl.ds(pl.multiple_of(place * width, width), width)
                columns = pl.ds(pl.multiple_of((part * ROW + q) * B, B), B)
                out_high[rows, columns], out_low[rows, columns] = split(jnp.transpose(tile))


def project_kernel(me, old_high, old_low, new, out):
    x, _ = member(me)
    tiles = [new[turn_to(q, x)] for q in range(ROW)]
    v_high, v_low = split(jnp.concatenate(tiles + [turned(t) for t in tiles], axis=0))
    out[...] = product(old_high[...], old_low[...], v_high, v_low)


def tail_kernel(scale, me, sums, new, *outs):
    x, _ = member(me)
    share = 4
    total = jnp.sum(sums[...].reshape(-1, ROW * share, B), axis=0) * scale
    for j, out in enumerate(outs):
        out[:B, :] = new[j]
        for q in range(ROW):

            @pl.when(q == lax.rem(x + j, ROW))
            def _():
                out[B : B + share, :] = total[q * share : (q + 1) * share, :]


def finish_kernel(me, mine, b1, b2, b3, propagated, owned, held):
    x, _ = member(me)
    share = owned.shape[1]
    for j, ref in enumerate((mine, b1, b2, b3)):
        held[turn_to(x, j)] = ref[...]
    for q in range(ROW):
        columns = slice(q * HALF, (q + 1) * HALF)
        for part in range(2):
            lanes = slice(part * HALF, (part + 1) * HALF)
            propagated[part, 0, :, columns] = held[q, :B, lanes]
            owned[part, :, columns] = held[q, B : B + share, lanes]


def local(rows, coefficients, margin, step_matrix, neighbours, pattern):
    width = coefficients.shape[3]
    domains = rows * ROW
    me = lax.axis_index(("row", "x", "orb")).astype(jnp.int32).reshape(1)
    struct = jax.ShapeDtypeStruct
    tile_bytes = 4 * B * B
    step_flops = 2 * 3 * B * BAND * B * B

    def call(kernel, out_shape, args, flops, moved, name, scratch=(), scalars=1):
        return pl.pallas_call(
            kernel,
            out_shape=out_shape,
            in_specs=[SMEM] * scalars + [VMEM] * (len(args) - scalars),
            out_specs=jax.tree.map(lambda _: VMEM, out_shape),
            scratch_shapes=list(scratch),
            cost_estimate=cost(flops, moved * tile_bytes),
            name=name,
            compiler_params=pltpu.CompilerParams(vmem_limit_bytes=40 * 2**20),
        )(*args)

    def in_row(value, by):
        return lax.ppermute(value, "x", [(x, (x + by) % ROW) for x in range(ROW)])

    def swap(value):
        return lax.ppermute(value, "orb", [(0, 1), (1, 0)])

    def exchange(to_a, to_b):
        def swap_rows(value, first):
            pairs = [(r, r + 1) for r in range(first, rows - 1, 2)]
            return lax.ppermute(value, "row", pairs + [(j, i) for i, j in pairs])

        return [swap_rows(to_a, 0), swap_rows(to_b, 1)]

    chunks = 1
    slots = neighbours.shape[1]
    half_block = pl.BlockSpec(
        (1, slots, HALF // chunks, B), lambda i, where, nbr, pat: (0, 0, lax.rem(where[0], 2) * chunks + i, 0)
    )
    packed_shape = (ROW, B + 2 * BAND * HALF, B)
    packed = pl.pallas_call(
        pack_kernel,
        grid_spec=pltpu.PrefetchScalarGridSpec(
            num_scalar_prefetch=3,
            grid=(chunks,),
            in_specs=[pl.BlockSpec(coefficients.shape, lambda i, *_: (0, 0, 0, 0)), half_block, half_block],
            out_specs=pl.BlockSpec(packed_shape, lambda i, *_: (0, 0, 0)),
        ),
        out_shape=struct(packed_shape, F32),
        cost_estimate=cost(10**6, 44 * tile_bytes),
        name="pack",
    )(me, neighbours, pattern, coefficients, margin, step_matrix)
    mine = lax.all_to_all(packed, "x", 0, 0, tiled=True)

    state = struct((ROW * B, B), F32)
    edge = struct((2 * B + 2 * BAND * HALF, B), F32)
    edges = call(edge_kernel, [edge, edge], [me, mine], 10**5, 28, "edges")
    *edges, held = lax.optimization_barrier((*edges, mine))
    other = swap(held)
    from_a, from_b = exchange(*edges)

    _, held = lax.optimization_barrier((edges[0], coefficients))
    old = [coefficients, in_row(held, 1), None, in_row(held, ROW - 1)]
    _, held = lax.optimization_barrier((other, coefficients))
    old[2] = in_row(held, 2)
    from_b, old[1], old[3] = lax.optimization_barrier((from_b, old[1], old[3]))
    y0 = call(
        margin_kernel, state, [me, mine, other, from_a, from_b], ROW * step_flops, 60, "margin",
        scratch=[pltpu.VMEM((ROW, B, BAND * B), F32)] + [pltpu.VMEM((2 * ROW * B, B), BF16)] * 2,
    )
    parts_type = struct((2 * ROW, B, BAND * B), BF16)
    step = list(
        call(
            parts_kernel, [parts_type, parts_type], [me, mine, other, from_a, from_b, swap(from_a), swap(from_b)],
            10**6, 80, "step_parts",
        )
    )
    scratch = [pltpu.VMEM((3 * ROW * B, B), BF16)] * 2 + [pltpu.VMEM((2 * ROW * B, B), BF16)] * 2
    arrived = exchange(y0, y0)
    arrived[0], old[2] = lax.optimization_barrier((arrived[0], old[2]))
    y1, y2 = call(
        functools.partial(two_kernel, 1), [state, state], [me] + step + arrived + [y0], 3 * ROW * step_flops, 64,
        "two", scratch=scratch,
    )
    arrived = exchange(y2, y2)
    old_type = struct((2 * width, 2 * ROW * B), BF16)
    old_high, old_low = call(
        old_kernel, [old_type, old_type], [me] + old + [swap(o) for o in old], 10**6, 64, "old_parts"
    )
    arrived[0], old_high = lax.optimization_barrier((arrived[0], old_high))
    new = call(
        functools.partial(last_kernel, 3), struct((ROW, B, B), F32), [me] + step + arrived + [y2, y0, y1],
        3 * ROW * step_flops, 72, "last", scratch=scratch,
    )
    partial_value = call(
        project_kernel, struct((2 * width, B), F32), [me, old_high, old_low, new],
        2 * 3 * 2 * width * 2 * ROW * B * B, 44, "project",
    )
    sums = lax.all_to_all(partial_value, "row", 0, 0, tiled=True)
    share = 2 * width // domains
    sent = struct((B + 2 * share, B), F32)
    tail = call(
        functools.partial(tail_kernel, 1.0 / (domains * B)), [sent] * ROW, [me, sums, new], 10**5, 12, "tail"
    )
    tail = [tail[0]] + [in_row(tail[j], j) for j in range(1, ROW)]
    return call(
        finish_kernel, (struct((2, 1, B, width), F32), struct((2, share, width), F32)), [me] + tail, 10**5, 8,
        "finish", scratch=[pltpu.VMEM((ROW, B + 2 * share, B), F32)],
    )


def solution(mesh):
    rows = mesh.shape["space"] // ROW
    grouped = Mesh(mesh.devices.reshape(rows, ROW, mesh.shape["orb"]), ("row", "x", "orb"))
    space = ("row", "x")
    return jax.shard_map(
        functools.partial(local, rows),
        mesh=grouped,
        in_specs=(
            P(None, space, None, "orb"),
            P(space, None, None, None),
            P(space, None, None, None),
            P(space, None),
            P(space, None),
        ),
        out_specs=(P(None, space, None, "orb"), P(None, space, "orb")),
        check_vma=False,
    )
```

```python
import functools

import jax
import jax.numpy as jnp
from jax import lax
from jax.experimental import pallas as pl
from jax.experimental.pallas import tpu as pltpu
from jax.sharding import Mesh, PartitionSpec as P

ORDER = 4
ROW = 4
BAND = 5
B = 128
HALF = B // 2
F32 = jnp.float32
BF16 = jnp.bfloat16

SMEM = pl.BlockSpec(memory_space=pltpu.SMEM)
VMEM = pl.BlockSpec(memory_space=pltpu.VMEM)


def cost(flops, moved):
    return pl.CostEstimate(flops=flops, bytes_accessed=moved, transcendentals=0)


def split(value):
    high = value.astype(BF16)
    return high, (value - high.astype(F32)).astype(BF16)


def product(a_high, a_low, b_high, b_low):
    dot = functools.partial(jnp.dot, preferred_element_type=F32)
    return dot(a_high, b_high) + (dot(a_high, b_low) + dot(a_low, b_high))


def turned(value):
    lane = lax.broadcasted_iota(jnp.int32, value.shape, 1)
    rolled = pltpu.roll(value, HALF, axis=1)
    return jnp.where(lane < HALF, rolled, -rolled)


def member(me):
    return lax.rem(lax.div(me[0], 2), ROW), lax.rem(me[0], 2)


def turn_to(q, x):
    return lax.rem(q - x + ROW, ROW)


def parity(me):
    return 1 - lax.rem(lax.div(me[0], 2 * ROW), 2)


def pack_kernel(me, nbr, pat, coef, margin, step, out):
    chunk = pl.program_id(0)

    @pl.when(chunk == 0)
    def _():
        for q in range(ROW):
            columns = slice(q * HALF, (q + 1) * HALF)
            out[q, :B, :] = jnp.concatenate([coef[0, 0, :, columns], coef[1, 0, :, columns]], axis=1)

    first = lax.div(me[0], 2) - 2
    size = margin.shape[2]
    for i, source in enumerate((margin, step)):
        totals = [jnp.zeros((size, B), F32)] * BAND
        for k in range(source.shape[1]):
            block = source[0, k]
            weight = F32(1.0) if k == 0 else pat[0, k].astype(F32)
            for d in range(BAND):
                totals[d] = totals[d] + block * jnp.where(nbr[0, k] == first + d, weight, F32(0.0))
        for d in range(BAND):
            start = pl.multiple_of(B + (i * BAND + d) * HALF + chunk * size, size)
            for q in range(ROW):
                out[q, pl.ds(start, size), :] = totals[d]


def place_half(out, q, place, source, first):
    rows = pl.ds(pl.multiple_of(place * HALF, HALF), HALF)
    for d in range(BAND):
        start = first + d * HALF
        yield q, rows, slice(d * B, (d + 1) * B), source(slice(start, start + HALF))


def edge_kernel(me, mine, to_a, to_b):
    odd = parity(me)
    for out, first in ((to_a, 2 - 2 * odd), (to_b, 2 * odd)):
        for q in range(2):
            out[q * B : (q + 1) * B, :] = mine[first + q, :B, :]
            start = 2 * B + q * BAND * HALF
            out[start : start + BAND * HALF, :] = mine[first + q, B + BAND * HALF :, :]


def window(odd, from_a, from_b, own, v_high, v_low):
    reach, size = from_a.shape[0], own.shape[0]
    v_high[reach : reach + size, :], v_low[reach : reach + size, :] = split(own)
    for start, tile in (((1 - odd) * (reach + size), from_a), (odd * (reach + size), from_b)):
        rows = pl.ds(pl.multiple_of(start, B), reach)
        v_high[rows, :], v_low[rows, :] = split(tile)


def margin_kernel(me, mine, other, from_a, from_b, out, full, v_high, v_low):
    _, core = member(me)
    own = [mine[q, :B, :] for q in range(ROW)]
    window(parity(me), from_a[: 2 * B, :], from_b[: 2 * B, :], jnp.concatenate(own, axis=0), v_high, v_low)
    for q in range(ROW):
        for place, ref in ((core, mine), (1 - core, other)):
            for _, rows, columns, tile in place_half(full, q, place, lambda at: ref[q, at, :], B):
                full[q, rows, columns] = tile
    for q in range(ROW):
        m_high, m_low = split(full[q])
        rows = slice(q * B, (q + BAND) * B)
        out[q * B : (q + 1) * B, :] = own[q] + product(m_high, m_low, v_high[rows], v_low[rows])


def parts_kernel(me, mine, other, from_a, from_b, other_a, other_b, out_high, out_low):
    _, core = member(me)
    odd = parity(me)
    for q in range(ROW):
        for place, ref in ((core, mine), (1 - core, other)):
            for to, rows, columns, tile in place_half(out_high, q + 2, place, lambda at: ref[q, at, :], B + BAND * HALF):
                out_high[to, rows, columns], out_low[to, rows, columns] = split(tile)
    for start, own, across in (((1 - odd) * 6, from_a, other_a), (odd * 6, from_b, other_b)):
        for q in range(2):
            for place, ref in ((core, own), (1 - core, across)):
                first = 2 * B + q * BAND * HALF
                for to, rows, columns, tile in place_half(out_high, start + q, place, lambda at: ref[at, :], first):
                    out_high[to, rows, columns], out_low[to, rows, columns] = split(tile)


def two_steps(n, me, m_high, m_low, from_a, from_b, own, v_high, v_low, w_high, w_low):
    window(parity(me), from_a[...], from_b[...], own[...], v_high, v_low)
    firsts = []
    for q in range(2 * ROW):
        rows = slice(q * B, (q + BAND) * B)
        value = product(m_high[q], m_low[q], v_high[rows], v_low[rows]) * F32(1.0 / n)
        w_high[q * B : (q + 1) * B, :], w_low[q * B : (q + 1) * B, :] = split(value)
        firsts.append(value)
    for q in range(ROW):
        rows = slice(q * B, (q + BAND) * B)
        second = product(m_high[q + 2], m_low[q + 2], w_high[rows], w_low[rows]) * F32(1.0 / (n + 1))
        yield q, firsts[q + 2], second


def two_kernel(n, me, m_high, m_low, from_a, from_b, own, first, second, *scratch):
    for q, a, b in two_steps(n, me, m_high, m_low, from_a, from_b, own, *scratch):
        first[q * B : (q + 1) * B, :] = a
        second[q * B : (q + 1) * B, :] = b


def last_kernel(n, me, m_high, m_low, from_a, from_b, own, y0, y1, out, *scratch):
    x, _ = member(me)
    for q, y3, y4 in two_steps(n, me, m_high, m_low, from_a, from_b, own, *scratch):
        rows = slice(q * B, (q + 1) * B)
        out[turn_to(q, x)] = (y0[rows, :] - own[rows, :]) + y4 + turned(y1[rows, :] - y3)


def old_kernel(me, c0, c1, c2, c3, o0, o1, o2, o3, out_high, out_low):
    x, core = member(me)
    width = c0.shape[3]
    for j, (ref, other) in enumerate(((c0, o0), (c1, o1), (c2, o2), (c3, o3))):
        q = turn_to(x, j)
        for part in range(2):
            for place, tile in ((core, ref[part, 0]), (1 - core, other[part, 0])):
                rows = pl.ds(pl.multiple_of(place * width, width), width)
                columns = pl.ds(pl.multiple_of((part * ROW + q) * B, B), B)
                out_high[rows, columns], out_low[rows, columns] = split(jnp.transpose(tile))


def project_kernel(me, old_high, old_low, new, out):
    x, _ = member(me)
    tiles = [new[turn_to(q, x)] for q in range(ROW)]
    v_high, v_low = split(jnp.concatenate(tiles + [turned(t) for t in tiles], axis=0))
    out[...] = product(old_high[...], old_low[...], v_high, v_low)


def tail_kernel(scale, me, sums, new, *outs):
    x, _ = member(me)
    share = 4
    total = jnp.sum(sums[...].reshape(-1, ROW * share, B), axis=0) * scale
    for j, out in enumerate(outs):
        out[:B, :] = new[j]
        for q in range(ROW):

            @pl.when(q == lax.rem(x + j, ROW))
            def _():
                out[B : B + share, :] = total[q * share : (q + 1) * share, :]


def finish_kernel(me, mine, b1, b2, b3, propagated, owned, held):
    x, _ = member(me)
    share = owned.shape[1]
    for j, ref in enumerate((mine, b1, b2, b3)):
        held[turn_to(x, j)] = ref[...]
    for q in range(ROW):
        columns = slice(q * HALF, (q + 1) * HALF)
        for part in range(2):
            lanes = slice(part * HALF, (part + 1) * HALF)
            propagated[part, 0, :, columns] = held[q, :B, lanes]
            owned[part, :, columns] = held[q, B : B + share, lanes]


def local(rows, coefficients, margin, step_matrix, neighbours, pattern):
    width = coefficients.shape[3]
    domains = rows * ROW
    me = lax.axis_index(("row", "x", "orb")).astype(jnp.int32).reshape(1)
    struct = jax.ShapeDtypeStruct
    tile_bytes = 4 * B * B
    step_flops = 2 * 3 * B * BAND * B * B

    def call(kernel, out_shape, args, flops, moved, name, scratch=(), scalars=1):
        return pl.pallas_call(
            kernel,
            out_shape=out_shape,
            in_specs=[SMEM] * scalars + [VMEM] * (len(args) - scalars),
            out_specs=jax.tree.map(lambda _: VMEM, out_shape),
            scratch_shapes=list(scratch),
            cost_estimate=cost(flops, moved * tile_bytes),
            name=name,
            compiler_params=pltpu.CompilerParams(vmem_limit_bytes=16 * 2**20),
        )(*args)

    def in_row(value, by):
        return lax.ppermute(value, "x", [(x, (x + by) % ROW) for x in range(ROW)])

    def swap(value):
        return lax.ppermute(value, "orb", [(0, 1), (1, 0)])

    def exchange(to_a, to_b):
        def swap_rows(value, first):
            pairs = [(r, r + 1) for r in range(first, rows - 1, 2)]
            return lax.ppermute(value, "row", pairs + [(j, i) for i, j in pairs])

        return [swap_rows(to_a, 1), swap_rows(to_b, 0)]

    chunks = 1
    slots = neighbours.shape[1]
    half_block = pl.BlockSpec(
        (1, slots, HALF // chunks, B), lambda i, where, nbr, pat: (0, 0, lax.rem(where[0], 2) * chunks + i, 0)
    )
    packed_shape = (ROW, B + 2 * BAND * HALF, B)
    packed = pl.pallas_call(
        pack_kernel,
        grid_spec=pltpu.PrefetchScalarGridSpec(
            num_scalar_prefetch=3,
            grid=(chunks,),
            in_specs=[pl.BlockSpec(coefficients.shape, lambda i, *_: (0, 0, 0, 0)), half_block, half_block],
            out_specs=pl.BlockSpec(packed_shape, lambda i, *_: (0, 0, 0)),
        ),
        out_shape=struct(packed_shape, F32),
        cost_estimate=cost(10**6, 44 * tile_bytes),
        name="pack",
        compiler_params=pltpu.CompilerParams(vmem_limit_bytes=16 * 2**20),
    )(me, neighbours, pattern, coefficients, margin, step_matrix)
    mine = lax.all_to_all(packed, "x", 0, 0, tiled=True)

    state = struct((ROW * B, B), F32)
    edge = struct((2 * B + 2 * BAND * HALF, B), F32)
    edges = call(edge_kernel, [edge, edge], [me, mine], 10**5, 28, "edges")
    *edges, held = lax.optimization_barrier((*edges, mine))
    other = swap(held)
    from_a, from_b = exchange(*edges)

    _, held = lax.optimization_barrier((edges[0], coefficients))
    old = [coefficients, in_row(held, 1), None, in_row(held, ROW - 1)]
    _, held = lax.optimization_barrier((other, coefficients))
    old[2] = in_row(held, 2)
    from_b, old[1], old[3] = lax.optimization_barrier((from_b, old[1], old[3]))
    y0 = call(
        margin_kernel, state, [me, mine, other, from_a, from_b], ROW * step_flops, 60, "margin",
        scratch=[pltpu.VMEM((ROW, B, BAND * B), F32)] + [pltpu.VMEM((2 * ROW * B, B), BF16)] * 2,
    )
    parts_type = struct((2 * ROW, B, BAND * B), BF16)
    step = list(
        call(
            parts_kernel, [parts_type, parts_type], [me, mine, other, from_a, from_b, swap(from_a), swap(from_b)],
            10**6, 80, "step_parts",
        )
    )
    scratch = [pltpu.VMEM((3 * ROW * B, B), BF16)] * 2 + [pltpu.VMEM((2 * ROW * B, B), BF16)] * 2
    arrived = exchange(y0, y0)
    arrived[0], old[2] = lax.optimization_barrier((arrived[0], old[2]))
    y1, y2 = call(
        functools.partial(two_kernel, 1), [state, state], [me] + step + arrived + [y0], 3 * ROW * step_flops, 64,
        "two", scratch=scratch,
    )
    arrived = exchange(y2, y2)
    old_type = struct((2 * width, 2 * ROW * B), BF16)
    old_high, old_low = call(
        old_kernel, [old_type, old_type], [me] + old + [swap(o) for o in old], 10**6, 64, "old_parts"
    )
    arrived[0], old_high = lax.optimization_barrier((arrived[0], old_high))
    new = call(
        functools.partial(last_kernel, 3), struct((ROW, B, B), F32), [me] + step + arrived + [y2, y0, y1],
        3 * ROW * step_flops, 72, "last", scratch=scratch,
    )
    partial_value = call(
        project_kernel, struct((2 * width, B), F32), [me, old_high, old_low, new],
        2 * 3 * 2 * width * 2 * ROW * B * B, 44, "project",
    )
    sums = lax.all_to_all(partial_value, "row", 0, 0, tiled=True)
    share = 2 * width // domains
    sent = struct((B + 2 * share, B), F32)
    tail = call(
        functools.partial(tail_kernel, 1.0 / (domains * B)), [sent] * ROW, [me, sums, new], 10**5, 12, "tail"
    )
    tail = [tail[0]] + [in_row(tail[j], j) for j in range(1, ROW)]
    return call(
        finish_kernel, (struct((2, 1, B, width), F32), struct((2, share, width), F32)), [me] + tail, 10**5, 8,
        "finish", scratch=[pltpu.VMEM((ROW, B + 2 * share, B), F32)],
    )


def solution(mesh):
    rows = mesh.shape["space"] // ROW
    grouped = Mesh(mesh.devices.reshape(rows, ROW, mesh.shape["orb"]), ("row", "x", "orb"))
    space = ("row", "x")
    return jax.shard_map(
        functools.partial(local, rows),
        mesh=grouped,
        in_specs=(
            P(None, space, None, "orb"),
            P(space, None, None, None),
            P(space, None, None, None),
            P(space, None),
            P(space, None),
        ),
        out_specs=(P(None, space, None, "orb"), P(None, space, "orb")),
        check_vma=False,
    )
```

```python
import functools

import jax
import jax.numpy as jnp
from jax import lax
from jax.experimental import pallas as pl
from jax.experimental.pallas import tpu as pltpu
from jax.sharding import Mesh, PartitionSpec as P

ORDER = 4
ROW = 4
BAND = 5
B = 128
HALF = B // 2
F32 = jnp.float32
BF16 = jnp.bfloat16

SMEM = pl.BlockSpec(memory_space=pltpu.SMEM)
VMEM = pl.BlockSpec(memory_space=pltpu.VMEM)


def cost(flops, moved):
    return pl.CostEstimate(flops=flops, bytes_accessed=moved, transcendentals=0)


def split(value):
    high = value.astype(BF16)
    return high, (value - high.astype(F32)).astype(BF16)


def product(a_high, a_low, b_high, b_low):
    dot = functools.partial(jnp.dot, preferred_element_type=F32)
    return dot(a_high, b_high) + (dot(a_high, b_low) + dot(a_low, b_high))


def turned(value):
    lane = lax.broadcasted_iota(jnp.int32, value.shape, 1)
    rolled = pltpu.roll(value, HALF, axis=1)
    return jnp.where(lane < HALF, rolled, -rolled)


def member(me):
    return lax.rem(lax.div(me[0], 2), ROW), lax.rem(me[0], 2)


def turn_to(q, x):
    return lax.rem(q - x + ROW, ROW)


def parity(me):
    return lax.rem(lax.div(me[0], 2 * ROW), 2)


def pack_kernel(me, nbr, pat, coef_hbm, margin_hbm, step_hbm, out, coef, margin, step, done):
    core = lax.rem(me[0], 2)
    rows = pl.ds(pl.multiple_of(core * HALF, HALF), HALF)
    copies = [
        pltpu.make_async_copy(margin_hbm.at[0, :, rows, :], margin, done.at[0]),
        pltpu.make_async_copy(step_hbm.at[0, :, rows, :], step, done.at[1]),
        pltpu.make_async_copy(coef_hbm, coef, done.at[2]),
    ]
    for copy in copies:
        copy.start()
    first = lax.div(me[0], 2) - 2
    slots = margin.shape[0]
    for i, source in enumerate((margin, step)):
        copies[i].wait()
        for d in range(BAND):
            total = None
            for k in range(slots):
                weight = F32(1.0) if k == 0 else pat[0, k].astype(F32)
                part = source[k] * jnp.where(nbr[0, k] == first + d, weight, F32(0.0))
                total = part if total is None else total + part
            start = B + (i * BAND + d) * HALF
            for q in range(ROW):
                out[q, start : start + HALF, :] = total
    copies[2].wait()
    for q in range(ROW):
        columns = slice(q * HALF, (q + 1) * HALF)
        out[q, :B, :] = jnp.concatenate([coef[0, 0, :, columns], coef[1, 0, :, columns]], axis=1)


def place_half(out, q, place, source, first):
    rows = pl.ds(pl.multiple_of(place * HALF, HALF), HALF)
    for d in range(BAND):
        start = first + d * HALF
        yield q, rows, slice(d * B, (d + 1) * B), source(slice(start, start + HALF))


def edge_kernel(me, mine, to_a, to_b):
    odd = parity(me)
    for out, first in ((to_a, 2 - 2 * odd), (to_b, 2 * odd)):
        for q in range(2):
            out[q * B : (q + 1) * B, :] = mine[first + q, :B, :]


def step_edge_kernel(me, mine, other, out):
    _, core = member(me)
    first = 2 * lax.rem(parity(me) + core + 1, 2)
    for q in range(2):
        for place, ref in ((core, mine), (1 - core, other)):
            for to, rows, columns, tile in place_half(out, q, place, lambda at: ref[first + q, at, :], B + BAND * HALF):
                out[to, rows, columns] = tile


def window(odd, from_a, from_b, own, v_high, v_low):
    reach, size = from_a.shape[0], own.shape[0]
    v_high[reach : reach + size, :], v_low[reach : reach + size, :] = split(own)
    for start, tile in (((1 - odd) * (reach + size), from_a), (odd * (reach + size), from_b)):
        rows = pl.ds(pl.multiple_of(start, B), reach)
        v_high[rows, :], v_low[rows, :] = split(tile)


def margin_kernel(me, mine, other, from_a, from_b, out, full, v_high, v_low):
    _, core = member(me)
    own = [mine[q, :B, :] for q in range(ROW)]
    window(parity(me), from_a[...], from_b[...], jnp.concatenate(own, axis=0), v_high, v_low)
    for q in range(ROW):
        for place, ref in ((core, mine), (1 - core, other)):
            for _, rows, columns, tile in place_half(full, q, place, lambda at: ref[q, at, :], B):
                full[q, rows, columns] = tile
    for q in range(ROW):
        m_high, m_low = split(full[q])
        rows = slice(q * B, (q + BAND) * B)
        out[q * B : (q + 1) * B, :] = own[q] + product(m_high, m_low, v_high[rows], v_low[rows])


def parts_kernel(me, mine, other, edge, edge_other, out_high, out_low):
    _, core = member(me)
    odd = parity(me)
    for q in range(ROW):
        for place, ref in ((core, mine), (1 - core, other)):
            for to, rows, columns, tile in place_half(out_high, q + 2, place, lambda at: ref[q, at, :], B + BAND * HALF):
                out_high[to, rows, columns], out_low[to, rows, columns] = split(tile)
    ahead = lax.rem(odd + core + 1, 2)
    for start, ref in ((ahead * 6, edge), ((1 - ahead) * 6, edge_other)):
        for q in range(2):
            out_high[start + q], out_low[start + q] = split(ref[q])


def two_steps(n, me, m_high, m_low, from_a, from_b, own, v_high, v_low, w_high, w_low):
    window(parity(me), from_a[...], from_b[...], own[...], v_high, v_low)
    firsts = []
    for q in range(2 * ROW):
        rows = slice(q * B, (q + BAND) * B)
        value = product(m_high[q], m_low[q], v_high[rows], v_low[rows]) * F32(1.0 / n)
        w_high[q * B : (q + 1) * B, :], w_low[q * B : (q + 1) * B, :] = split(value)
        firsts.append(value)
    for q in range(ROW):
        rows = slice(q * B, (q + BAND) * B)
        second = product(m_high[q + 2], m_low[q + 2], w_high[rows], w_low[rows]) * F32(1.0 / (n + 1))
        yield q, firsts[q + 2], second


def two_kernel(n, me, m_high, m_low, from_a, from_b, own, first, second, *scratch):
    for q, a, b in two_steps(n, me, m_high, m_low, from_a, from_b, own, *scratch):
        first[q * B : (q + 1) * B, :] = a
        second[q * B : (q + 1) * B, :] = b


def last_kernel(n, me, m_high, m_low, from_a, from_b, own, y0, y1, out, *scratch):
    x, _ = member(me)
    for q, y3, y4 in two_steps(n, me, m_high, m_low, from_a, from_b, own, *scratch):
        rows = slice(q * B, (q + 1) * B)
        out[turn_to(q, x)] = (y0[rows, :] - own[rows, :]) + y4 + turned(y1[rows, :] - y3)


def old_kernel(me, c0, c1, c2, c3, o0, o1, o2, o3, out_high, out_low):
    x, core = member(me)
    width = c0.shape[3]
    for j, (ref, other) in enumerate(((c0, o0), (c1, o1), (c2, o2), (c3, o3))):
        q = turn_to(x, j)
        for part in range(2):
            for place, tile in ((core, ref[part, 0]), (1 - core, other[part, 0])):
                rows = pl.ds(pl.multiple_of(place * width, width), width)
                columns = pl.ds(pl.multiple_of((part * ROW + q) * B, B), B)
                out_high[rows, columns], out_low[rows, columns] = split(jnp.transpose(tile))


def project_kernel(me, old_high, old_low, new, out):
    x, _ = member(me)
    tiles = [new[turn_to(q, x)] for q in range(ROW)]
    v_high, v_low = split(jnp.concatenate(tiles + [turned(t) for t in tiles], axis=0))
    out[...] = product(old_high[...], old_low[...], v_high, v_low)


def tail_kernel(scale, me, sums, new, *outs):
    x, _ = member(me)
    share = 4
    total = jnp.sum(sums[...].reshape(-1, ROW * share, B), axis=0) * scale
    for j, out in enumerate(outs):
        out[:B, :] = new[j]
        for q in range(ROW):

            @pl.when(q == lax.rem(x + j, ROW))
            def _():
                out[B : B + share, :] = total[q * share : (q + 1) * share, :]


def finish_kernel(me, mine, b1, b2, b3, propagated, owned, held):
    x, _ = member(me)
    share = owned.shape[1]
    for j, ref in enumerate((mine, b1, b2, b3)):
        held[turn_to(x, j)] = ref[...]
    for q in range(ROW):
        columns = slice(q * HALF, (q + 1) * HALF)
        for part in range(2):
            lanes = slice(part * HALF, (part + 1) * HALF)
            propagated[part, 0, :, columns] = held[q, :B, lanes]
            owned[part, :, columns] = held[q, B : B + share, lanes]


def local(rows, coefficients, margin, step_matrix, neighbours, pattern):
    width = coefficients.shape[3]
    domains = rows * ROW
    me = lax.axis_index(("row", "x", "orb")).astype(jnp.int32).reshape(1)
    struct = jax.ShapeDtypeStruct
    tile_bytes = 4 * B * B
    step_flops = 2 * 3 * B * BAND * B * B

    def call(kernel, out_shape, args, flops, moved, name, scratch=(), scalars=1):
        return pl.pallas_call(
            kernel,
            out_shape=out_shape,
            in_specs=[SMEM] * scalars + [VMEM] * (len(args) - scalars),
            out_specs=jax.tree.map(lambda _: VMEM, out_shape),
            scratch_shapes=list(scratch),
            cost_estimate=cost(flops, moved * tile_bytes),
            name=name,
            compiler_params=pltpu.CompilerParams(vmem_limit_bytes=32 * 2**20),
        )(*args)

    def in_row(value, by):
        return lax.ppermute(value, "x", [(x, (x + by) % ROW) for x in range(ROW)])

    def swap(value):
        return lax.ppermute(value, "orb", [(0, 1), (1, 0)])

    def exchange(to_a, to_b):
        def swap_rows(value, first):
            pairs = [(r, r + 1) for r in range(first, rows - 1, 2)]
            return lax.ppermute(value, "row", pairs + [(j, i) for i, j in pairs])

        return [swap_rows(to_a, 0), swap_rows(to_b, 1)]

    def apart(value):
        pairs = []
        for core in range(2):
            for r in range(core, rows - 1, 2):
                for x in range(ROW):
                    ends = [((r + i) * ROW + x) * 2 + core for i in range(2)]
                    pairs += [tuple(ends), tuple(ends[::-1])]
        return lax.ppermute(value, ("row", "x", "orb"), pairs)

    slots = neighbours.shape[1]
    hbm = pl.BlockSpec(memory_space=pltpu.HBM)
    half_blocks = pltpu.VMEM((slots, HALF, B), F32)
    packed = pl.pallas_call(
        pack_kernel,
        in_specs=[SMEM] * 3 + [hbm] * 3,
        out_specs=VMEM,
        out_shape=struct((ROW, B + 2 * BAND * HALF, B), F32),
        scratch_shapes=[
            pltpu.VMEM(coefficients.shape, F32), half_blocks, half_blocks, pltpu.SemaphoreType.DMA((3,))
        ],
        cost_estimate=cost(10**6, 44 * tile_bytes),
        name="pack",
        compiler_params=pltpu.CompilerParams(vmem_limit_bytes=60 * 2**20),
    )(me, neighbours, pattern, coefficients, margin, step_matrix)
    mine = lax.all_to_all(packed, "x", 0, 0, tiled=True)

    state = struct((ROW * B, B), F32)
    edge = struct((2 * B, B), F32)
    edges = call(edge_kernel, [edge, edge], [me, mine], 10**5, 28, "edges")
    *edges, held = lax.optimization_barrier((*edges, mine))
    other = swap(held)
    from_a, from_b = exchange(*edges)
    step_edge = call(step_edge_kernel, struct((2, B, BAND * B), F32), [me, mine, other], 10**5, 20, "step_edges")
    step_edge = apart(step_edge)

    _, held = lax.optimization_barrier((other, coefficients))
    old = [coefficients, in_row(held, 1), in_row(held, 2), None]
    y0 = call(
        margin_kernel, state, [me, mine, other, from_a, from_b], 10**10, 60, "margin",
        scratch=[pltpu.VMEM((ROW, B, BAND * B), F32)] + [pltpu.VMEM((2 * ROW * B, B), BF16)] * 2,
    )
    arrived = exchange(y0, y0)
    _, held = lax.optimization_barrier((old[2], coefficients))
    old[3] = in_row(held, 3)
    *arrived, step_edge, old[1], old[2], old[3] = lax.optimization_barrier((*arrived, step_edge, *old[1:]))
    parts_type = struct((2 * ROW, B, BAND * B), BF16)
    step = list(
        call(
            parts_kernel, [parts_type, parts_type], [me, mine, other, step_edge, swap(step_edge)],
            10**6, 80, "step_parts",
        )
    )
    scratch = [pltpu.VMEM((3 * ROW * B, B), BF16)] * 2 + [pltpu.VMEM((2 * ROW * B, B), BF16)] * 2
    y1, y2 = call(
        functools.partial(two_kernel, 1), [state, state], [me] + step + arrived + [y0], 3 * ROW * step_flops, 64,
        "two", scratch=scratch,
    )
    arrived = exchange(y2, y2)
    old_type = struct((2 * width, 2 * ROW * B), BF16)
    old_high, old_low = call(
        old_kernel, [old_type, old_type], [me] + old + [swap(o) for o in old], 10**6, 64, "old_parts"
    )
    arrived[0], old_high = lax.optimization_barrier((arrived[0], old_high))
    new = call(
        functools.partial(last_kernel, 3), struct((ROW, B, B), F32), [me] + step + arrived + [y2, y0, y1],
        3 * ROW * step_flops, 72, "last", scratch=scratch,
    )
    partial_value = call(
        project_kernel, struct((2 * width, B), F32), [me, old_high, old_low, new],
        2 * 3 * 2 * width * 2 * ROW * B * B, 44, "project",
    )
    sums = lax.all_to_all(partial_value, "row", 0, 0, tiled=True)
    share = 2 * width // domains
    sent = struct((B + 2 * share, B), F32)
    tail = call(
        functools.partial(tail_kernel, 1.0 / (domains * B)), [sent] * ROW, [me, sums, new], 10**5, 12, "tail"
    )
    tail = [tail[0]] + [in_row(tail[j], j) for j in range(1, ROW)]
    return call(
        finish_kernel, (struct((2, 1, B, width), F32), struct((2, share, width), F32)), [me] + tail, 10**5, 8,
        "finish", scratch=[pltpu.VMEM((ROW, B + 2 * share, B), F32)],
    )


def solution(mesh):
    rows = mesh.shape["space"] // ROW
    grouped = Mesh(mesh.devices.reshape(rows, ROW, mesh.shape["orb"]), ("row", "x", "orb"))
    space = ("row", "x")
    return jax.shard_map(
        functools.partial(local, rows),
        mesh=grouped,
        in_specs=(
            P(None, space, None, "orb"),
            P(space, None, None, None),
            P(space, None, None, None),
            P(space, None),
            P(space, None),
        ),
        out_specs=(P(None, space, None, "orb"), P(None, space, "orb")),
        check_vma=False,
    )
```

```python
import functools

import jax
import jax.numpy as jnp
from jax import lax
from jax.experimental import pallas as pl
from jax.experimental.pallas import tpu as pltpu
from jax.sharding import Mesh, PartitionSpec as P

ORDER = 4
ROW = 4
BAND = 5
B = 128
HALF = B // 2
F32 = jnp.float32
BF16 = jnp.bfloat16

SMEM = pl.BlockSpec(memory_space=pltpu.SMEM)
VMEM = pl.BlockSpec(memory_space=pltpu.VMEM)


def cost(flops, moved):
    return pl.CostEstimate(flops=flops, bytes_accessed=moved, transcendentals=0)


def split(value):
    high = value.astype(BF16)
    return high, (value - high.astype(F32)).astype(BF16)


def product(a_high, a_low, b):
    dot = functools.partial(jnp.dot, preferred_element_type=F32)
    both = dot(a_high, b)
    return both[:, :B] + (both[:, B:] + dot(a_low, b[:, :B]))


def put_parts(out, rows, value):
    out[rows, :B], out[rows, B:] = split(value)


def turned(value):
    lane = lax.broadcasted_iota(jnp.int32, value.shape, 1)
    rolled = pltpu.roll(value, HALF, axis=1)
    return jnp.where(lane < HALF, rolled, -rolled)


def member(me):
    return lax.rem(lax.div(me[0], 2), ROW), lax.rem(me[0], 2)


def turn_to(q, x):
    return lax.rem(q - x + ROW, ROW)


def parity(me):
    return lax.rem(lax.div(me[0], 2 * ROW), 2)


def pack_kernel(me, nbr, pat, coef_hbm, margin_hbm, step_hbm, out, coef, margin, step, done):
    core = lax.rem(me[0], 2)
    rows = pl.ds(pl.multiple_of(core * HALF, HALF), HALF)
    copies = [
        pltpu.make_async_copy(margin_hbm.at[0, :, rows, :], margin, done.at[0]),
        pltpu.make_async_copy(step_hbm.at[0, :, rows, :], step, done.at[1]),
        pltpu.make_async_copy(coef_hbm, coef, done.at[2]),
    ]
    for copy in copies:
        copy.start()
    first = lax.div(me[0], 2) - 2
    slots = margin.shape[0]
    for i, source in enumerate((margin, step)):
        copies[i].wait()
        for d in range(BAND):
            total = None
            for k in range(slots):
                weight = F32(1.0) if k == 0 else pat[0, k].astype(F32)
                part = source[k] * jnp.where(nbr[0, k] == first + d, weight, F32(0.0))
                total = part if total is None else total + part
            start = B + (i * BAND + d) * HALF
            for q in range(ROW):
                out[q, start : start + HALF, :] = total
    copies[2].wait()
    for q in range(ROW):
        columns = slice(q * HALF, (q + 1) * HALF)
        out[q, :B, :] = jnp.concatenate([coef[0, 0, :, columns], coef[1, 0, :, columns]], axis=1)


def place_half(out, q, place, source, first):
    rows = pl.ds(pl.multiple_of(place * HALF, HALF), HALF)
    for d in range(BAND):
        start = first + d * HALF
        yield q, rows, slice(d * B, (d + 1) * B), source(slice(start, start + HALF))


def edge_kernel(me, mine, to_a, to_b):
    odd = parity(me)
    for out, first in ((to_a, 2 - 2 * odd), (to_b, 2 * odd)):
        for q in range(2):
            out[q * B : (q + 1) * B, :] = mine[first + q, :B, :]


def step_edge_kernel(me, mine, other, out):
    _, core = member(me)
    first = 2 * lax.rem(parity(me) + core + 1, 2)
    for q in range(2):
        for place, ref in ((core, mine), (1 - core, other)):
            for to, rows, columns, tile in place_half(out, q, place, lambda at: ref[first + q, at, :], B + BAND * HALF):
                out[to, rows, columns] = tile


def window(odd, from_a, from_b, own, v):
    reach, size = from_a.shape[0], own.shape[0]
    put_parts(v, slice(reach, reach + size), own)
    for start, tile in (((1 - odd) * (reach + size), from_a), (odd * (reach + size), from_b)):
        put_parts(v, pl.ds(pl.multiple_of(start, B), reach), tile)


def margin_kernel(me, mine, other, from_a, from_b, out, full, v):
    _, core = member(me)
    own = [mine[q, :B, :] for q in range(ROW)]
    window(parity(me), from_a[...], from_b[...], jnp.concatenate(own, axis=0), v)
    for q in range(ROW):
        for place, ref in ((core, mine), (1 - core, other)):
            for _, rows, columns, tile in place_half(full, q, place, lambda at: ref[q, at, :], B):
                full[q, rows, columns] = tile
    for q in range(ROW):
        m_high, m_low = split(full[q])
        rows = slice(q * B, (q + BAND) * B)
        out[q * B : (q + 1) * B, :] = own[q] + product(m_high, m_low, v[rows, :])


def parts_kernel(me, mine, other, edge, edge_other, out_high, out_low):
    _, core = member(me)
    odd = parity(me)
    for q in range(ROW):
        for place, ref in ((core, mine), (1 - core, other)):
            for to, rows, columns, tile in place_half(out_high, q + 2, place, lambda at: ref[q, at, :], B + BAND * HALF):
                out_high[to, rows, columns], out_low[to, rows, columns] = split(tile)
    ahead = lax.rem(odd + core + 1, 2)
    for start, ref in ((ahead * 6, edge), ((1 - ahead) * 6, edge_other)):
        for q in range(2):
            out_high[start + q], out_low[start + q] = split(ref[q])


def two_steps(n, me, m_high, m_low, from_a, from_b, own, v, w):
    window(parity(me), from_a[...], from_b[...], own[...], v)
    firsts = []
    for q in range(2 * ROW):
        rows = slice(q * B, (q + BAND) * B)
        value = product(m_high[q], m_low[q], v[rows, :]) * F32(1.0 / n)
        put_parts(w, slice(q * B, (q + 1) * B), value)
        firsts.append(value)
    for q in range(ROW):
        rows = slice(q * B, (q + BAND) * B)
        second = product(m_high[q + 2], m_low[q + 2], w[rows, :]) * F32(1.0 / (n + 1))
        yield q, firsts[q + 2], second


def two_kernel(n, me, m_high, m_low, from_a, from_b, own, first, second, *scratch):
    for q, a, b in two_steps(n, me, m_high, m_low, from_a, from_b, own, *scratch):
        first[q * B : (q + 1) * B, :] = a
        second[q * B : (q + 1) * B, :] = b


def last_kernel(n, me, m_high, m_low, from_a, from_b, own, y0, y1, out, *scratch):
    x, _ = member(me)
    for q, y3, y4 in two_steps(n, me, m_high, m_low, from_a, from_b, own, *scratch):
        rows = slice(q * B, (q + 1) * B)
        out[turn_to(q, x)] = (y0[rows, :] - own[rows, :]) + y4 + turned(y1[rows, :] - y3)


def old_kernel(me, c0, c1, c2, c3, o0, o1, o2, o3, out_high, out_low):
    x, core = member(me)
    width = c0.shape[3]
    for j, (ref, other) in enumerate(((c0, o0), (c1, o1), (c2, o2), (c3, o3))):
        q = turn_to(x, j)
        for part in range(2):
            for place, tile in ((core, ref[part, 0]), (1 - core, other[part, 0])):
                rows = pl.ds(pl.multiple_of(place * width, width), width)
                columns = pl.ds(pl.multiple_of((part * ROW + q) * B, B), B)
                out_high[rows, columns], out_low[rows, columns] = split(jnp.transpose(tile))


def project_kernel(me, old_high, old_low, new, out):
    x, _ = member(me)
    tiles = [new[turn_to(q, x)] for q in range(ROW)]
    parts = split(jnp.concatenate(tiles + [turned(t) for t in tiles], axis=0))
    out[...] = product(old_high[...], old_low[...], jnp.concatenate(parts, axis=1))


def tail_kernel(scale, me, sums, new, *outs):
    x, _ = member(me)
    share = 4
    total = jnp.sum(sums[...].reshape(-1, ROW * share, B), axis=0) * scale
    for j, out in enumerate(outs):
        out[:B, :] = new[j]
        for q in range(ROW):

            @pl.when(q == lax.rem(x + j, ROW))
            def _():
                out[B : B + share, :] = total[q * share : (q + 1) * share, :]


def finish_kernel(me, mine, b1, b2, b3, propagated, owned, held):
    x, _ = member(me)
    share = owned.shape[1]
    for j, ref in enumerate((mine, b1, b2, b3)):
        held[turn_to(x, j)] = ref[...]
    for q in range(ROW):
        columns = slice(q * HALF, (q + 1) * HALF)
        for part in range(2):
            lanes = slice(part * HALF, (part + 1) * HALF)
            propagated[part, 0, :, columns] = held[q, :B, lanes]
            owned[part, :, columns] = held[q, B : B + share, lanes]


def local(rows, coefficients, margin, step_matrix, neighbours, pattern):
    width = coefficients.shape[3]
    domains = rows * ROW
    me = lax.axis_index(("row", "x", "orb")).astype(jnp.int32).reshape(1)
    struct = jax.ShapeDtypeStruct
    tile_bytes = 4 * B * B
    step_flops = 2 * 3 * B * BAND * B * B

    def call(kernel, out_shape, args, flops, moved, name, scratch=(), scalars=1):
        return pl.pallas_call(
            kernel,
            out_shape=out_shape,
            in_specs=[SMEM] * scalars + [VMEM] * (len(args) - scalars),
            out_specs=jax.tree.map(lambda _: VMEM, out_shape),
            scratch_shapes=list(scratch),
            cost_estimate=cost(flops, moved * tile_bytes),
            name=name,
            compiler_params=pltpu.CompilerParams(vmem_limit_bytes=32 * 2**20),
        )(*args)

    def in_row(value, by):
        return lax.ppermute(value, "x", [(x, (x + by) % ROW) for x in range(ROW)])

    def swap(value):
        return lax.ppermute(value, "orb", [(0, 1), (1, 0)])

    def exchange(to_a, to_b):
        def swap_rows(value, first):
            pairs = [(r, r + 1) for r in range(first, rows - 1, 2)]
            return lax.ppermute(value, "row", pairs + [(j, i) for i, j in pairs])

        return [swap_rows(to_a, 0), swap_rows(to_b, 1)]

    def apart(value):
        pairs = []
        for core in range(2):
            for r in range(core, rows - 1, 2):
                for x in range(ROW):
                    ends = [((r + i) * ROW + x) * 2 + core for i in range(2)]
                    pairs += [tuple(ends), tuple(ends[::-1])]
        return lax.ppermute(value, ("row", "x", "orb"), pairs)

    slots = neighbours.shape[1]
    hbm = pl.BlockSpec(memory_space=pltpu.HBM)
    half_blocks = pltpu.VMEM((slots, HALF, B), F32)
    packed = pl.pallas_call(
        pack_kernel,
        in_specs=[SMEM] * 3 + [hbm] * 3,
        out_specs=VMEM,
        out_shape=struct((ROW, B + 2 * BAND * HALF, B), F32),
        scratch_shapes=[
            pltpu.VMEM(coefficients.shape, F32), half_blocks, half_blocks, pltpu.SemaphoreType.DMA((3,))
        ],
        cost_estimate=cost(10**6, 44 * tile_bytes),
        name="pack",
        compiler_params=pltpu.CompilerParams(vmem_limit_bytes=60 * 2**20),
    )(me, neighbours, pattern, coefficients, margin, step_matrix)
    mine = lax.all_to_all(packed, "x", 0, 0, tiled=True)

    state = struct((ROW * B, B), F32)
    edge = struct((2 * B, B), F32)
    edges = call(edge_kernel, [edge, edge], [me, mine], 10**5, 28, "edges")
    *edges, held = lax.optimization_barrier((*edges, mine))
    other = swap(held)
    from_a, from_b = exchange(*edges)
    step_edge = call(step_edge_kernel, struct((2, B, BAND * B), F32), [me, mine, other], 10**5, 20, "step_edges")
    step_edge = apart(step_edge)

    _, held = lax.optimization_barrier((other, coefficients))
    old = [coefficients, in_row(held, 1), in_row(held, 2), None]
    y0 = call(
        margin_kernel, state, [me, mine, other, from_a, from_b], 10**10, 60, "margin",
        scratch=[pltpu.VMEM((ROW, B, BAND * B), F32)] + [pltpu.VMEM((2 * ROW * B, 2 * B), BF16)],
    )
    arrived = exchange(y0, y0)
    _, held = lax.optimization_barrier((old[2], coefficients))
    old[3] = in_row(held, 3)
    *arrived, step_edge, old[1], old[2], old[3] = lax.optimization_barrier((*arrived, step_edge, *old[1:]))
    parts_type = struct((2 * ROW, B, BAND * B), BF16)
    step = list(
        call(
            parts_kernel, [parts_type, parts_type], [me, mine, other, step_edge, swap(step_edge)],
            10**6, 80, "step_parts",
        )
    )
    scratch = [pltpu.VMEM((3 * ROW * B, 2 * B), BF16), pltpu.VMEM((2 * ROW * B, 2 * B), BF16)]
    y1, y2 = call(
        functools.partial(two_kernel, 1), [state, state], [me] + step + arrived + [y0], 3 * ROW * step_flops, 64,
        "two", scratch=scratch,
    )
    arrived = exchange(y2, y2)
    old_type = struct((2 * width, 2 * ROW * B), BF16)
    old_high, old_low = call(
        old_kernel, [old_type, old_type], [me] + old + [swap(o) for o in old], 10**6, 64, "old_parts"
    )
    arrived[0], old_high = lax.optimization_barrier((arrived[0], old_high))
    new = call(
        functools.partial(last_kernel, 3), struct((ROW, B, B), F32), [me] + step + arrived + [y2, y0, y1],
        3 * ROW * step_flops, 72, "last", scratch=scratch,
    )
    partial_value = call(
        project_kernel, struct((2 * width, B), F32), [me, old_high, old_low, new],
        2 * 3 * 2 * width * 2 * ROW * B * B, 44, "project",
    )
    sums = lax.all_to_all(partial_value, "row", 0, 0, tiled=True)
    share = 2 * width // domains
    sent = struct((B + 2 * share, B), F32)
    tail = call(
        functools.partial(tail_kernel, 1.0 / (domains * B)), [sent] * ROW, [me, sums, new], 10**5, 12, "tail"
    )
    tail = [tail[0]] + [in_row(tail[j], j) for j in range(1, ROW)]
    return call(
        finish_kernel, (struct((2, 1, B, width), F32), struct((2, share, width), F32)), [me] + tail, 10**5, 8,
        "finish", scratch=[pltpu.VMEM((ROW, B + 2 * share, B), F32)],
    )


def solution(mesh):
    rows = mesh.shape["space"] // ROW
    grouped = Mesh(mesh.devices.reshape(rows, ROW, mesh.shape["orb"]), ("row", "x", "orb"))
    space = ("row", "x")
    return jax.shard_map(
        functools.partial(local, rows),
        mesh=grouped,
        in_specs=(
            P(None, space, None, "orb"),
            P(space, None, None, None),
            P(space, None, None, None),
            P(space, None),
            P(space, None),
        ),
        out_specs=(P(None, space, None, "orb"), P(None, space, "orb")),
        check_vma=False,
    )
```

```python
import functools

import jax
import jax.numpy as jnp
from jax import lax
from jax.experimental import pallas as pl
from jax.experimental.pallas import tpu as pltpu
from jax.sharding import Mesh, PartitionSpec as P

ORDER = 4
ROW = 4
BAND = 5
B = 128
HALF = B // 2
F32 = jnp.float32
BF16 = jnp.bfloat16

SMEM = pl.BlockSpec(memory_space=pltpu.SMEM)
VMEM = pl.BlockSpec(memory_space=pltpu.VMEM)


def cost(flops, moved):
    return pl.CostEstimate(flops=flops, bytes_accessed=moved, transcendentals=0)


def split(value):
    high = value.astype(BF16)
    return high, (value - high.astype(F32)).astype(BF16)


def product(a_high, a_low, b):
    dot = functools.partial(jnp.dot, preferred_element_type=F32)
    both = dot(a_high, b)
    return both[:, :B] + (both[:, B:] + dot(a_low, b[:, :B]))


def put_parts(out, rows, value):
    out[rows, :B], out[rows, B:] = split(value)


def turned(value):
    lane = lax.broadcasted_iota(jnp.int32, value.shape, 1)
    rolled = pltpu.roll(value, HALF, axis=1)
    return jnp.where(lane < HALF, rolled, -rolled)


def member(me):
    return lax.rem(lax.div(me[0], 2), ROW), lax.rem(me[0], 2)


def turn_to(q, x):
    return lax.rem(q - x + ROW, ROW)


def parity(me):
    return lax.rem(lax.div(me[0], 2 * ROW), 2)


def pack_kernel(me, nbr_hbm, pat_hbm, coef_hbm, margin_hbm, step_hbm, out, nbr, pat, coef, margin, step, done):
    core = lax.rem(me[0], 2)
    rows = pl.ds(pl.multiple_of(core * HALF, HALF), HALF)
    copies = [
        pltpu.make_async_copy(margin_hbm.at[0, :, rows, :], margin, done.at[0]),
        pltpu.make_async_copy(step_hbm.at[0, :, rows, :], step, done.at[1]),
        pltpu.make_async_copy(coef_hbm, coef, done.at[2]),
        pltpu.make_async_copy(nbr_hbm, nbr, done.at[3]),
        pltpu.make_async_copy(pat_hbm, pat, done.at[4]),
    ]
    for copy in copies[::-1]:
        copy.start()
    copies[3].wait()
    copies[4].wait()
    first = lax.div(me[0], 2) - 2
    slots = margin.shape[0]
    for i, source in enumerate((margin, step)):
        copies[i].wait()
        for d in range(BAND):
            total = None
            for k in range(slots):
                weight = F32(1.0) if k == 0 else pat[0, k].astype(F32)
                part = source[k] * jnp.where(nbr[0, k] == first + d, weight, F32(0.0))
                total = part if total is None else total + part
            start = B + (i * BAND + d) * HALF
            for q in range(ROW):
                out[q, start : start + HALF, :] = total
    copies[2].wait()
    for q in range(ROW):
        columns = slice(q * HALF, (q + 1) * HALF)
        out[q, :B, :] = jnp.concatenate([coef[0, 0, :, columns], coef[1, 0, :, columns]], axis=1)


def place_half(out, q, place, source, first):
    rows = pl.ds(pl.multiple_of(place * HALF, HALF), HALF)
    for d in range(BAND):
        start = first + d * HALF
        yield q, rows, slice(d * B, (d + 1) * B), source(slice(start, start + HALF))


def edge_kernel(me, mine, to_a, to_b):
    odd = parity(me)
    for out, first in ((to_a, 2 - 2 * odd), (to_b, 2 * odd)):
        for q in range(2):
            out[q * B : (q + 1) * B, :] = mine[first + q, :B, :]


def step_edge_kernel(me, mine, other, out):
    _, core = member(me)
    first = 2 * lax.rem(parity(me) + core + 1, 2)
    for q in range(2):
        for place, ref in ((core, mine), (1 - core, other)):
            for to, rows, columns, tile in place_half(out, q, place, lambda at: ref[first + q, at, :], B + BAND * HALF):
                out[to, rows, columns] = tile


def window(odd, from_a, from_b, own, v):
    reach, size = from_a.shape[0], own.shape[0]
    put_parts(v, slice(reach, reach + size), own)
    for start, tile in (((1 - odd) * (reach + size), from_a), (odd * (reach + size), from_b)):
        put_parts(v, pl.ds(pl.multiple_of(start, B), reach), tile)


def margin_kernel(me, mine, other, from_a, from_b, out, full, v):
    _, core = member(me)
    own = [mine[q, :B, :] for q in range(ROW)]
    window(parity(me), from_a[...], from_b[...], jnp.concatenate(own, axis=0), v)
    for q in range(ROW):
        for place, ref in ((core, mine), (1 - core, other)):
            for _, rows, columns, tile in place_half(full, q, place, lambda at: ref[q, at, :], B):
                full[q, rows, columns] = tile
    for q in range(ROW):
        m_high, m_low = split(full[q])
        rows = slice(q * B, (q + BAND) * B)
        out[q * B : (q + 1) * B, :] = own[q] + product(m_high, m_low, v[rows, :])


def parts_kernel(me, mine, other, edge, edge_other, out_high, out_low):
    _, core = member(me)
    odd = parity(me)
    for q in range(ROW):
        for place, ref in ((core, mine), (1 - core, other)):
            for to, rows, columns, tile in place_half(out_high, q + 2, place, lambda at: ref[q, at, :], B + BAND * HALF):
                out_high[to, rows, columns], out_low[to, rows, columns] = split(tile)
    ahead = lax.rem(odd + core + 1, 2)
    for start, ref in ((ahead * 6, edge), ((1 - ahead) * 6, edge_other)):
        for q in range(2):
            out_high[start + q], out_low[start + q] = split(ref[q])


def two_steps(n, me, m_high, m_low, from_a, from_b, own, v, w):
    window(parity(me), from_a[...], from_b[...], own[...], v)
    firsts = []
    for q in range(2 * ROW):
        rows = slice(q * B, (q + BAND) * B)
        value = product(m_high[q], m_low[q], v[rows, :]) * F32(1.0 / n)
        put_parts(w, slice(q * B, (q + 1) * B), value)
        firsts.append(value)
    for q in range(ROW):
        rows = slice(q * B, (q + BAND) * B)
        second = product(m_high[q + 2], m_low[q + 2], w[rows, :]) * F32(1.0 / (n + 1))
        yield q, firsts[q + 2], second


def two_kernel(n, me, m_high, m_low, from_a, from_b, own, first, second, *scratch):
    for q, a, b in two_steps(n, me, m_high, m_low, from_a, from_b, own, *scratch):
        first[q * B : (q + 1) * B, :] = a
        second[q * B : (q + 1) * B, :] = b


def last_kernel(n, me, m_high, m_low, from_a, from_b, own, y0, y1, out, *scratch):
    x, _ = member(me)
    for q, y3, y4 in two_steps(n, me, m_high, m_low, from_a, from_b, own, *scratch):
        rows = slice(q * B, (q + 1) * B)
        out[turn_to(q, x)] = (y0[rows, :] - own[rows, :]) + y4 + turned(y1[rows, :] - y3)


def old_kernel(me, c0, c1, c2, c3, o0, o1, o2, o3, out_high, out_low):
    x, core = member(me)
    width = c0.shape[3]
    for j, (ref, other) in enumerate(((c0, o0), (c1, o1), (c2, o2), (c3, o3))):
        q = turn_to(x, j)
        for part in range(2):
            for place, tile in ((core, ref[part, 0]), (1 - core, other[part, 0])):
                rows = pl.ds(pl.multiple_of(place * width, width), width)
                columns = pl.ds(pl.multiple_of((part * ROW + q) * B, B), B)
                out_high[rows, columns], out_low[rows, columns] = split(jnp.transpose(tile))


def project_kernel(me, old_high, old_low, new, out):
    x, _ = member(me)
    tiles = [new[turn_to(q, x)] for q in range(ROW)]
    parts = split(jnp.concatenate(tiles + [turned(t) for t in tiles], axis=0))
    out[...] = product(old_high[...], old_low[...], jnp.concatenate(parts, axis=1))


def tail_kernel(scale, me, sums, new, *outs):
    x, _ = member(me)
    share = 4
    total = jnp.sum(sums[...].reshape(-1, ROW * share, B), axis=0) * scale
    for j, out in enumerate(outs):
        out[:B, :] = new[j]
        for q in range(ROW):

            @pl.when(q == lax.rem(x + j, ROW))
            def _():
                out[B : B + share, :] = total[q * share : (q + 1) * share, :]


def finish_kernel(me, mine, b1, b2, b3, propagated, owned, held):
    x, _ = member(me)
    share = owned.shape[1]
    for j, ref in enumerate((mine, b1, b2, b3)):
        held[turn_to(x, j)] = ref[...]
    for q in range(ROW):
        columns = slice(q * HALF, (q + 1) * HALF)
        for part in range(2):
            lanes = slice(part * HALF, (part + 1) * HALF)
            propagated[part, 0, :, columns] = held[q, :B, lanes]
            owned[part, :, columns] = held[q, B : B + share, lanes]


def local(rows, coefficients, margin, step_matrix, neighbours, pattern):
    width = coefficients.shape[3]
    domains = rows * ROW
    me = lax.axis_index(("row", "x", "orb")).astype(jnp.int32).reshape(1)
    struct = jax.ShapeDtypeStruct
    tile_bytes = 4 * B * B
    step_flops = 2 * 3 * B * BAND * B * B

    def call(kernel, out_shape, args, flops, moved, name, scratch=(), scalars=1):
        return pl.pallas_call(
            kernel,
            out_shape=out_shape,
            in_specs=[SMEM] * scalars + [VMEM] * (len(args) - scalars),
            out_specs=jax.tree.map(lambda _: VMEM, out_shape),
            scratch_shapes=list(scratch),
            cost_estimate=cost(flops, moved * tile_bytes),
            name=name,
            compiler_params=pltpu.CompilerParams(vmem_limit_bytes=32 * 2**20),
        )(*args)

    def in_row(value, by):
        return lax.ppermute(value, "x", [(x, (x + by) % ROW) for x in range(ROW)])

    def swap(value):
        return lax.ppermute(value, "orb", [(0, 1), (1, 0)])

    def exchange(to_a, to_b):
        def swap_rows(value, first):
            pairs = [(r, r + 1) for r in range(first, rows - 1, 2)]
            return lax.ppermute(value, "row", pairs + [(j, i) for i, j in pairs])

        return [swap_rows(to_a, 0), swap_rows(to_b, 1)]

    def apart(value):
        pairs = []
        for core in range(2):
            for r in range(core, rows - 1, 2):
                for x in range(ROW):
                    ends = [((r + i) * ROW + x) * 2 + core for i in range(2)]
                    pairs += [tuple(ends), tuple(ends[::-1])]
        return lax.ppermute(value, ("row", "x", "orb"), pairs)

    slots = neighbours.shape[1]
    hbm = pl.BlockSpec(memory_space=pltpu.HBM)
    half_blocks = pltpu.VMEM((slots, HALF, B), F32)
    packed = pl.pallas_call(
        pack_kernel,
        in_specs=[SMEM] + [hbm] * 5,
        out_specs=VMEM,
        out_shape=struct((ROW, B + 2 * BAND * HALF, B), F32),
        scratch_shapes=[
            pltpu.SMEM(neighbours.shape, jnp.int32), pltpu.SMEM(pattern.shape, jnp.int32),
            pltpu.VMEM(coefficients.shape, F32), half_blocks, half_blocks, pltpu.SemaphoreType.DMA((5,)),
        ],
        cost_estimate=cost(10**6, 44 * tile_bytes),
        name="pack",
        compiler_params=pltpu.CompilerParams(vmem_limit_bytes=28 * 2**20),
    )(me, *(pltpu.with_memory_space_constraint(a, pltpu.HBM) for a in (neighbours, pattern, coefficients, margin, step_matrix)))
    mine = lax.all_to_all(packed, "x", 0, 0, tiled=True)

    state = struct((ROW * B, B), F32)
    edge = struct((2 * B, B), F32)
    edges = call(edge_kernel, [edge, edge], [me, mine], 10**5, 28, "edges")
    *edges, held = lax.optimization_barrier((*edges, mine))
    other = swap(held)
    from_a, from_b = exchange(*edges)
    step_edge = call(step_edge_kernel, struct((2, B, BAND * B), F32), [me, mine, other], 10**5, 20, "step_edges")
    step_edge = apart(step_edge)

    _, held = lax.optimization_barrier((other, coefficients))
    old = [coefficients, in_row(held, 1), in_row(held, 2), None]
    y0 = call(
        margin_kernel, state, [me, mine, other, from_a, from_b], 10**10, 60, "margin",
        scratch=[pltpu.VMEM((ROW, B, BAND * B), F32)] + [pltpu.VMEM((2 * ROW * B, 2 * B), BF16)],
    )
    arrived = exchange(y0, y0)
    _, held = lax.optimization_barrier((old[2], coefficients))
    old[3] = in_row(held, 3)
    *arrived, step_edge, old[1], old[2], old[3] = lax.optimization_barrier((*arrived, step_edge, *old[1:]))
    parts_type = struct((2 * ROW, B, BAND * B), BF16)
    step = list(
        call(
            parts_kernel, [parts_type, parts_type], [me, mine, other, step_edge, swap(step_edge)],
            10**6, 80, "step_parts",
        )
    )
    scratch = [pltpu.VMEM((3 * ROW * B, 2 * B), BF16), pltpu.VMEM((2 * ROW * B, 2 * B), BF16)]
    y1, y2 = call(
        functools.partial(two_kernel, 1), [state, state], [me] + step + arrived + [y0], 3 * ROW * step_flops, 64,
        "two", scratch=scratch,
    )
    arrived = exchange(y2, y2)
    old_type = struct((2 * width, 2 * ROW * B), BF16)
    old_high, old_low = call(
        old_kernel, [old_type, old_type], [me] + old + [swap(o) for o in old], 10**6, 64, "old_parts"
    )
    arrived[0], old_high = lax.optimization_barrier((arrived[0], old_high))
    new = call(
        functools.partial(last_kernel, 3), struct((ROW, B, B), F32), [me] + step + arrived + [y2, y0, y1],
        3 * ROW * step_flops, 72, "last", scratch=scratch,
    )
    partial_value = call(
        project_kernel, struct((2 * width, B), F32), [me, old_high, old_low, new],
        2 * 3 * 2 * width * 2 * ROW * B * B, 44, "project",
    )
    sums = lax.all_to_all(partial_value, "row", 0, 0, tiled=True)
    share = 2 * width // domains
    sent = struct((B + 2 * share, B), F32)
    tail = call(
        functools.partial(tail_kernel, 1.0 / (domains * B)), [sent] * ROW, [me, sums, new], 10**5, 12, "tail"
    )
    tail = [tail[0]] + [in_row(tail[j], j) for j in range(1, ROW)]
    return call(
        finish_kernel, (struct((2, 1, B, width), F32), struct((2, share, width), F32)), [me] + tail, 10**5, 8,
        "finish", scratch=[pltpu.VMEM((ROW, B + 2 * share, B), F32)],
    )


def solution(mesh):
    rows = mesh.shape["space"] // ROW
    grouped = Mesh(mesh.devices.reshape(rows, ROW, mesh.shape["orb"]), ("row", "x", "orb"))
    space = ("row", "x")
    return jax.shard_map(
        functools.partial(local, rows),
        mesh=grouped,
        in_specs=(
            P(None, space, None, "orb"),
            P(space, None, None, None),
            P(space, None, None, None),
            P(space, None),
            P(space, None),
        ),
        out_specs=(P(None, space, None, "orb"), P(None, space, "orb")),
        check_vma=False,
    )
```

```python
import functools

import jax
import jax.numpy as jnp
from jax import lax
from jax.experimental import pallas as pl
from jax.experimental.pallas import tpu as pltpu
from jax.sharding import Mesh, PartitionSpec as P

ORDER = 4
ROW = 4
BAND = 5
B = 128
HALF = B // 2
F32 = jnp.float32
BF16 = jnp.bfloat16

SMEM = pl.BlockSpec(memory_space=pltpu.SMEM)
VMEM = pl.BlockSpec(memory_space=pltpu.VMEM)


def cost(flops, moved):
    return pl.CostEstimate(flops=flops, bytes_accessed=moved, transcendentals=0)


def split(value):
    high = value.astype(BF16)
    return high, (value - high.astype(F32)).astype(BF16)


def product(a_high, a_low, b):
    dot = functools.partial(jnp.dot, preferred_element_type=F32)
    both = dot(a_high, b)
    return both[:, :B] + (both[:, B:] + dot(a_low, b[:, :B]))


def put_parts(out, rows, value):
    out[rows, :B], out[rows, B:] = split(value)


def turned(value):
    lane = lax.broadcasted_iota(jnp.int32, value.shape, 1)
    rolled = pltpu.roll(value, HALF, axis=1)
    return jnp.where(lane < HALF, rolled, -rolled)


def member(me):
    return lax.rem(lax.div(me[0], 2), ROW), lax.rem(me[0], 2)


def turn_to(q, x):
    return lax.rem(q - x + ROW, ROW)


def parity(me):
    return lax.rem(lax.div(me[0], 2 * ROW), 2)


def tile_kernel(me, coef, *refs):
    *outs, held = refs
    x, _ = member(me)
    for q in range(ROW):
        columns = slice(q * HALF, (q + 1) * HALF)
        held[turn_to(q, x)] = jnp.concatenate([coef[0, 0, :, columns], coef[1, 0, :, columns]], axis=1)
    for j, out in enumerate(outs):
        out[...] = held[j]


def pack_kernel(me, nbr_hbm, pat_hbm, margin_hbm, step_hbm, out, nbr, pat, margin, step, done):
    core = lax.rem(me[0], 2)
    rows = pl.ds(pl.multiple_of(core * HALF, HALF), HALF)
    copies = [
        pltpu.make_async_copy(margin_hbm.at[0, :, rows, :], margin, done.at[0]),
        pltpu.make_async_copy(step_hbm.at[0, :, rows, :], step, done.at[1]),
        pltpu.make_async_copy(nbr_hbm, nbr, done.at[2]),
        pltpu.make_async_copy(pat_hbm, pat, done.at[3]),
    ]
    for copy in copies[::-1]:
        copy.start()
    copies[2].wait()
    copies[3].wait()
    first = lax.div(me[0], 2) - 2
    slots = margin.shape[0]
    for i, source in enumerate((margin, step)):
        copies[i].wait()
        for d in range(BAND):
            total = None
            for k in range(slots):
                weight = F32(1.0) if k == 0 else pat[0, k].astype(F32)
                part = source[k] * jnp.where(nbr[0, k] == first + d, weight, F32(0.0))
                total = part if total is None else total + part
            start = (i * BAND + d) * HALF
            out[start : start + HALF, :] = total


def gather_kernel(me, mine, g1, g2, g3, out):
    x, _ = member(me)
    for j, ref in enumerate((mine, g1, g2, g3)):
        out[turn_to(x, j)] = ref[...]


def place_half(out, q, place, source, first):
    rows = pl.ds(pl.multiple_of(place * HALF, HALF), HALF)
    for d in range(BAND):
        start = first + d * HALF
        yield q, rows, slice(d * B, (d + 1) * B), source(slice(start, start + HALF))


def edge_kernel(me, t0, t1, t2, t3, own, to_a, to_b):
    x, _ = member(me)
    odd = parity(me)
    for j, ref in enumerate((t0, t1, t2, t3)):
        own[pl.ds(pl.multiple_of(turn_to(x, j) * B, B), B), :] = ref[...]
    for out, first in ((to_a, 2 - 2 * odd), (to_b, 2 * odd)):
        out[...] = own[pl.ds(pl.multiple_of(first * B, B), 2 * B), :]


def step_edge_kernel(me, mine, other, out):
    _, core = member(me)
    first = 2 * lax.rem(parity(me) + core + 1, 2)
    for q in range(2):
        for place, ref in ((core, mine), (1 - core, other)):
            for to, rows, columns, tile in place_half(out, q, place, lambda at: ref[first + q, at, :], BAND * HALF):
                out[to, rows, columns] = tile


def window(odd, from_a, from_b, own, v):
    reach, size = from_a.shape[0], own.shape[0]
    put_parts(v, slice(reach, reach + size), own)
    for start, tile in (((1 - odd) * (reach + size), from_a), (odd * (reach + size), from_b)):
        put_parts(v, pl.ds(pl.multiple_of(start, B), reach), tile)


def margin_kernel(me, own, mine, other, from_a, from_b, out, full, v):
    _, core = member(me)
    window(parity(me), from_a[...], from_b[...], own[...], v)
    for q in range(ROW):
        for place, ref in ((core, mine), (1 - core, other)):
            for _, rows, columns, tile in place_half(full, q, place, lambda at: ref[q, at, :], 0):
                full[q, rows, columns] = tile
    for q in range(ROW):
        m_high, m_low = split(full[q])
        rows = slice(q * B, (q + BAND) * B)
        out[q * B : (q + 1) * B, :] = own[q * B : (q + 1) * B, :] + product(m_high, m_low, v[rows, :])


def parts_kernel(me, mine, other, edge, edge_other, out_high, out_low):
    _, core = member(me)
    odd = parity(me)
    for q in range(ROW):
        for place, ref in ((core, mine), (1 - core, other)):
            for to, rows, columns, tile in place_half(out_high, q + 2, place, lambda at: ref[q, at, :], BAND * HALF):
                out_high[to, rows, columns], out_low[to, rows, columns] = split(tile)
    ahead = lax.rem(odd + core + 1, 2)
    for start, ref in ((ahead * 6, edge), ((1 - ahead) * 6, edge_other)):
        for q in range(2):
            out_high[start + q], out_low[start + q] = split(ref[q])


def two_steps(n, me, m_high, m_low, from_a, from_b, own, v, w):
    window(parity(me), from_a[...], from_b[...], own[...], v)
    firsts = []
    for q in range(2 * ROW):
        rows = slice(q * B, (q + BAND) * B)
        value = product(m_high[q], m_low[q], v[rows, :]) * F32(1.0 / n)
        put_parts(w, slice(q * B, (q + 1) * B), value)
        firsts.append(value)
    for q in range(ROW):
        rows = slice(q * B, (q + BAND) * B)
        second = product(m_high[q + 2], m_low[q + 2], w[rows, :]) * F32(1.0 / (n + 1))
        yield q, firsts[q + 2], second


def two_kernel(n, me, m_high, m_low, from_a, from_b, own, first, second, *scratch):
    for q, a, b in two_steps(n, me, m_high, m_low, from_a, from_b, own, *scratch):
        first[q * B : (q + 1) * B, :] = a
        second[q * B : (q + 1) * B, :] = b


def last_kernel(n, me, m_high, m_low, from_a, from_b, own, y0, y1, out, *scratch):
    x, _ = member(me)
    for q, y3, y4 in two_steps(n, me, m_high, m_low, from_a, from_b, own, *scratch):
        rows = slice(q * B, (q + 1) * B)
        out[turn_to(q, x)] = (y0[rows, :] - own[rows, :]) + y4 + turned(y1[rows, :] - y3)


def old_kernel(me, c0, c1, c2, c3, o0, o1, o2, o3, out_high, out_low):
    x, core = member(me)
    width = c0.shape[3]
    for j, (ref, other) in enumerate(((c0, o0), (c1, o1), (c2, o2), (c3, o3))):
        q = turn_to(x, j)
        for part in range(2):
            for place, tile in ((core, ref[part, 0]), (1 - core, other[part, 0])):
                rows = pl.ds(pl.multiple_of(place * width, width), width)
                columns = pl.ds(pl.multiple_of((part * ROW + q) * B, B), B)
                out_high[rows, columns], out_low[rows, columns] = split(jnp.transpose(tile))


def project_kernel(me, old_high, old_low, new, out):
    x, _ = member(me)
    tiles = [new[turn_to(q, x)] for q in range(ROW)]
    parts = split(jnp.concatenate(tiles + [turned(t) for t in tiles], axis=0))
    out[...] = product(old_high[...], old_low[...], jnp.concatenate(parts, axis=1))


def tail_kernel(scale, me, sums, new, *outs):
    x, _ = member(me)
    share = 4
    total = jnp.sum(sums[...].reshape(-1, ROW * share, B), axis=0) * scale
    for j, out in enumerate(outs):
        out[:B, :] = new[j]
        for q in range(ROW):

            @pl.when(q == lax.rem(x + j, ROW))
            def _():
                out[B : B + share, :] = total[q * share : (q + 1) * share, :]


def finish_kernel(me, mine, b1, b2, b3, propagated, owned, held):
    x, _ = member(me)
    share = owned.shape[1]
    for j, ref in enumerate((mine, b1, b2, b3)):
        held[turn_to(x, j)] = ref[...]
    for q in range(ROW):
        columns = slice(q * HALF, (q + 1) * HALF)
        for part in range(2):
            lanes = slice(part * HALF, (part + 1) * HALF)
            propagated[part, 0, :, columns] = held[q, :B, lanes]
            owned[part, :, columns] = held[q, B : B + share, lanes]


def local(rows, coefficients, margin, step_matrix, neighbours, pattern):
    width = coefficients.shape[3]
    domains = rows * ROW
    me = lax.axis_index(("row", "x", "orb")).astype(jnp.int32).reshape(1)
    struct = jax.ShapeDtypeStruct
    tile_bytes = 4 * B * B
    step_flops = 2 * 3 * B * BAND * B * B

    def call(kernel, out_shape, args, flops, moved, name, scratch=(), scalars=1):
        return pl.pallas_call(
            kernel,
            out_shape=out_shape,
            in_specs=[SMEM] * scalars + [VMEM] * (len(args) - scalars),
            out_specs=jax.tree.map(lambda _: VMEM, out_shape),
            scratch_shapes=list(scratch),
            cost_estimate=cost(flops, moved * tile_bytes),
            name=name,
            compiler_params=pltpu.CompilerParams(vmem_limit_bytes=32 * 2**20),
        )(*args)

    def in_row(value, by):
        return lax.ppermute(value, "x", [(x, (x + by) % ROW) for x in range(ROW)])

    def swap(value):
        return lax.ppermute(value, "orb", [(0, 1), (1, 0)])

    def exchange(to_a, to_b):
        def swap_rows(value, first):
            pairs = [(r, r + 1) for r in range(first, rows - 1, 2)]
            return lax.ppermute(value, "row", pairs + [(j, i) for i, j in pairs])

        return [swap_rows(to_a, 0), swap_rows(to_b, 1)]

    def apart(value):
        pairs = []
        for core in range(2):
            for r in range(core, rows - 1, 2):
                for x in range(ROW):
                    ends = [((r + i) * ROW + x) * 2 + core for i in range(2)]
                    pairs += [tuple(ends), tuple(ends[::-1])]
        return lax.ppermute(value, ("row", "x", "orb"), pairs)

    slots = neighbours.shape[1]
    tile = struct((B, B), F32)
    tiles = call(tile_kernel, [tile] * ROW, [me, coefficients], 10**5, 8, "tiles", scratch=[pltpu.VMEM((ROW, B, B), F32)])
    tiles = [tiles[0]] + [in_row(tiles[j], j) for j in range(1, ROW)]
    hbm = pl.BlockSpec(memory_space=pltpu.HBM)
    half_blocks = pltpu.VMEM((slots, HALF, B), F32)
    packed = pl.pallas_call(
        pack_kernel,
        in_specs=[SMEM] + [hbm] * 4,
        out_specs=VMEM,
        out_shape=struct((2 * BAND * HALF, B), F32),
        scratch_shapes=[
            pltpu.SMEM(neighbours.shape, jnp.int32), pltpu.SMEM(pattern.shape, jnp.int32),
            half_blocks, half_blocks, pltpu.SemaphoreType.DMA((4,)),
        ],
        cost_estimate=cost(10**6, 44 * tile_bytes),
        name="pack",
        compiler_params=pltpu.CompilerParams(vmem_limit_bytes=28 * 2**20),
    )(me, *(pltpu.with_memory_space_constraint(a, pltpu.HBM) for a in (neighbours, pattern, margin, step_matrix)))
    bands = [in_row(packed, j) for j in range(1, ROW)]

    state = struct((ROW * B, B), F32)
    edge = struct((2 * B, B), F32)
    own, *edges = call(edge_kernel, [state, edge, edge], [me] + tiles, 10**5, 12, "edges")
    from_a, from_b = exchange(*edges)
    from_a, from_b, *bands = lax.optimization_barrier((from_a, from_b, *bands))
    mine = call(gather_kernel, struct((ROW, 2 * BAND * HALF, B), F32), [me, packed] + bands, 10**5, 80, "gather")
    other = swap(mine)
    step_edge = call(step_edge_kernel, struct((2, B, BAND * B), F32), [me, mine, other], 10**5, 20, "step_edges")
    step_edge = apart(step_edge)

    _, held = lax.optimization_barrier((other, coefficients))
    old = [coefficients, in_row(held, 1), in_row(held, 2), None]
    y0 = call(
        margin_kernel, state, [me, own, mine, other, from_a, from_b], 10**10, 60, "margin",
        scratch=[pltpu.VMEM((ROW, B, BAND * B), F32)] + [pltpu.VMEM((2 * ROW * B, 2 * B), BF16)],
    )
    arrived = exchange(y0, y0)
    _, held = lax.optimization_barrier((old[2], coefficients))
    old[3] = in_row(held, 3)
    *arrived, step_edge, old[1], old[2], old[3] = lax.optimization_barrier((*arrived, step_edge, *old[1:]))
    parts_type = struct((2 * ROW, B, BAND * B), BF16)
    step = list(
        call(
            parts_kernel, [parts_type, parts_type], [me, mine, other, step_edge, swap(step_edge)],
            10**6, 80, "step_parts",
        )
    )
    scratch = [pltpu.VMEM((3 * ROW * B, 2 * B), BF16), pltpu.VMEM((2 * ROW * B, 2 * B), BF16)]
    y1, y2 = call(
        functools.partial(two_kernel, 1), [state, state], [me] + step + arrived + [y0], 3 * ROW * step_flops, 64,
        "two", scratch=scratch,
    )
    arrived = exchange(y2, y2)
    old_type = struct((2 * width, 2 * ROW * B), BF16)
    old_high, old_low = call(
        old_kernel, [old_type, old_type], [me] + old + [swap(o) for o in old], 10**6, 64, "old_parts"
    )
    arrived[0], old_high = lax.optimization_barrier((arrived[0], old_high))
    new = call(
        functools.partial(last_kernel, 3), struct((ROW, B, B), F32), [me] + step + arrived + [y2, y0, y1],
        3 * ROW * step_flops, 72, "last", scratch=scratch,
    )
    partial_value = call(
        project_kernel, struct((2 * width, B), F32), [me, old_high, old_low, new],
        2 * 3 * 2 * width * 2 * ROW * B * B, 44, "project",
    )
    sums = lax.all_to_all(partial_value, "row", 0, 0, tiled=True)
    share = 2 * width // domains
    sent = struct((B + 2 * share, B), F32)
    tail = call(
        functools.partial(tail_kernel, 1.0 / (domains * B)), [sent] * ROW, [me, sums, new], 10**5, 12, "tail"
    )
    tail = [tail[0]] + [in_row(tail[j], j) for j in range(1, ROW)]
    return call(
        finish_kernel, (struct((2, 1, B, width), F32), struct((2, share, width), F32)), [me] + tail, 10**5, 8,
        "finish", scratch=[pltpu.VMEM((ROW, B + 2 * share, B), F32)],
    )


def solution(mesh):
    rows = mesh.shape["space"] // ROW
    grouped = Mesh(mesh.devices.reshape(rows, ROW, mesh.shape["orb"]), ("row", "x", "orb"))
    space = ("row", "x")
    return jax.shard_map(
        functools.partial(local, rows),
        mesh=grouped,
        in_specs=(
            P(None, space, None, "orb"),
            P(space, None, None, None),
            P(space, None, None, None),
            P(space, None),
            P(space, None),
        ),
        out_specs=(P(None, space, None, "orb"), P(None, space, "orb")),
        check_vma=False,
    )
```

```python
import functools

import jax
import jax.numpy as jnp
from jax import lax
from jax.experimental import pallas as pl
from jax.experimental.pallas import tpu as pltpu
from jax.sharding import Mesh, PartitionSpec as P

ORDER = 4
ROW = 4
BAND = 5
B = 128
HALF = B // 2
F32 = jnp.float32
BF16 = jnp.bfloat16

SMEM = pl.BlockSpec(memory_space=pltpu.SMEM)
VMEM = pl.BlockSpec(memory_space=pltpu.VMEM)


def cost(flops, moved):
    return pl.CostEstimate(flops=flops, bytes_accessed=moved, transcendentals=0)


def split(value):
    high = value.astype(BF16)
    return high, (value - high.astype(F32)).astype(BF16)


def product(a_high, a_low, b):
    dot = functools.partial(jnp.dot, preferred_element_type=F32)
    both = dot(a_high, b)
    return both[:, :B] + (both[:, B:] + dot(a_low, b[:, :B]))


def put_parts(out, rows, value):
    out[rows, :B], out[rows, B:] = split(value)


def turned(value):
    lane = lax.broadcasted_iota(jnp.int32, value.shape, 1)
    rolled = pltpu.roll(value, HALF, axis=1)
    return jnp.where(lane < HALF, rolled, -rolled)


def member(me):
    return lax.rem(lax.div(me[0], 2), ROW), lax.rem(me[0], 2)


def turn_to(q, x):
    return lax.rem(q - x + ROW, ROW)


def parity(me):
    return lax.rem(lax.div(me[0], 2 * ROW), 2)


def tile_kernel(coef, out):
    for q in range(ROW):
        columns = slice(q * HALF, (q + 1) * HALF)
        out[q] = jnp.concatenate([coef[0, 0, :, columns], coef[1, 0, :, columns]], axis=1)


def pack_kernel(me, nbr_hbm, pat_hbm, margin_hbm, step_hbm, out, nbr, pat, margin, step, done):
    core = lax.rem(me[0], 2)
    rows = pl.ds(pl.multiple_of(core * HALF, HALF), HALF)
    copies = [
        pltpu.make_async_copy(margin_hbm.at[0, :, rows, :], margin, done.at[0]),
        pltpu.make_async_copy(step_hbm.at[0, :, rows, :], step, done.at[1]),
        pltpu.make_async_copy(nbr_hbm, nbr, done.at[2]),
        pltpu.make_async_copy(pat_hbm, pat, done.at[3]),
    ]
    for copy in copies[::-1]:
        copy.start()
    copies[2].wait()
    copies[3].wait()
    first = lax.div(me[0], 2) - 2
    slots = margin.shape[0]
    for i, source in enumerate((margin, step)):
        copies[i].wait()
        for d in range(BAND):
            total = None
            for k in range(slots):
                weight = F32(1.0) if k == 0 else pat[0, k].astype(F32)
                part = source[k] * jnp.where(nbr[0, k] == first + d, weight, F32(0.0))
                total = part if total is None else total + part
            start = (i * BAND + d) * HALF
            out[start : start + HALF, :] = total


def gather_kernel(me, mine, g1, g2, g3, out):
    x, _ = member(me)
    for j, ref in enumerate((mine, g1, g2, g3)):
        out[turn_to(x, j)] = ref[...]


def place_half(out, q, place, source, first):
    rows = pl.ds(pl.multiple_of(place * HALF, HALF), HALF)
    for d in range(BAND):
        start = first + d * HALF
        yield q, rows, slice(d * B, (d + 1) * B), source(slice(start, start + HALF))


def edge_kernel(me, own, to_a, to_b):
    odd = parity(me)
    for out, first in ((to_a, 2 - 2 * odd), (to_b, 2 * odd)):
        out[...] = own[pl.ds(pl.multiple_of(first * B, B), 2 * B), :]


def step_edge_kernel(me, mine, other, out):
    _, core = member(me)
    first = 2 * lax.rem(parity(me) + core + 1, 2)
    for q in range(2):
        for place, ref in ((core, mine), (1 - core, other)):
            for to, rows, columns, tile in place_half(out, q, place, lambda at: ref[first + q, at, :], BAND * HALF):
                out[to, rows, columns] = tile


def window(odd, from_a, from_b, own, v):
    reach, size = from_a.shape[0], own.shape[0]
    put_parts(v, slice(reach, reach + size), own)
    for start, tile in (((1 - odd) * (reach + size), from_a), (odd * (reach + size), from_b)):
        put_parts(v, pl.ds(pl.multiple_of(start, B), reach), tile)


def margin_kernel(me, own, mine, other, from_a, from_b, out, full, v):
    _, core = member(me)
    window(parity(me), from_a[...], from_b[...], own[...], v)
    for q in range(ROW):
        for place, ref in ((core, mine), (1 - core, other)):
            for _, rows, columns, tile in place_half(full, q, place, lambda at: ref[q, at, :], 0):
                full[q, rows, columns] = tile
    for q in range(ROW):
        m_high, m_low = split(full[q])
        rows = slice(q * B, (q + BAND) * B)
        out[q * B : (q + 1) * B, :] = own[q * B : (q + 1) * B, :] + product(m_high, m_low, v[rows, :])


def parts_kernel(me, mine, other, edge, edge_other, out_high, out_low):
    _, core = member(me)
    odd = parity(me)
    for q in range(ROW):
        for place, ref in ((core, mine), (1 - core, other)):
            for to, rows, columns, tile in place_half(out_high, q + 2, place, lambda at: ref[q, at, :], BAND * HALF):
                out_high[to, rows, columns], out_low[to, rows, columns] = split(tile)
    ahead = lax.rem(odd + core + 1, 2)
    for start, ref in ((ahead * 6, edge), ((1 - ahead) * 6, edge_other)):
        for q in range(2):
            out_high[start + q], out_low[start + q] = split(ref[q])


def two_steps(n, me, m_high, m_low, from_a, from_b, own, v, w):
    window(parity(me), from_a[...], from_b[...], own[...], v)
    firsts = []
    for q in range(2 * ROW):
        rows = slice(q * B, (q + BAND) * B)
        value = product(m_high[q], m_low[q], v[rows, :]) * F32(1.0 / n)
        put_parts(w, slice(q * B, (q + 1) * B), value)
        firsts.append(value)
    for q in range(ROW):
        rows = slice(q * B, (q + BAND) * B)
        second = product(m_high[q + 2], m_low[q + 2], w[rows, :]) * F32(1.0 / (n + 1))
        yield q, firsts[q + 2], second


def two_kernel(n, me, m_high, m_low, from_a, from_b, own, first, second, *scratch):
    for q, a, b in two_steps(n, me, m_high, m_low, from_a, from_b, own, *scratch):
        first[q * B : (q + 1) * B, :] = a
        second[q * B : (q + 1) * B, :] = b


def last_kernel(n, me, m_high, m_low, from_a, from_b, own, y0, y1, out, *scratch):
    x, _ = member(me)
    for q, y3, y4 in two_steps(n, me, m_high, m_low, from_a, from_b, own, *scratch):
        rows = slice(q * B, (q + 1) * B)
        out[turn_to(q, x)] = (y0[rows, :] - own[rows, :]) + y4 + turned(y1[rows, :] - y3)


def old_kernel(me, c0, c1, c2, c3, o0, o1, o2, o3, out_high, out_low):
    x, core = member(me)
    width = c0.shape[3]
    for j, (ref, other) in enumerate(((c0, o0), (c1, o1), (c2, o2), (c3, o3))):
        q = turn_to(x, j)
        for part in range(2):
            for place, tile in ((core, ref[part, 0]), (1 - core, other[part, 0])):
                rows = pl.ds(pl.multiple_of(place * width, width), width)
                columns = pl.ds(pl.multiple_of((part * ROW + q) * B, B), B)
                out_high[rows, columns], out_low[rows, columns] = split(jnp.transpose(tile))


def project_kernel(me, old_high, old_low, new, out):
    x, _ = member(me)
    tiles = [new[turn_to(q, x)] for q in range(ROW)]
    parts = split(jnp.concatenate(tiles + [turned(t) for t in tiles], axis=0))
    out[...] = product(old_high[...], old_low[...], jnp.concatenate(parts, axis=1))


def tail_kernel(scale, me, sums, new, *outs):
    x, _ = member(me)
    share = 4
    total = jnp.sum(sums[...].reshape(-1, ROW * share, B), axis=0) * scale
    for j, out in enumerate(outs):
        out[:B, :] = new[j]
        for q in range(ROW):

            @pl.when(q == lax.rem(x + j, ROW))
            def _():
                out[B : B + share, :] = total[q * share : (q + 1) * share, :]


def finish_kernel(me, mine, b1, b2, b3, propagated, owned, held):
    x, _ = member(me)
    share = owned.shape[1]
    for j, ref in enumerate((mine, b1, b2, b3)):
        held[turn_to(x, j)] = ref[...]
    for q in range(ROW):
        columns = slice(q * HALF, (q + 1) * HALF)
        for part in range(2):
            lanes = slice(part * HALF, (part + 1) * HALF)
            propagated[part, 0, :, columns] = held[q, :B, lanes]
            owned[part, :, columns] = held[q, B : B + share, lanes]


def local(rows, coefficients, margin, step_matrix, neighbours, pattern):
    width = coefficients.shape[3]
    domains = rows * ROW
    me = lax.axis_index(("row", "x", "orb")).astype(jnp.int32).reshape(1)
    struct = jax.ShapeDtypeStruct
    tile_bytes = 4 * B * B
    step_flops = 2 * 3 * B * BAND * B * B

    def call(kernel, out_shape, args, flops, moved, name, scratch=(), scalars=1):
        return pl.pallas_call(
            kernel,
            out_shape=out_shape,
            in_specs=[SMEM] * scalars + [VMEM] * (len(args) - scalars),
            out_specs=jax.tree.map(lambda _: VMEM, out_shape),
            scratch_shapes=list(scratch),
            cost_estimate=cost(flops, moved * tile_bytes),
            name=name,
            compiler_params=pltpu.CompilerParams(vmem_limit_bytes=32 * 2**20),
        )(*args)

    def in_row(value, by):
        return lax.ppermute(value, "x", [(x, (x + by) % ROW) for x in range(ROW)])

    def swap(value):
        return lax.ppermute(value, "orb", [(0, 1), (1, 0)])

    def exchange(to_a, to_b):
        def swap_rows(value, first):
            pairs = [(r, r + 1) for r in range(first, rows - 1, 2)]
            return lax.ppermute(value, "row", pairs + [(j, i) for i, j in pairs])

        return [swap_rows(to_a, 0), swap_rows(to_b, 1)]

    def apart(value):
        pairs = []
        for core in range(2):
            for r in range(core, rows - 1, 2):
                for x in range(ROW):
                    ends = [((r + i) * ROW + x) * 2 + core for i in range(2)]
                    pairs += [tuple(ends), tuple(ends[::-1])]
        return lax.ppermute(value, ("row", "x", "orb"), pairs)

    slots = neighbours.shape[1]
    tiles = call(tile_kernel, struct((ROW, B, B), F32), [coefficients], 10**5, 8, "tiles", scalars=0)
    hbm = pl.BlockSpec(memory_space=pltpu.HBM)
    half_blocks = pltpu.VMEM((slots, HALF, B), F32)
    packed = pl.pallas_call(
        pack_kernel,
        in_specs=[SMEM] + [hbm] * 4,
        out_specs=VMEM,
        out_shape=struct((2 * BAND * HALF, B), F32),
        scratch_shapes=[
            pltpu.SMEM(neighbours.shape, jnp.int32), pltpu.SMEM(pattern.shape, jnp.int32),
            half_blocks, half_blocks, pltpu.SemaphoreType.DMA((4,)),
        ],
        cost_estimate=cost(10**6, 44 * tile_bytes),
        name="pack",
        compiler_params=pltpu.CompilerParams(vmem_limit_bytes=28 * 2**20),
    )(me, *(pltpu.with_memory_space_constraint(a, pltpu.HBM) for a in (neighbours, pattern, margin, step_matrix)))
    tiles, packed = lax.optimization_barrier((tiles, packed))
    own = lax.all_to_all(tiles, "x", 0, 0, tiled=True).reshape(ROW * B, B)
    own, packed = lax.optimization_barrier((own, packed))
    bands = [in_row(packed, j) for j in range(1, ROW)]

    state = struct((ROW * B, B), F32)
    edge = struct((2 * B, B), F32)
    edges = call(edge_kernel, [edge, edge], [me, own], 10**5, 8, "edges")
    from_a, from_b = exchange(*edges)
    from_a, from_b, *bands = lax.optimization_barrier((from_a, from_b, *bands))
    mine = call(gather_kernel, struct((ROW, 2 * BAND * HALF, B), F32), [me, packed] + bands, 10**5, 80, "gather")
    other = swap(mine)
    _, held = lax.optimization_barrier((other, coefficients))
    old = [coefficients, in_row(held, 1), in_row(held, 2), None]
    y0 = call(
        margin_kernel, state, [me, own, mine, other, from_a, from_b], 10**10, 60, "margin",
        scratch=[pltpu.VMEM((ROW, B, BAND * B), F32)] + [pltpu.VMEM((2 * ROW * B, 2 * B), BF16)],
    )
    y0, late = lax.optimization_barrier((y0, mine))
    step_edge = call(step_edge_kernel, struct((2, B, BAND * B), F32), [me, late, other], 10**5, 20, "step_edges")
    step_edge = apart(step_edge)

    arrived = exchange(y0, y0)
    _, held = lax.optimization_barrier((old[2], coefficients))
    old[3] = in_row(held, 3)
    *arrived, step_edge, old[1], old[2], old[3] = lax.optimization_barrier((*arrived, step_edge, *old[1:]))
    parts_type = struct((2 * ROW, B, BAND * B), BF16)
    step = list(
        call(
            parts_kernel, [parts_type, parts_type], [me, mine, other, step_edge, swap(step_edge)],
            10**6, 80, "step_parts",
        )
    )
    scratch = [pltpu.VMEM((3 * ROW * B, 2 * B), BF16), pltpu.VMEM((2 * ROW * B, 2 * B), BF16)]
    y1, y2 = call(
        functools.partial(two_kernel, 1), [state, state], [me] + step + arrived + [y0], 3 * ROW * step_flops, 64,
        "two", scratch=scratch,
    )
    arrived = exchange(y2, y2)
    old_type = struct((2 * width, 2 * ROW * B), BF16)
    old_high, old_low = call(
        old_kernel, [old_type, old_type], [me] + old + [swap(o) for o in old], 10**6, 64, "old_parts"
    )
    arrived[0], old_high = lax.optimization_barrier((arrived[0], old_high))
    new = call(
        functools.partial(last_kernel, 3), struct((ROW, B, B), F32), [me] + step + arrived + [y2, y0, y1],
        3 * ROW * step_flops, 72, "last", scratch=scratch,
    )
    partial_value = call(
        project_kernel, struct((2 * width, B), F32), [me, old_high, old_low, new],
        2 * 3 * 2 * width * 2 * ROW * B * B, 44, "project",
    )
    sums = lax.all_to_all(partial_value, "row", 0, 0, tiled=True)
    share = 2 * width // domains
    sent = struct((B + 2 * share, B), F32)
    tail = call(
        functools.partial(tail_kernel, 1.0 / (domains * B)), [sent] * ROW, [me, sums, new], 10**5, 12, "tail"
    )
    tail = [tail[0]] + [in_row(tail[j], j) for j in range(1, ROW)]
    return call(
        finish_kernel, (struct((2, 1, B, width), F32), struct((2, share, width), F32)), [me] + tail, 10**5, 8,
        "finish", scratch=[pltpu.VMEM((ROW, B + 2 * share, B), F32)],
    )


def solution(mesh):
    rows = mesh.shape["space"] // ROW
    grouped = Mesh(mesh.devices.reshape(rows, ROW, mesh.shape["orb"]), ("row", "x", "orb"))
    space = ("row", "x")
    return jax.shard_map(
        functools.partial(local, rows),
        mesh=grouped,
        in_specs=(
            P(None, space, None, "orb"),
            P(space, None, None, None),
            P(space, None, None, None),
            P(space, None),
            P(space, None),
        ),
        out_specs=(P(None, space, None, "orb"), P(None, space, "orb")),
        check_vma=False,
    )
```

```python
import functools

import jax
import jax.numpy as jnp
from jax import lax
from jax.experimental import pallas as pl
from jax.experimental.pallas import tpu as pltpu
from jax.sharding import Mesh, PartitionSpec as P

ORDER = 4
ROW = 4
BAND = 5
B = 128
HALF = B // 2
F32 = jnp.float32
BF16 = jnp.bfloat16

SMEM = pl.BlockSpec(memory_space=pltpu.SMEM)
VMEM = pl.BlockSpec(memory_space=pltpu.VMEM)


def cost(flops, moved):
    return pl.CostEstimate(flops=flops, bytes_accessed=moved, transcendentals=0)


def split(value):
    high = value.astype(BF16)
    return high, (value - high.astype(F32)).astype(BF16)


def product(a_high, a_low, b):
    dot = functools.partial(jnp.dot, preferred_element_type=F32)
    both = dot(a_high, b)
    return both[:, :B] + (both[:, B:] + dot(a_low, b[:, :B]))


def put_parts(out, rows, value):
    out[rows, :B], out[rows, B:] = split(value)


def turned(value):
    lane = lax.broadcasted_iota(jnp.int32, value.shape, 1)
    rolled = pltpu.roll(value, HALF, axis=1)
    return jnp.where(lane < HALF, rolled, -rolled)


def member(me):
    return lax.rem(lax.div(me[0], 2), ROW), lax.rem(me[0], 2)


def turn_to(q, x):
    return lax.rem(q - x + ROW, ROW)


def parity(me):
    return lax.rem(lax.div(me[0], 2 * ROW), 2)


def pack_kernel(me, nbr_hbm, pat_hbm, coef_hbm, margin_hbm, step_hbm, out, nbr, pat, coef, margin, step, done):
    core = lax.rem(me[0], 2)
    rows = pl.ds(pl.multiple_of(core * HALF, HALF), HALF)
    copies = [
        pltpu.make_async_copy(margin_hbm.at[0, :, rows, :], margin, done.at[0]),
        pltpu.make_async_copy(step_hbm.at[0, :, rows, :], step, done.at[1]),
        pltpu.make_async_copy(coef_hbm, coef, done.at[2]),
        pltpu.make_async_copy(nbr_hbm, nbr, done.at[3]),
        pltpu.make_async_copy(pat_hbm, pat, done.at[4]),
    ]
    for copy in copies[::-1]:
        copy.start()
    copies[3].wait()
    copies[4].wait()
    first = lax.div(me[0], 2) - 2
    slots = margin.shape[0]
    for i, source in enumerate((margin, step)):
        copies[i].wait()
        for d in range(BAND):
            total = None
            for k in range(slots):
                weight = F32(1.0) if k == 0 else pat[0, k].astype(F32)
                part = source[k] * jnp.where(nbr[0, k] == first + d, weight, F32(0.0))
                total = part if total is None else total + part
            start = B + (i * BAND + d) * HALF
            for q in range(ROW):
                out[q, start : start + HALF, :] = total
    copies[2].wait()
    for q in range(ROW):
        columns = slice(q * HALF, (q + 1) * HALF)
        out[q, :B, :] = jnp.concatenate([coef[0, 0, :, columns], coef[1, 0, :, columns]], axis=1)


def place_half(out, q, place, source, first):
    rows = pl.ds(pl.multiple_of(place * HALF, HALF), HALF)
    for d in range(BAND):
        start = first + d * HALF
        yield q, rows, slice(d * B, (d + 1) * B), source(slice(start, start + HALF))


def edge_kernel(me, mine, to_a, to_b):
    odd = parity(me)
    for out, first in ((to_a, 2 - 2 * odd), (to_b, 2 * odd)):
        for q in range(2):
            out[q * B : (q + 1) * B, :] = mine[first + q, :B, :]


def step_edge_kernel(me, mine, other, out):
    _, core = member(me)
    first = 2 * lax.rem(parity(me) + core + 1, 2)
    for q in range(2):
        for place, ref in ((core, mine), (1 - core, other)):
            for to, rows, columns, tile in place_half(out, q, place, lambda at: ref[first + q, at, :], B + BAND * HALF):
                out[to, rows, columns] = tile


def window(odd, from_a, from_b, own, v):
    reach, size = from_a.shape[0], own.shape[0]
    put_parts(v, slice(reach, reach + size), own)
    for start, tile in (((1 - odd) * (reach + size), from_a), (odd * (reach + size), from_b)):
        put_parts(v, pl.ds(pl.multiple_of(start, B), reach), tile)


def margin_kernel(me, mine, other, from_a, from_b, out, full, v):
    _, core = member(me)
    own = [mine[q, :B, :] for q in range(ROW)]
    window(parity(me), from_a[...], from_b[...], jnp.concatenate(own, axis=0), v)
    for q in range(ROW):
        for place, ref in ((core, mine), (1 - core, other)):
            for _, rows, columns, tile in place_half(full, q, place, lambda at: ref[q, at, :], B):
                full[q, rows, columns] = tile
    for q in range(ROW):
        m_high, m_low = split(full[q])
        rows = slice(q * B, (q + BAND) * B)
        out[q * B : (q + 1) * B, :] = own[q] + product(m_high, m_low, v[rows, :])


def parts_kernel(me, mine, other, edge, edge_other, out_high, out_low):
    _, core = member(me)
    odd = parity(me)
    for q in range(ROW):
        for place, ref in ((core, mine), (1 - core, other)):
            for to, rows, columns, tile in place_half(out_high, q + 2, place, lambda at: ref[q, at, :], B + BAND * HALF):
                out_high[to, rows, columns], out_low[to, rows, columns] = split(tile)
    ahead = lax.rem(odd + core + 1, 2)
    for start, ref in ((ahead * 6, edge), ((1 - ahead) * 6, edge_other)):
        for q in range(2):
            out_high[start + q], out_low[start + q] = split(ref[q])


def two_steps(n, me, m_high, m_low, from_a, from_b, own, v, w):
    window(parity(me), from_a[...], from_b[...], own[...], v)
    firsts = []
    for q in range(2 * ROW):
        rows = slice(q * B, (q + BAND) * B)
        value = product(m_high[q], m_low[q], v[rows, :]) * F32(1.0 / n)
        put_parts(w, slice(q * B, (q + 1) * B), value)
        firsts.append(value)
    for q in range(ROW):
        rows = slice(q * B, (q + BAND) * B)
        second = product(m_high[q + 2], m_low[q + 2], w[rows, :]) * F32(1.0 / (n + 1))
        yield q, firsts[q + 2], second


def two_kernel(n, me, m_high, m_low, from_a, from_b, own, first, second, *scratch):
    for q, a, b in two_steps(n, me, m_high, m_low, from_a, from_b, own, *scratch):
        first[q * B : (q + 1) * B, :] = a
        second[q * B : (q + 1) * B, :] = b


def last_kernel(n, me, m_high, m_low, from_a, from_b, own, y0, y1, out, *scratch):
    x, _ = member(me)
    for q, y3, y4 in two_steps(n, me, m_high, m_low, from_a, from_b, own, *scratch):
        rows = slice(q * B, (q + 1) * B)
        out[turn_to(q, x)] = (y0[rows, :] - own[rows, :]) + y4 + turned(y1[rows, :] - y3)


def old_kernel(me, c0, c1, c2, c3, o0, o1, o2, o3, out_high, out_low):
    x, core = member(me)
    width = c0.shape[3]
    for j, (ref, other) in enumerate(((c0, o0), (c1, o1), (c2, o2), (c3, o3))):
        q = turn_to(x, j)
        for part in range(2):
            for place, tile in ((core, ref[part, 0]), (1 - core, other[part, 0])):
                rows = pl.ds(pl.multiple_of(place * width, width), width)
                columns = pl.ds(pl.multiple_of((part * ROW + q) * B, B), B)
                out_high[rows, columns], out_low[rows, columns] = split(jnp.transpose(tile))


def project_kernel(me, old_high, old_low, new, out):
    x, _ = member(me)
    tiles = [new[turn_to(q, x)] for q in range(ROW)]
    parts = split(jnp.concatenate(tiles + [turned(t) for t in tiles], axis=0))
    out[...] = product(old_high[...], old_low[...], jnp.concatenate(parts, axis=1))


def tail_kernel(scale, me, sums, new, *outs):
    x, _ = member(me)
    share = 4
    total = jnp.sum(sums[...].reshape(-1, ROW * share, B), axis=0) * scale
    for j, out in enumerate(outs):
        out[:B, :] = new[j]
        for q in range(ROW):

            @pl.when(q == lax.rem(x + j, ROW))
            def _():
                out[B : B + share, :] = total[q * share : (q + 1) * share, :]


def finish_kernel(me, mine, b1, b2, b3, propagated, owned, held):
    x, _ = member(me)
    share = owned.shape[1]
    for j, ref in enumerate((mine, b1, b2, b3)):
        held[turn_to(x, j)] = ref[...]
    for q in range(ROW):
        columns = slice(q * HALF, (q + 1) * HALF)
        for part in range(2):
            lanes = slice(part * HALF, (part + 1) * HALF)
            propagated[part, 0, :, columns] = held[q, :B, lanes]
            owned[part, :, columns] = held[q, B : B + share, lanes]


def local(rows, coefficients, margin, step_matrix, neighbours, pattern):
    width = coefficients.shape[3]
    domains = rows * ROW
    me = lax.axis_index(("row", "x", "orb")).astype(jnp.int32).reshape(1)
    struct = jax.ShapeDtypeStruct
    tile_bytes = 4 * B * B
    step_flops = 2 * 3 * B * BAND * B * B

    def call(kernel, out_shape, args, flops, moved, name, scratch=(), scalars=1):
        return pl.pallas_call(
            kernel,
            out_shape=out_shape,
            in_specs=[SMEM] * scalars + [VMEM] * (len(args) - scalars),
            out_specs=jax.tree.map(lambda _: VMEM, out_shape),
            scratch_shapes=list(scratch),
            cost_estimate=cost(flops, moved * tile_bytes),
            name=name,
            compiler_params=pltpu.CompilerParams(vmem_limit_bytes=32 * 2**20),
        )(*args)

    def in_row(value, by):
        return lax.ppermute(value, "x", [(x, (x + by) % ROW) for x in range(ROW)])

    def swap(value):
        return lax.ppermute(value, "orb", [(0, 1), (1, 0)])

    def exchange(to_a, to_b):
        def swap_rows(value, first):
            pairs = [(r, r + 1) for r in range(first, rows - 1, 2)]
            return lax.ppermute(value, "row", pairs + [(j, i) for i, j in pairs])

        return [swap_rows(to_a, 0), swap_rows(to_b, 1)]

    def apart(value):
        pairs = []
        for core in range(2):
            for r in range(core, rows - 1, 2):
                for x in range(ROW):
                    ends = [((r + i) * ROW + x) * 2 + core for i in range(2)]
                    pairs += [tuple(ends), tuple(ends[::-1])]
        return lax.ppermute(value, ("row", "x", "orb"), pairs)

    slots = neighbours.shape[1]
    hbm = pl.BlockSpec(memory_space=pltpu.HBM)
    half_blocks = pltpu.VMEM((slots, HALF, B), F32)
    packed = pl.pallas_call(
        pack_kernel,
        in_specs=[SMEM] + [hbm] * 5,
        out_specs=VMEM,
        out_shape=struct((ROW, B + 2 * BAND * HALF, B), F32),
        scratch_shapes=[
            pltpu.SMEM(neighbours.shape, jnp.int32), pltpu.SMEM(pattern.shape, jnp.int32),
            pltpu.VMEM(coefficients.shape, F32), half_blocks, half_blocks, pltpu.SemaphoreType.DMA((5,)),
        ],
        cost_estimate=cost(10**6, 44 * tile_bytes),
        name="pack",
        compiler_params=pltpu.CompilerParams(vmem_limit_bytes=28 * 2**20),
    )(me, *(pltpu.with_memory_space_constraint(a, pltpu.HBM) for a in (neighbours, pattern, coefficients, margin, step_matrix)))
    mine = lax.all_to_all(packed, "x", 0, 0, tiled=True)

    state = struct((ROW * B, B), F32)
    edge = struct((2 * B, B), F32)
    edges = call(edge_kernel, [edge, edge], [me, mine], 10**5, 28, "edges")
    *edges, held = lax.optimization_barrier((*edges, mine))
    other = swap(held)
    from_a, from_b = exchange(*edges)
    step_edge = call(step_edge_kernel, struct((2, B, BAND * B), F32), [me, mine, other], 10**5, 20, "step_edges")
    step_edge = apart(step_edge)

    _, held = lax.optimization_barrier((other, coefficients))
    old = [coefficients, in_row(held, 1), in_row(held, 2), None]
    y0 = call(
        margin_kernel, state, [me, mine, other, from_a, from_b], 10**10, 60, "margin",
        scratch=[pltpu.VMEM((ROW, B, BAND * B), F32)] + [pltpu.VMEM((2 * ROW * B, 2 * B), BF16)],
    )
    arrived = exchange(y0, y0)
    _, held = lax.optimization_barrier((old[2], coefficients))
    old[3] = in_row(held, 3)
    *arrived, step_edge, old[1], old[2], old[3] = lax.optimization_barrier((*arrived, step_edge, *old[1:]))
    parts_type = struct((2 * ROW, B, BAND * B), BF16)
    step = list(
        call(
            parts_kernel, [parts_type, parts_type], [me, mine, other, step_edge, swap(step_edge)],
            10**6, 80, "step_parts",
        )
    )
    step[0], *old = lax.optimization_barrier((step[0], *old))
    scratch = [pltpu.VMEM((3 * ROW * B, 2 * B), BF16), pltpu.VMEM((2 * ROW * B, 2 * B), BF16)]
    y1, y2 = call(
        functools.partial(two_kernel, 1), [state, state], [me] + step + arrived + [y0], 3 * ROW * step_flops, 64,
        "two", scratch=scratch,
    )
    arrived = exchange(y2, y2)
    old_type = struct((2 * width, 2 * ROW * B), BF16)
    old_high, old_low = call(
        old_kernel, [old_type, old_type], [me] + old + [swap(o) for o in old], 10**6, 64, "old_parts"
    )
    arrived[0], old_high = lax.optimization_barrier((arrived[0], old_high))
    new = call(
        functools.partial(last_kernel, 3), struct((ROW, B, B), F32), [me] + step + arrived + [y2, y0, y1],
        3 * ROW * step_flops, 72, "last", scratch=scratch,
    )
    partial_value = call(
        project_kernel, struct((2 * width, B), F32), [me, old_high, old_low, new],
        2 * 3 * 2 * width * 2 * ROW * B * B, 44, "project",
    )
    sums = lax.all_to_all(partial_value, "row", 0, 0, tiled=True)
    share = 2 * width // domains
    sent = struct((B + 2 * share, B), F32)
    tail = call(
        functools.partial(tail_kernel, 1.0 / (domains * B)), [sent] * ROW, [me, sums, new], 10**5, 12, "tail"
    )
    tail = [tail[0]] + [in_row(tail[j], j) for j in range(1, ROW)]
    return call(
        finish_kernel, (struct((2, 1, B, width), F32), struct((2, share, width), F32)), [me] + tail, 10**5, 8,
        "finish", scratch=[pltpu.VMEM((ROW, B + 2 * share, B), F32)],
    )


def solution(mesh):
    rows = mesh.shape["space"] // ROW
    grouped = Mesh(mesh.devices.reshape(rows, ROW, mesh.shape["orb"]), ("row", "x", "orb"))
    space = ("row", "x")
    return jax.shard_map(
        functools.partial(local, rows),
        mesh=grouped,
        in_specs=(
            P(None, space, None, "orb"),
            P(space, None, None, None),
            P(space, None, None, None),
            P(space, None),
            P(space, None),
        ),
        out_specs=(P(None, space, None, "orb"), P(None, space, "orb")),
        check_vma=False,
    )
```

```python
import functools

import jax
import jax.numpy as jnp
from jax import lax
from jax.experimental import pallas as pl
from jax.experimental.pallas import tpu as pltpu
from jax.sharding import Mesh, PartitionSpec as P

ORDER = 4
ROW = 4
BAND = 5
B = 128
HALF = B // 2
F32 = jnp.float32
BF16 = jnp.bfloat16

SMEM = pl.BlockSpec(memory_space=pltpu.SMEM)
VMEM = pl.BlockSpec(memory_space=pltpu.VMEM)


def cost(flops, moved):
    return pl.CostEstimate(flops=flops, bytes_accessed=moved, transcendentals=0)


def split(value):
    high = value.astype(BF16)
    return high, (value - high.astype(F32)).astype(BF16)


def product(a_high, a_low, b):
    dot = functools.partial(jnp.dot, preferred_element_type=F32)
    both = dot(a_high, b)
    return both[:, :B] + (both[:, B:] + dot(a_low, b[:, :B]))


def put_parts(out, rows, value):
    out[rows, :B], out[rows, B:] = split(value)


def turned(value):
    lane = lax.broadcasted_iota(jnp.int32, value.shape, 1)
    rolled = pltpu.roll(value, HALF, axis=1)
    return jnp.where(lane < HALF, rolled, -rolled)


def member(me):
    return lax.rem(lax.div(me[0], 2), ROW), lax.rem(me[0], 2)


def turn_to(q, x):
    return lax.rem(q - x + ROW, ROW)


def parity(me):
    return lax.rem(lax.div(me[0], 2 * ROW), 2)


def pack_kernel(me, nbr_hbm, pat_hbm, coef_hbm, margin_hbm, step_hbm, out, nbr, pat, coef, margin, step, done):
    core = lax.rem(me[0], 2)
    rows = pl.ds(pl.multiple_of(core * HALF, HALF), HALF)
    copies = [
        pltpu.make_async_copy(margin_hbm.at[0, :, rows, :], margin, done.at[0]),
        pltpu.make_async_copy(step_hbm.at[0, :, rows, :], step, done.at[1]),
        pltpu.make_async_copy(coef_hbm, coef, done.at[2]),
        pltpu.make_async_copy(nbr_hbm, nbr, done.at[3]),
        pltpu.make_async_copy(pat_hbm, pat, done.at[4]),
    ]
    for copy in copies[::-1]:
        copy.start()
    copies[3].wait()
    copies[4].wait()
    first = lax.div(me[0], 2) - 2
    slots = margin.shape[0]
    for i, source in enumerate((margin, step)):
        copies[i].wait()
        for d in range(BAND):
            total = None
            for k in range(slots):
                weight = F32(1.0) if k == 0 else pat[0, k].astype(F32)
                part = source[k] * jnp.where(nbr[0, k] == first + d, weight, F32(0.0))
                total = part if total is None else total + part
            start = B + (i * BAND + d) * HALF
            for q in range(ROW):
                out[q, start : start + HALF, :] = total
    copies[2].wait()
    for q in range(ROW):
        columns = slice(q * HALF, (q + 1) * HALF)
        out[q, :B, :] = jnp.concatenate([coef[0, 0, :, columns], coef[1, 0, :, columns]], axis=1)


def place_half(out, q, place, source, first):
    rows = pl.ds(pl.multiple_of(place * HALF, HALF), HALF)
    for d in range(BAND):
        start = first + d * HALF
        yield q, rows, slice(d * B, (d + 1) * B), source(slice(start, start + HALF))


def edge_kernel(me, mine, to_a, to_b):
    odd = parity(me)
    for out, first in ((to_a, 2 - 2 * odd), (to_b, 2 * odd)):
        for q in range(2):
            out[q * B : (q + 1) * B, :] = mine[first + q, :B, :]


def step_edge_kernel(me, mine, other, out):
    _, core = member(me)
    first = 2 * lax.rem(parity(me) + core + 1, 2)
    for q in range(2):
        for place, ref in ((core, mine), (1 - core, other)):
            for to, rows, columns, tile in place_half(out, q, place, lambda at: ref[first + q, at, :], B + BAND * HALF):
                out[to, rows, columns] = tile


def window(odd, from_a, from_b, own, v):
    reach, size = from_a.shape[0], own.shape[0]
    put_parts(v, slice(reach, reach + size), own)
    for start, tile in (((1 - odd) * (reach + size), from_a), (odd * (reach + size), from_b)):
        put_parts(v, pl.ds(pl.multiple_of(start, B), reach), tile)


def margin_kernel(me, mine, other, from_a, from_b, out, full, v):
    _, core = member(me)
    own = [mine[q, :B, :] for q in range(ROW)]
    window(parity(me), from_a[...], from_b[...], jnp.concatenate(own, axis=0), v)
    for q in range(ROW):
        for place, ref in ((core, mine), (1 - core, other)):
            for _, rows, columns, tile in place_half(full, q, place, lambda at: ref[q, at, :], B):
                full[q, rows, columns] = tile
    for q in range(ROW):
        m_high, m_low = split(full[q])
        rows = slice(q * B, (q + BAND) * B)
        out[q * B : (q + 1) * B, :] = own[q] + product(m_high, m_low, v[rows, :])


def parts_kernel(me, mine, other, edge, edge_other, out_high, out_low):
    _, core = member(me)
    odd = parity(me)
    for q in range(ROW):
        for place, ref in ((core, mine), (1 - core, other)):
            for to, rows, columns, tile in place_half(out_high, q + 2, place, lambda at: ref[q, at, :], B + BAND * HALF):
                out_high[to, rows, columns], out_low[to, rows, columns] = split(tile)
    ahead = lax.rem(odd + core + 1, 2)
    for start, ref in ((ahead * 6, edge), ((1 - ahead) * 6, edge_other)):
        for q in range(2):
            out_high[start + q], out_low[start + q] = split(ref[q])


def two_steps(n, me, m_high, m_low, from_a, from_b, own, v, w):
    window(parity(me), from_a[...], from_b[...], own[...], v)
    firsts = []
    for q in range(2 * ROW):
        rows = slice(q * B, (q + BAND) * B)
        value = product(m_high[q], m_low[q], v[rows, :]) * F32(1.0 / n)
        put_parts(w, slice(q * B, (q + 1) * B), value)
        firsts.append(value)
    for q in range(ROW):
        rows = slice(q * B, (q + BAND) * B)
        second = product(m_high[q + 2], m_low[q + 2], w[rows, :]) * F32(1.0 / (n + 1))
        yield q, firsts[q + 2], second


def two_kernel(n, me, m_high, m_low, from_a, from_b, own, first, second, *scratch):
    for q, a, b in two_steps(n, me, m_high, m_low, from_a, from_b, own, *scratch):
        first[q * B : (q + 1) * B, :] = a
        second[q * B : (q + 1) * B, :] = b


def last_kernel(n, me, m_high, m_low, from_a, from_b, own, y0, y1, out, *scratch):
    x, _ = member(me)
    for q, y3, y4 in two_steps(n, me, m_high, m_low, from_a, from_b, own, *scratch):
        rows = slice(q * B, (q + 1) * B)
        out[turn_to(q, x)] = (y0[rows, :] - own[rows, :]) + y4 + turned(y1[rows, :] - y3)


def old_kernel(me, c0, c1, c2, c3, o0, o1, o2, o3, out_high, out_low):
    x, core = member(me)
    width = c0.shape[3]
    for j, (ref, other) in enumerate(((c0, o0), (c1, o1), (c2, o2), (c3, o3))):
        q = turn_to(x, j)
        for part in range(2):
            for place, tile in ((core, ref[part, 0]), (1 - core, other[part, 0])):
                rows = pl.ds(pl.multiple_of(place * width, width), width)
                columns = pl.ds(pl.multiple_of((part * ROW + q) * B, B), B)
                out_high[rows, columns], out_low[rows, columns] = split(jnp.transpose(tile))


def project_kernel(me, old_high, old_low, new, out):
    x, _ = member(me)
    tiles = [new[turn_to(q, x)] for q in range(ROW)]
    parts = split(jnp.concatenate(tiles + [turned(t) for t in tiles], axis=0))
    out[...] = product(old_high[...], old_low[...], jnp.concatenate(parts, axis=1))


def tail_kernel(scale, me, sums, new, *outs):
    x, _ = member(me)
    share = 4
    total = jnp.sum(sums[...].reshape(-1, ROW * share, B), axis=0) * scale
    for j, out in enumerate(outs):
        out[:B, :] = new[j]
        for q in range(ROW):

            @pl.when(q == lax.rem(x + j, ROW))
            def _():
                out[B : B + share, :] = total[q * share : (q + 1) * share, :]


def finish_kernel(me, mine, b1, b2, b3, propagated, owned, held):
    x, _ = member(me)
    share = owned.shape[1]
    for j, ref in enumerate((mine, b1, b2, b3)):
        held[turn_to(x, j)] = ref[...]
    for q in range(ROW):
        columns = slice(q * HALF, (q + 1) * HALF)
        for part in range(2):
            lanes = slice(part * HALF, (part + 1) * HALF)
            propagated[part, 0, :, columns] = held[q, :B, lanes]
            owned[part, :, columns] = held[q, B : B + share, lanes]


def local(rows, coefficients, margin, step_matrix, neighbours, pattern):
    width = coefficients.shape[3]
    domains = rows * ROW
    me = lax.axis_index(("row", "x", "orb")).astype(jnp.int32).reshape(1)
    struct = jax.ShapeDtypeStruct
    tile_bytes = 4 * B * B
    step_flops = 2 * 3 * B * BAND * B * B

    def call(kernel, out_shape, args, flops, moved, name, scratch=(), scalars=1):
        return pl.pallas_call(
            kernel,
            out_shape=out_shape,
            in_specs=[SMEM] * scalars + [VMEM] * (len(args) - scalars),
            out_specs=jax.tree.map(lambda _: VMEM, out_shape),
            scratch_shapes=list(scratch),
            cost_estimate=cost(flops, moved * tile_bytes),
            name=name,
            compiler_params=pltpu.CompilerParams(vmem_limit_bytes=32 * 2**20),
        )(*args)

    def in_row(value, by):
        return lax.ppermute(value, "x", [(x, (x + by) % ROW) for x in range(ROW)])

    def swap(value):
        return lax.ppermute(value, "orb", [(0, 1), (1, 0)])

    def exchange(to_a, to_b):
        def swap_rows(value, first):
            pairs = [(r, r + 1) for r in range(first, rows - 1, 2)]
            return lax.ppermute(value, "row", pairs + [(j, i) for i, j in pairs])

        return [swap_rows(to_a, 0), swap_rows(to_b, 1)]

    def apart(value):
        pairs = []
        for core in range(2):
            for r in range(core, rows - 1, 2):
                for x in range(ROW):
                    ends = [((r + i) * ROW + x) * 2 + core for i in range(2)]
                    pairs += [tuple(ends), tuple(ends[::-1])]
        return lax.ppermute(value, ("row", "x", "orb"), pairs)

    slots = neighbours.shape[1]
    hbm = pl.BlockSpec(memory_space=pltpu.HBM)
    half_blocks = pltpu.VMEM((slots, HALF, B), F32)
    packed = pl.pallas_call(
        pack_kernel,
        in_specs=[SMEM] + [hbm] * 5,
        out_specs=VMEM,
        out_shape=struct((ROW, B + 2 * BAND * HALF, B), F32),
        scratch_shapes=[
            pltpu.SMEM(neighbours.shape, jnp.int32), pltpu.SMEM(pattern.shape, jnp.int32),
            pltpu.VMEM(coefficients.shape, F32), half_blocks, half_blocks, pltpu.SemaphoreType.DMA((5,)),
        ],
        cost_estimate=cost(10**6, 44 * tile_bytes),
        name="pack",
        compiler_params=pltpu.CompilerParams(vmem_limit_bytes=28 * 2**20),
    )(me, *(pltpu.with_memory_space_constraint(a, pltpu.HBM) for a in (neighbours, pattern, coefficients, margin, step_matrix)))
    mine = lax.all_to_all(packed, "x", 0, 0, tiled=True)

    state = struct((ROW * B, B), F32)
    edge = struct((2 * B, B), F32)
    edges = call(edge_kernel, [edge, edge], [me, mine], 10**5, 28, "edges")
    *edges, held = lax.optimization_barrier((*edges, mine))
    other, first_across = lax.optimization_barrier((swap(held), swap(coefficients)))
    from_a, from_b = exchange(*edges)
    step_edge = call(step_edge_kernel, struct((2, B, BAND * B), F32), [me, mine, other], 10**5, 20, "step_edges")
    step_edge = apart(step_edge)

    _, held = lax.optimization_barrier((other, coefficients))
    old = [coefficients, in_row(held, 1), in_row(held, 2), None]
    y0 = call(
        margin_kernel, state, [me, mine, other, from_a, from_b], 10**10, 60, "margin",
        scratch=[pltpu.VMEM((ROW, B, BAND * B), F32)] + [pltpu.VMEM((2 * ROW * B, 2 * B), BF16)],
    )
    arrived = exchange(y0, y0)
    _, held = lax.optimization_barrier((old[2], coefficients))
    old[3] = in_row(held, 3)
    *arrived, step_edge, old[1], old[2], old[3] = lax.optimization_barrier((*arrived, step_edge, *old[1:]))
    parts_type = struct((2 * ROW, B, BAND * B), BF16)
    step = list(
        call(
            parts_kernel, [parts_type, parts_type], [me, mine, other, step_edge, swap(step_edge)],
            10**6, 80, "step_parts",
        )
    )
    scratch = [pltpu.VMEM((3 * ROW * B, 2 * B), BF16), pltpu.VMEM((2 * ROW * B, 2 * B), BF16)]
    y1, y2 = call(
        functools.partial(two_kernel, 1), [state, state], [me] + step + arrived + [y0], 3 * ROW * step_flops, 64,
        "two", scratch=scratch,
    )
    arrived = exchange(y2, y2)
    old_type = struct((2 * width, 2 * ROW * B), BF16)
    old_high, old_low = call(
        old_kernel, [old_type, old_type], [me] + old + [first_across] + [swap(o) for o in old[1:]], 10**6, 64, "old_parts"
    )
    arrived[0], old_high = lax.optimization_barrier((arrived[0], old_high))
    new = call(
        functools.partial(last_kernel, 3), struct((ROW, B, B), F32), [me] + step + arrived + [y2, y0, y1],
        3 * ROW * step_flops, 72, "last", scratch=scratch,
    )
    partial_value = call(
        project_kernel, struct((2 * width, B), F32), [me, old_high, old_low, new],
        2 * 3 * 2 * width * 2 * ROW * B * B, 44, "project",
    )
    sums = lax.all_to_all(partial_value, "row", 0, 0, tiled=True)
    share = 2 * width // domains
    sent = struct((B + 2 * share, B), F32)
    tail = call(
        functools.partial(tail_kernel, 1.0 / (domains * B)), [sent] * ROW, [me, sums, new], 10**5, 12, "tail"
    )
    tail = [tail[0]] + [in_row(tail[j], j) for j in range(1, ROW)]
    return call(
        finish_kernel, (struct((2, 1, B, width), F32), struct((2, share, width), F32)), [me] + tail, 10**5, 8,
        "finish", scratch=[pltpu.VMEM((ROW, B + 2 * share, B), F32)],
    )


def solution(mesh):
    rows = mesh.shape["space"] // ROW
    grouped = Mesh(mesh.devices.reshape(rows, ROW, mesh.shape["orb"]), ("row", "x", "orb"))
    space = ("row", "x")
    return jax.shard_map(
        functools.partial(local, rows),
        mesh=grouped,
        in_specs=(
            P(None, space, None, "orb"),
            P(space, None, None, None),
            P(space, None, None, None),
            P(space, None),
            P(space, None),
        ),
        out_specs=(P(None, space, None, "orb"), P(None, space, "orb")),
        check_vma=False,
    )
```
